32 devices in a mesh: node: 8 (over z, x), query: 4 (over y, core).
Axes of the slice: x: 2, y: 2, z: 4, core: 2. Of those that a mesh axis runs over, the one named last changes fastest.
Arguments:
- entity_state: bfloat16 [8192, 2048], P('node', 'query'), may hold values from -6 to 6
- edge_tiles: int32 [128, 3, 512], P('node'), may hold values from 0 to 4095, as said below
- query_head: int32 [64], P('query'), may hold values from 0 to 8191
- query_relation: int32 [64], P('query'), may hold values from 0 to 821
- query_table: float32 [822, 32], replicated, may hold values from -6 to 6
- rel_vectors: float32 [2, 822, 32], replicated, may hold values from -1.8 to 1.8
- mix_weight: float32 [2, 32, 32], replicated, may hold values from -1 to 1
- mix_bias: float32 [2, 32], replicated, may hold values from -3 to 3
- cotangent: bfloat16 [8192, 2048], P('node', 'query'), may hold values from -6 to 6
Outputs:
- final_state: bfloat16 [8192, 2048], P('node', 'query')
- weight_grads: float32 [2, 32, 32], replicated
- bias_grads: float32 [2, 32], replicated
The draws below stay inside these ranges and needn't reach their ends.
Inputs may be any that keep to these rules, and one draw needn't show every extreme that they name: edge_tiles[t,0,:] lies in 0 to 4095, edge_tiles[t,1,:] in 0 to 63, edge_tiles[t,2,:] in 0 to 821.
All inputs are finite; a program needn't handle non-finite values.
Results may differ from the reference program's by a relative error of at most 0.0056.
Values may be sent and summed in bfloat16 or wider, within the bound.
No kernel may reach another device: no remote copies, remote signals or barrier semaphores. Data moves between devices by JAX's collectives and lax.ppermute only.
A program may use at most 192 MiB of HBM per device.

```python
import jax
import jax.numpy as jnp
from jax import lax

DIM = 32
NREL = 822
EDGE_SLOTS = 512
TILES = 16
ROWS_DEV = 1024
NENT = 8192
NTILES = 128
QUERIES = 64
N_NODE = 8


def draw_edge_tiles(key, part):
    keys = jax.random.split(jax.random.fold_in(key, 7), 5)
    shape = (NTILES, 1, EDGE_SLOTS)
    slots = jax.random.randint(keys[0], shape, 0, 4 * ROWS_DEV, dtype=jnp.int32)
    rows_first = jax.random.randint(keys[1], shape, 0, 64, dtype=jnp.int32)
    rows_second = jax.random.randint(keys[2], shape, 0, 64, dtype=jnp.int32)
    rels_first = jax.random.randint(keys[3], shape, 0, NREL, dtype=jnp.int32)
    rels_second = jax.random.randint(keys[4], shape, 0, NREL, dtype=jnp.int32)
    target_rows = jnp.minimum(rows_first, rows_second)
    relations = jnp.minimum(rels_first, rels_second)
    return jnp.concatenate([slots, target_rows, relations], axis=1).astype(jnp.int32)


def touch_ends(values, own_key, least, top_value):
    longest = values.shape.index(max(values.shape))
    spots = []
    for shift in (0, 1):
        where = [jax.random.randint(jax.random.fold_in(own_key, axis), (), 0, length) for axis, length in enumerate(values.shape)]
        where[longest] = (where[longest] + shift) % values.shape[longest]
        spots.append(tuple(where))
    return values.at[spots[0]].set(least).at[spots[1]].set(top_value)


def shard_levels(key, extent, pieces, least, high):
    gain, own = 1.0, jax.random.fold_in(key, 6)
    for axis_at, blocks in pieces:
        heights = jnp.exp(jax.random.uniform(jax.random.fold_in(own, axis_at), (blocks,), jnp.float32, least / len(pieces), high / len(pieces)))
        gain = gain * jnp.repeat(heights, extent[axis_at] // blocks).reshape([-1 if axis == axis_at else 1 for axis in range(len(extent))])
    return gain


def scatter_about(stream_key, shape, width, limit, shards=(), kind=jnp.bfloat16):
    values = jax.random.normal(stream_key, shape, jnp.float32) * width
    if len(shards) > 0:
        values = shard_levels(stream_key, shape, shards, -0.22, 0.18) * values
    return jnp.clip(values, min=-limit, max=limit).astype(kind)


def setup_inputs(seed: int = 0) -> dict:
    splits = jax.random.split(jax.random.key(seed), 10)
    entity_state = scatter_about(splits[0], (NENT, QUERIES * DIM), 1.0, 6.0, ((0, 8), (1, 4)))
    edge_tiles = draw_edge_tiles(jax.random.fold_in(splits[9], 71), 0)
    query_head = touch_ends(jax.random.randint(splits[2], (QUERIES,), 0, NENT), jax.random.fold_in(splits[2], 1), 0, NENT - 1).astype(jnp.int32)
    query_relation = touch_ends(jax.random.randint(splits[3], (QUERIES,), 0, NREL), jax.random.fold_in(splits[3], 1), 0, NREL - 1).astype(jnp.int32)
    query_table = scatter_about(splits[4], (NREL, DIM), 1.0, 6.0, (), jnp.float32)
    rel_vectors = scatter_about(splits[5], (2, NREL, DIM), 0.3, 1.8, (), jnp.float32)
    mix_weight = scatter_about(splits[6], (2, DIM, DIM), DIM ** -0.5, 1.0, (), jnp.float32)
    mix_bias = scatter_about(splits[7], (2, DIM), 0.5, 3.0, (), jnp.float32)
    cotangent = scatter_about(splits[8], (NENT, QUERIES * DIM), 1.0, 6.0, ((0, 8), (1, 4)))
    return dict(entity_state=entity_state, edge_tiles=edge_tiles, query_head=query_head, query_relation=query_relation, query_table=query_table, rel_vectors=rel_vectors, mix_weight=mix_weight, mix_bias=mix_bias, cotangent=cotangent)


def silu_slope(values):
    sigma = jax.nn.sigmoid(values)
    return sigma * (1.0 + values * (1.0 - sigma))


def source_ids(block, part_index):
    slots = block[:, 0, :]
    quarter = slots // ROWS_DEV
    offsets = jnp.array([-1, 0, 1, N_NODE // 2], dtype=jnp.int32)[quarter]
    return (((part_index + offsets) % N_NODE) * ROWS_DEV + slots % ROWS_DEV).astype(jnp.int32)


def propagate(state, rel_table, edge_tiles):
    col_count = state.shape[1]

    def one_part(part_index):
        block = lax.dynamic_slice_in_dim(edge_tiles, (part_index * TILES).astype(jnp.int32), TILES, 0)
        sources = source_ids(block, part_index).reshape(-1)
        targets = (lax.iota(jnp.int32, TILES)[:, None] * 64 + block[:, 1, :]).reshape(-1)
        rel_scale = rel_table[block[:, 2, :].reshape(-1)]
        picked = state[sources].astype(jnp.float32).reshape(-1, col_count // DIM, DIM)
        message = (picked * rel_scale[:, None, :]).astype(jnp.bfloat16).reshape(-1, col_count)
        return jax.ops.segment_sum(message.astype(jnp.float32), targets, num_segments=ROWS_DEV)

    parts = lax.map(one_part, jnp.arange(N_NODE, dtype=jnp.int32))
    return parts.reshape(NENT, col_count)


def adjoint(grad_panel, rel_table, edge_tiles):
    col_count = grad_panel.shape[1]

    def add_part(total, part_index):
        block = lax.dynamic_slice_in_dim(edge_tiles, (part_index * TILES).astype(jnp.int32), TILES, 0)
        slots = block[:, 0, :].reshape(-1)
        targets = (part_index * ROWS_DEV + lax.iota(jnp.int32, TILES)[:, None] * 64 + block[:, 1, :]).reshape(-1)
        rel_scale = rel_table[block[:, 2, :].reshape(-1)]
        picked = grad_panel[targets].astype(jnp.float32).reshape(-1, col_count // DIM, DIM)
        edge_terms = (picked * rel_scale[:, None, :]).reshape(-1, col_count)
        window_terms = jax.ops.segment_sum(edge_terms, slots, num_segments=4 * ROWS_DEV).reshape(4, ROWS_DEV, col_count)
        rounded = lax.optimization_barrier(window_terms.astype(jnp.bfloat16)).astype(jnp.float32)
        keep_own = (lax.iota(jnp.int32, 4) == 1)[:, None, None]
        window_terms = jnp.where(keep_own, window_terms, rounded)
        offsets = jnp.array([-1, 0, 1, N_NODE // 2], dtype=jnp.int32)
        rows = (((part_index + offsets) % N_NODE) * ROWS_DEV)[:, None] + lax.iota(jnp.int32, ROWS_DEV)[None, :]
        return total.at[rows.reshape(-1)].add(window_terms.reshape(-1, col_count)), None

    start = jnp.zeros((NENT, col_count), jnp.float32)
    total, unused = lax.scan(add_part, start, jnp.arange(N_NODE, dtype=jnp.int32))
    return total


def reference(entity_state, edge_tiles, query_head, query_relation, query_table, rel_vectors, mix_weight, mix_bias, cotangent):
    highest = lax.Precision.HIGHEST
    col_count = entity_state.shape[1]
    query_vec = query_table[query_relation]
    entity_ids = jnp.arange(NENT, dtype=jnp.int32)
    head_match = (entity_ids[:, None] == query_head[None, :]).astype(jnp.float32)
    boundary = (head_match[:, :, None] * query_vec[None, :, :]).reshape(NENT, col_count).astype(jnp.bfloat16)

    def run_layer(state, layer_index):
        mixed_in = boundary.astype(jnp.float32) + propagate(state, rel_vectors[layer_index], edge_tiles)
        update = jnp.einsum("rqd,de->rqe", mixed_in.reshape(NENT, QUERIES, DIM), mix_weight[layer_index], precision=highest) + mix_bias[layer_index]
        result = (state.astype(jnp.float32) + jax.nn.silu(update).reshape(NENT, col_count)).astype(jnp.bfloat16)
        return mixed_in, update, result

    mixed_zero, update_zero, state_one = run_layer(entity_state, 0)
    mixed_one, update_one, state_two = run_layer(state_one, 1)
    grad_out = cotangent.astype(jnp.float32)
    grad_update_one = grad_out.reshape(NENT, QUERIES, DIM) * silu_slope(update_one)
    grad_mixed_one = jnp.einsum("rqe,de->rqd", grad_update_one, mix_weight[1], precision=highest).reshape(NENT, col_count).astype(jnp.bfloat16)
    grad_state_one = grad_out + adjoint(grad_mixed_one, rel_vectors[1], edge_tiles)
    grad_update_zero = grad_state_one.reshape(NENT, QUERIES, DIM) * silu_slope(update_zero)
    weight_zero = jnp.einsum("rqd,rqe->de", mixed_zero.reshape(NENT, QUERIES, DIM), grad_update_zero, precision=highest)
    weight_one = jnp.einsum("rqd,rqe->de", mixed_one.reshape(NENT, QUERIES, DIM), grad_update_one, precision=highest)
    bias_zero = jnp.sum(grad_update_zero, axis=(0, 1))
    bias_one = jnp.sum(grad_update_one, axis=(0, 1))
    return state_two, jnp.stack([weight_zero, weight_one]), jnp.stack([bias_zero, bias_one])
```

```python
import functools

import jax
import jax.numpy as jnp
from jax import lax
from jax.experimental import pallas as pl
from jax.experimental.pallas import tpu as pltpu
from jax.sharding import PartitionSpec as P

DIM = 32
LANES = 128
UNROLL = 24
SUMS = 3
CHUNK = 256
AXES = ("node", "query")
HIGHEST = lax.Precision.HIGHEST
SMEM = pl.BlockSpec(memory_space=pltpu.SMEM)
VMEM = pl.BlockSpec(memory_space=pltpu.VMEM)


def silu_slope(values):
    sigma = jax.nn.sigmoid(values)
    return sigma * (1.0 + values * (1.0 - sigma))


class Seats:
    def __init__(self, nodes, queries):
        self.nodes, self.queries = nodes, queries

    def home(self, part, column):
        return part * self.queries + column

    def seat(self, part, column):
        half = self.nodes // 2
        low = part % half
        node = (column & 1) * half + (low ^ (low >> 1))
        return node * self.queries + (column >> 1) * 2 + part // half

    def blocks(self):
        return [(p, c) for p in range(self.nodes) for c in range(self.queries)]

    def gather(self):
        return [(self.home(p, c), self.seat(p, c)) for p, c in self.blocks()]

    def give_back(self):
        return [(target, source) for source, target in self.gather()]

    def shift(self, step):
        return [
            (self.seat((p - step) % self.nodes, c), self.seat(p, c)) for p, c in self.blocks()
        ]

    def mirror(self):
        return [
            (self.seat(p, c), self.seat((p + self.nodes // 2) % self.nodes, c))
            for p, c in self.blocks()
        ]

    def parts(self):
        table = [0] * (self.nodes * self.queries)
        for p, c in self.blocks():
            table[self.seat(p, c)] = p
        return table


def spread(block_ref, window_ref, first):
    if block_ref.shape[1] == LANES:
        rows = block_ref.shape[0]

        def step(i, carry):
            at = pl.multiple_of(i * CHUNK, CHUNK)
            window_ref[pl.ds(first + at, CHUNK), :] = block_ref[pl.ds(at, CHUNK), :].astype(
                jnp.float32
            )
            return carry

        lax.fori_loop(0, rows // CHUNK, step, 0)
        return
    rows, cols = block_ref.shape
    groups = cols // LANES
    size = CHUNK // groups

    def step(i, carry):
        at = pl.multiple_of(i * size, size)
        for j in range(groups):
            window_ref[pl.ds(first + at * groups + j, size, stride=groups), :] = block_ref[
                pl.ds(at, size), j * LANES : (j + 1) * LANES
            ].astype(jnp.float32)
        return carry

    lax.fori_loop(0, rows // size, step, 0)


def clear(sums):
    def step(i, carry):
        at = pl.multiple_of(i * CHUNK, CHUNK)
        for ref in sums:
            ref[pl.ds(at, CHUNK), :] = jnp.zeros((CHUNK, LANES), jnp.float32)
        return carry

    lax.fori_loop(0, sums[0].shape[0] // CHUNK, step, 0)


def walk(groups, begin, end, from_ref, to_ref, rel_ref, window, table, sums):
    def step(i, carry):
        first = begin + i * UNROLL
        for u in range(UNROLL):
            source = pl.multiple_of(from_ref[first + u], groups)
            target = pl.multiple_of(to_ref[first + u], groups)
            scale = table[pl.ds(rel_ref[first + u], groups, stride=0), :]
            sums[u % SUMS][pl.ds(target, groups), :] += (
                window[pl.ds(source, groups), :] * scale
            )
        return carry

    lax.fori_loop(0, (end - begin) // UNROLL, step, 0)


def total_of(sums, at):
    value = sums[0][pl.ds(at, CHUNK), :]
    for ref in sums[1:]:
        value = value + ref[pl.ds(at, CHUNK), :]
    return value


def bucket_kernel(pos_ref, word_ref, count_ref, out_ref, *, edges, dummy):
    unroll = 16

    def step(i, carry):
        for u in range(unroll):
            out_ref[pos_ref[i * unroll + u]] = word_ref[i * unroll + u]
        return carry

    lax.fori_loop(0, edges // unroll, step, 0)

    def fill(i, carry):
        out_ref[i] = dummy
        return carry

    for k in range(4):
        lax.fori_loop(count_ref[k], count_ref[k + 4], fill, 0)


def near_kernel(groups, ends, source, target, rel, own, mirror, table, out, window, *sums):
    half = window.shape[0] // 2
    spread(own, window, 0)
    spread(mirror, window, half)
    clear(sums)
    walk(groups, 0, ends[1], source, target, rel, window, table, sums)

    def step(i, carry):
        at = pl.multiple_of(i * CHUNK, CHUNK)
        out[pl.ds(at, CHUNK), :] = total_of(sums, at)
        return carry

    lax.fori_loop(0, half // CHUNK, step, 0)


def add_boundary(groups, heads, head_rows, ref):
    for q in range(head_rows.shape[0]):
        row = heads[q]

        @pl.when((row >= 0) & (row < ref.shape[0] // groups))
        def _():
            at = row * groups + q * DIM // LANES
            ref[pl.ds(at, 1), :] += head_rows[q : q + 1, :]


def far_sums(groups, ends, source, target, rel, left, right, near, table, heads, head_rows, window, sums):
    half = window.shape[0] // 2
    spread(left, window, 0)
    spread(right, window, half)
    clear(sums[1:])

    def step(i, carry):
        at = pl.multiple_of(i * CHUNK, CHUNK)
        sums[0][pl.ds(at, CHUNK), :] = near[pl.ds(at, CHUNK), :]
        return carry

    lax.fori_loop(0, half // CHUNK, step, 0)
    add_boundary(groups, heads, head_rows, sums[0])
    walk(groups, ends[1], ends[3], source, target, rel, window, table, sums)


def times(left, right):
    return jnp.dot(left, right, precision=HIGHEST, preferred_element_type=jnp.float32)


def outer(left, right):
    return lax.dot_general(
        left, right, (((0,), (0,)), ((), ())), precision=HIGHEST, preferred_element_type=jnp.float32
    )


def first_kernel(
    groups, ends, heads, source, target, rel, left, right, near, own, table, head_rows, weight, bias,
    state, mixed, update, window, *sums,
):
    far_sums(groups, ends, source, target, rel, left, right, near, table, heads, head_rows, window, sums)
    spread(own, window, 0)

    def step(i, carry):
        at = pl.multiple_of(i * CHUNK, CHUNK)
        mix = total_of(sums, at)
        values = times(mix, weight[...]) + bias[...]
        mixed[pl.ds(at, CHUNK), :] = mix
        update[pl.ds(at, CHUNK), :] = values
        state[pl.ds(at, CHUNK), :] = (
            window[pl.ds(at, CHUNK), :] + values * jax.nn.sigmoid(values)
        ).astype(jnp.bfloat16)
        return carry

    lax.fori_loop(0, mixed.shape[0] // CHUNK, step, 0)


def second_kernel(
    groups, ends, heads, source, target, rel, left, right, near, own, table, head_rows, weight, bias,
    weight_back, cotangent, state, grad_mixed, weight_sum, bias_sum, window, *sums,
):
    far_sums(groups, ends, source, target, rel, left, right, near, table, heads, head_rows, window, sums)
    half = window.shape[0] // 2
    spread(own, window, 0)
    spread(cotangent, window, half)
    weight_sum[...] = jnp.zeros_like(weight_sum)
    bias_sum[...] = jnp.zeros_like(bias_sum)

    def step(i, carry):
        at = pl.multiple_of(i * CHUNK, CHUNK)
        mix = total_of(sums, at)
        values = times(mix, weight[...]) + bias[...]
        window[pl.ds(at, CHUNK), :] += values * jax.nn.sigmoid(values)
        grad = window[pl.ds(half + at, CHUNK), :] * silu_slope(values)
        grad_mixed[pl.ds(at, CHUNK), :] = times(grad, weight_back[...]).astype(jnp.bfloat16)
        weight_sum[...] += outer(mix, grad)
        bias_sum[...] += jnp.sum(grad, axis=0, keepdims=True)
        return carry

    lax.fori_loop(0, half // CHUNK, step, 0)
    rows = state.shape[0]
    size = CHUNK // groups

    def store(i, carry):
        at = pl.multiple_of(i * size, size)
        for j in range(groups):
            state[pl.ds(at, size), j * LANES : (j + 1) * LANES] = window[
                pl.ds(at * groups + j, size, stride=groups), :
            ].astype(jnp.bfloat16)
        return carry

    lax.fori_loop(0, rows // size, store, 0)


def adjoint_kernel(groups, kinds, ends, source, target, rel, grad_mixed, table, *refs):
    outs, window, sums = refs[: len(kinds)], refs[len(kinds)], refs[len(kinds) + 1 :]
    spread(grad_mixed, window, 0)
    for kind, out in zip(kinds, outs):
        clear(sums)
        begin = ends[kind - 1] if kind else 0
        walk(groups, begin, ends[kind], target, source, rel, window, table, sums)

        def step(i, carry):
            at = pl.multiple_of(i * CHUNK, CHUNK)
            out[pl.ds(at, CHUNK), :] = total_of(sums, at).astype(out.dtype)
            return carry

        lax.fori_loop(0, window.shape[0] // CHUNK, step, 0)


def folded(wide):
    value = wide[:DIM, :DIM]
    for g in range(1, LANES // DIM):
        value = value + wide[g * DIM : (g + 1) * DIM, g * DIM : (g + 1) * DIM]
    return value


def folded_row(wide):
    value = wide[:, :DIM]
    for g in range(1, LANES // DIM):
        value = value + wide[:, g * DIM : (g + 1) * DIM]
    return value


def last_kernel(
    groups, cotangent, own, left, right, mirror, update, mixed, weight_one, bias_one, out, window,
    weight_sum, bias_sum,
):
    spread(cotangent, window, 0)
    weight_sum[...] = jnp.zeros_like(weight_sum)
    bias_sum[...] = jnp.zeros_like(bias_sum)

    def step(i, carry):
        rows = pl.ds(pl.multiple_of(i * CHUNK, CHUNK), CHUNK)
        state_grad = window[rows, :] + own[rows, :]
        for ref in (left, right, mirror):
            state_grad = state_grad + ref[rows, :].astype(jnp.float32)
        grad = state_grad * silu_slope(update[rows, :])
        weight_sum[...] += outer(mixed[rows, :], grad)
        bias_sum[...] += jnp.sum(grad, axis=0, keepdims=True)
        return carry

    lax.fori_loop(0, window.shape[0] // CHUNK, step, 0)
    out[...] = jnp.zeros_like(out)
    out[0:DIM, 0:DIM] = folded(weight_sum[...])
    out[DIM : 2 * DIM, 0:DIM] = folded(weight_one[...])
    out[2 * DIM : 2 * DIM + 1, 0:DIM] = folded_row(bias_sum[...])
    out[2 * DIM + 1 : 2 * DIM + 2, 0:DIM] = folded_row(bias_one[...])


def edge_lists(edges, row_count, groups, rel_count):
    tile_count, slot_total = edges.shape[0], edges.shape[2]
    edge_count = tile_count * slot_total
    lines = edge_count // LANES
    slots = edges[:, 0, :].reshape(lines, LANES)
    rows = (edges[:, 1, :] + 64 * lax.iota(jnp.int32, tile_count)[:, None]).reshape(lines, LANES)
    rels = edges[:, 2, :].reshape(lines, LANES)
    quarter = slots // row_count
    local = slots % row_count
    kind = jnp.where(
        quarter == 1, 0, jnp.where(quarter == 3, 1, jnp.where(quarter == 0, 2, 3))
    )
    row_bits = (row_count - 1).bit_length()
    word = (rels << (2 * row_bits + 1)) | (rows << (row_bits + 1)) | ((kind & 1) * row_count + local)
    onehot = (kind[None] == lax.iota(jnp.int32, 4)[:, None, None]).astype(jnp.bfloat16)
    upto = (lax.iota(jnp.int32, LANES)[:, None] <= lax.iota(jnp.int32, LANES)[None, :]).astype(
        jnp.bfloat16
    )
    within = jnp.einsum("krl,lm->krm", onehot, upto, preferred_element_type=jnp.float32)
    per_line = within[:, :, -1]
    above = (lax.iota(jnp.int32, lines)[:, None] > lax.iota(jnp.int32, lines)[None, :]).astype(
        jnp.bfloat16
    )
    before = jnp.einsum(
        "rs,ks->kr", above, per_line.astype(jnp.bfloat16), preferred_element_type=jnp.float32
    )
    counts = jnp.sum(per_line, axis=1).astype(jnp.int32)
    padded = (counts + UNROLL - 1) // UNROLL * UNROLL
    ends = jnp.sum(
        jnp.where(lax.iota(jnp.int32, 4)[:, None] >= lax.iota(jnp.int32, 4)[None, :], padded[None], 0),
        axis=1,
    )
    begins = ends - padded
    place = begins.astype(jnp.float32)[:, None, None] + before[:, :, None] + within - 1.0
    pos = jnp.sum(jnp.where(onehot > 0, place, 0.0), axis=0).astype(jnp.int32)
    room = (edge_count + 4 * UNROLL + LANES - 1) // LANES * LANES
    words = pl.pallas_call(
        functools.partial(
            bucket_kernel, edges=edge_count, dummy=rel_count << (2 * row_bits + 1)
        ),
        out_shape=jax.ShapeDtypeStruct((room,), jnp.int32),
        in_specs=[SMEM] * 3,
        out_specs=SMEM,
        name="bucket",
    )(pos.reshape(-1), word.reshape(-1), jnp.concatenate([begins + counts, ends]))
    source = (words & (2 * row_count - 1)) * groups
    target = ((words >> (row_bits + 1)) & (row_count - 1)) * groups
    return ends, source, target, words >> (2 * row_bits + 1)


def body(
    entity_state,
    edge_tiles,
    query_head,
    query_relation,
    query_table,
    rel_vectors,
    mix_weight,
    mix_bias,
    cotangent,
):
    row_count, col_count = entity_state.shape
    groups = col_count // LANES
    long = row_count * groups
    query_count = query_head.shape[0]
    rel_count = rel_vectors.shape[1]
    seats = Seats(lax.axis_size("node"), lax.axis_size("query"))

    def send(block, route):
        return lax.ppermute(block, AXES, route)

    def kernel(fn, outs, specs, scratch, name):
        return pl.pallas_call(
            fn, out_shape=outs, in_specs=specs, out_specs=[VMEM] * len(outs), scratch_shapes=scratch,
            name=name,
        )

    wide_f32 = jax.ShapeDtypeStruct((long, LANES), jnp.float32)
    wide_bf16 = jax.ShapeDtypeStruct((long, LANES), jnp.bfloat16)
    pair = pltpu.VMEM((2 * long, LANES), jnp.float32)
    single = pltpu.VMEM((long, LANES), jnp.float32)
    sums = [single] * SUMS

    state_zero = send(entity_state, seats.gather())
    flat = jnp.concatenate([edge_tiles.reshape(-1), query_head, query_relation])
    edge_total = edge_tiles.size
    flat = jnp.pad(flat, (0, -flat.shape[0] % (8 * LANES))).reshape(-1, LANES)
    flat = send(flat, seats.gather()).reshape(-1)
    edges = flat[:edge_total].reshape(edge_tiles.shape)
    own_head = flat[edge_total : edge_total + query_count]
    own_relation = flat[edge_total + query_count : edge_total + 2 * query_count]
    moved = lax.optimization_barrier((cotangent, state_zero))
    grad_out = send(moved[0], seats.gather())
    state_zero = moved[1]

    linear = lax.axis_index("node") * seats.queries + lax.axis_index("query")
    part = jnp.array(seats.parts(), jnp.int32)[linear]
    heads = own_head - part * row_count
    choose_rel = (own_relation[:, None] == lax.iota(jnp.int32, query_table.shape[0])[None, :]).astype(
        jnp.float32
    )
    query_vec = (
        jnp.dot(choose_rel, query_table, precision=HIGHEST, preferred_element_type=jnp.float32)
        .astype(jnp.bfloat16)
        .astype(jnp.float32)
    )
    repeat = LANES // DIM
    lane_group = lax.iota(jnp.int32, LANES) // DIM
    head_rows = jnp.where(
        lane_group[None, :] == (lax.iota(jnp.int32, query_count) % repeat)[:, None],
        jnp.tile(query_vec, (1, repeat)),
        0.0,
    )
    tables = jnp.tile(jnp.pad(rel_vectors, ((0, 0), (0, -rel_count % 8 or 8), (0, 0))), (1, 1, repeat))
    same = lane_group[:, None] == lane_group[None, :]
    weights = jnp.where(same[None], jnp.tile(mix_weight, (1, repeat, repeat)), 0.0)
    weight_back = weights[1].T
    biases = jnp.tile(mix_bias, (1, repeat))[:, None, :]
    ends, source, target, rel = edge_lists(edges, row_count, groups, rel_count)
    source_local = source % long

    def layer(state, index, far, outs):
        mirror = send(state, seats.mirror())
        left = send(state, seats.shift(1))
        right = send(state, seats.shift(-1))
        (near,) = kernel(
            functools.partial(near_kernel, groups), [wide_f32], [SMEM] * 4 + [VMEM] * 3, [pair] + sums,
            f"near_{index}",
        )(ends, source, target, rel, state, mirror, tables[index])
        args = [left, right, near, state, tables[index], head_rows, weights[index], biases[index]]
        if index:
            args += [weight_back, grad_out]
        return kernel(
            functools.partial(far, groups), outs, [SMEM] * 5 + [VMEM] * len(args), [pair] + sums,
            f"far_{index}",
        )(ends, heads, source, target, rel, *args)

    state_one, mixed_zero, update_zero = layer(
        state_zero, 0, first_kernel, [wide_bf16, wide_f32, wide_f32]
    )
    square = jax.ShapeDtypeStruct((LANES, LANES), jnp.float32)
    line = jax.ShapeDtypeStruct((1, LANES), jnp.float32)
    state_two, grad_mixed, weight_one, bias_one = layer(
        state_one,
        1,
        second_kernel,
        [jax.ShapeDtypeStruct(entity_state.shape, jnp.bfloat16), wide_bf16, square, line],
    )

    def adjoint(kinds, outs, name):
        return kernel(
            functools.partial(adjoint_kernel, groups, kinds), outs, [SMEM] * 4 + [VMEM] * 2,
            [single] + sums, name,
        )(ends, source_local, target, rel, grad_mixed, tables[1])

    (to_left,) = adjoint((2,), [wide_bf16], "adjoint_left")
    from_right = send(to_left, seats.shift(-1))
    (to_right,) = adjoint((3,), [wide_bf16], "adjoint_right")
    from_left = send(to_right, seats.shift(1))
    own_terms, to_mirror = adjoint((0, 1), [wide_f32, wide_bf16], "adjoint_near")
    from_mirror = send(to_mirror, seats.mirror())
    final_state = send(state_two, seats.give_back())
    (grads,) = kernel(
        functools.partial(last_kernel, groups),
        [jax.ShapeDtypeStruct((2 * DIM + 8, LANES), jnp.float32)],
        [VMEM] * 9,
        [single, pltpu.VMEM((LANES, LANES), jnp.float32), pltpu.VMEM((1, LANES), jnp.float32)],
        "last",
    )(
        grad_out, own_terms, from_left, from_right, from_mirror, update_zero, mixed_zero, weight_one,
        bias_one,
    )
    devices = seats.nodes * seats.queries
    reach = 1
    while reach < devices:
        grads = grads + send(grads, [(i, i ^ reach) for i in range(devices)])
        reach *= 2
    weight_grads = grads[: 2 * DIM, :DIM].reshape(2, DIM, DIM)
    bias_grads = grads[2 * DIM : 2 * DIM + 2, :DIM]
    return (final_state, weight_grads, bias_grads)


def solution(mesh):
    placed = (
        P("node", "query"),
        P("node", None, None),
        P("query"),
        P("query"),
        P(),
        P(),
        P(),
        P(),
        P("node", "query"),
    )
    return jax.shard_map(
        body, mesh=mesh, in_specs=placed, out_specs=(P("node", "query"), P(), P()), check_vma=False
    )
```

```python
import functools

import jax
import jax.numpy as jnp
from jax import lax
from jax.experimental import pallas as pl
from jax.experimental.pallas import tpu as pltpu
from jax.sharding import PartitionSpec as P


DIM = 32
LANES = 128
UNROLL = 24
SUMS = 3
CHUNK = 256
AXES = ("node", "query")
HIGHEST = lax.Precision.HIGHEST
SMEM = pl.BlockSpec(memory_space=pltpu.SMEM)
VMEM = pl.BlockSpec(memory_space=pltpu.VMEM)
ANY = pl.BlockSpec(memory_space=pl.ANY)


def silu_slope(values):
    sigma = jax.nn.sigmoid(values)
    return sigma * (1.0 + values * (1.0 - sigma))


class Seats:
    def __init__(self, nodes, queries):
        self.nodes, self.queries = nodes, queries

    def home(self, part, column):
        return part * self.queries + column

    def seat(self, part, column):
        half = self.nodes // 2
        low = part % half
        node = (column & 1) * half + (low ^ (low >> 1))
        return node * self.queries + (column >> 1) * 2 + part // half

    def blocks(self):
        return [(p, c) for p in range(self.nodes) for c in range(self.queries)]

    def gather(self):
        return [(self.home(p, c), self.seat(p, c)) for p, c in self.blocks()]

    def give_back(self):
        return [(target, source) for source, target in self.gather()]

    def shift(self, step):
        return [
            (self.seat((p - step) % self.nodes, c), self.seat(p, c)) for p, c in self.blocks()
        ]

    def mirror(self):
        return [
            (self.seat(p, c), self.seat((p + self.nodes // 2) % self.nodes, c))
            for p, c in self.blocks()
        ]

    def parts(self):
        table = [0] * (self.nodes * self.queries)
        for p, c in self.blocks():
            table[self.seat(p, c)] = p
        return table


def spread(block_ref, window_ref, first):
    if block_ref.shape[1] == LANES:
        rows = block_ref.shape[0]

        def step(i, carry):
            at = pl.multiple_of(i * CHUNK, CHUNK)
            window_ref[pl.ds(first + at, CHUNK), :] = block_ref[pl.ds(at, CHUNK), :].astype(
                jnp.float32
            )
            return carry

        lax.fori_loop(0, rows // CHUNK, step, 0)
        return
    rows, cols = block_ref.shape
    groups = cols // LANES
    size = CHUNK // groups

    def step(i, carry):
        at = pl.multiple_of(i * size, size)
        for j in range(groups):
            window_ref[pl.ds(first + at * groups + j, size, stride=groups), :] = block_ref[
                pl.ds(at, size), j * LANES : (j + 1) * LANES
            ].astype(jnp.float32)
        return carry

    lax.fori_loop(0, rows // size, step, 0)


def clear(sums):
    def step(i, carry):
        at = pl.multiple_of(i * CHUNK, CHUNK)
        for ref in sums:
            ref[pl.ds(at, CHUNK), :] = jnp.zeros((CHUNK, LANES), jnp.float32)
        return carry

    lax.fori_loop(0, sums[0].shape[0] // CHUNK, step, 0)


def walk(groups, begin, end, from_ref, to_ref, rel_ref, window, table, sums):
    def step(i, carry):
        first = begin + i * UNROLL
        for u in range(UNROLL):
            source = pl.multiple_of(from_ref[first + u], groups)
            target = pl.multiple_of(to_ref[first + u], groups)
            scale = table[pl.ds(rel_ref[first + u], groups, stride=0), :]
            sums[u % SUMS][pl.ds(target, groups), :] += (
                window[pl.ds(source, groups), :] * scale
            )
        return carry

    lax.fori_loop(0, (end - begin) // UNROLL, step, 0)


def total_of(sums, at):
    value = sums[0][pl.ds(at, CHUNK), :]
    for ref in sums[1:]:
        value = value + ref[pl.ds(at, CHUNK), :]
    return value


def fetch(pairs, sems):
    copies = [pltpu.make_async_copy(src, dst, sems.at[i]) for i, (src, dst) in enumerate(pairs)]
    for copy in copies:
        copy.start()
    return copies


def wait(copies):
    for copy in copies:
        copy.wait()


def bucket_kernel(pos_ref, word_ref, count_ref, out_ref, *, edges, dummy):
    unroll = 32

    def step(i, carry):
        for u in range(unroll):
            out_ref[pos_ref[i * unroll + u]] = word_ref[i * unroll + u]
        return carry

    lax.fori_loop(0, edges // unroll, step, 0)

    def fill(i, carry):
        out_ref[i] = dummy
        return carry

    for k in range(4):
        lax.fori_loop(count_ref[k], count_ref[k + 4], fill, 0)


def split(values):
    high = values.astype(jnp.bfloat16)
    low = (values - high.astype(jnp.float32)).astype(jnp.bfloat16)
    return jnp.concatenate([high, low], axis=1)


def split_weight(weight):
    wide = split(weight)
    return jnp.concatenate([wide, wide], axis=0)


def times(values, wide):
    both = jnp.dot(split(values), wide, preferred_element_type=jnp.float32)
    return both[:, :LANES] + both[:, LANES:]


def outer(left, right):
    return lax.dot_general(
        split(left), split(right), (((0,), (0,)), ((), ())), preferred_element_type=jnp.float32
    )


def quarters(wide):
    return (
        wide[:LANES, :LANES] + wide[LANES:, :LANES] + wide[:LANES, LANES:] + wide[LANES:, LANES:]
    )


def near_kernel(
    groups, ends, source, target, rel, own, mirror, table, out,
    source_buf, target_buf, rel_buf, own_buf, mirror_buf, table_buf, window, sems, *sums,
):
    long = sums[0].shape[0]
    states = fetch([(own, own_buf), (mirror, mirror_buf)], sems)
    lists = fetch(
        [(source, source_buf), (target, target_buf), (rel, rel_buf), (table, table_buf)],
        sems.at[pl.ds(2, 4)],
    )
    clear(sums)
    states[0].wait()
    spread(own_buf, window, 0)
    states[1].wait()
    spread(mirror_buf, window, long)
    wait(lists)
    walk(groups, 0, ends[1], source_buf, target_buf, rel_buf, window, table_buf, sums)
    parts = 4
    size = long // parts
    stores = []
    for k in range(parts):

        def step(i, carry):
            at = pl.multiple_of(k * size + i * CHUNK, CHUNK)
            sums[0][pl.ds(at, CHUNK), :] = total_of(sums, at)
            return carry

        lax.fori_loop(0, size // CHUNK, step, 0)
        piece = pl.ds(k * size, size)
        stores += fetch([(sums[0].at[piece, :], out.at[piece, :])], sems.at[pl.ds(6 + k, 1)])
    wait(stores)


def add_boundary(groups, heads, head_rows, ref, long):
    for q in range(head_rows.shape[0]):
        row = heads[q]

        @pl.when((row >= 0) & (row < long // groups))
        def _():
            at = row * groups + q * DIM // LANES
            ref[pl.ds(at, 1), :] += head_rows[q : q + 1, :]


def far_sums(groups, long, ends, heads, inputs, bufs, head_rows, window, sems, sums):
    source, target, rel, left, right, near, table = inputs
    source_buf, target_buf, rel_buf, left_buf, right_buf, table_buf = bufs
    states = fetch(
        [(left, left_buf), (right, right_buf), (near, sums[0].at[pl.ds(0, long), :])], sems
    )
    lists = fetch(
        [(source, source_buf), (target, target_buf), (rel, rel_buf), (table, table_buf)],
        sems.at[pl.ds(3, 4)],
    )
    clear([ref.at[pl.ds(0, long), :] for ref in sums[1:]])
    states[0].wait()
    spread(left_buf, window, 0)
    states[1].wait()
    spread(right_buf, window, long)
    states[2].wait()
    add_boundary(groups, heads, head_rows, sums[0], long)
    wait(lists)
    walk(groups, ends[1], ends[3], source_buf, target_buf, rel_buf, window, table_buf, sums)


def first_kernel(
    groups, ends, heads, head_rows, weight, bias, source, target, rel, left, right, near, table, own,
    state, mixed, update,
    source_buf, target_buf, rel_buf, left_buf, right_buf, table_buf, own_buf, window, mixed_buf,
    update_buf, state_buf, sems, *sums,
):
    long = sums[0].shape[0]
    extra = fetch([(own, own_buf)], sems.at[pl.ds(7, 1)])
    far_sums(
        groups, long, ends, heads, (source, target, rel, left, right, near, table),
        (source_buf, target_buf, rel_buf, left_buf, right_buf, table_buf), head_rows, window, sems,
        sums,
    )
    wait(extra)
    spread(own_buf, window, 0)
    wide = split_weight(weight[...])
    parts = 4
    size = long // parts
    stores = []
    for k in range(parts):

        def step(i, carry):
            rows = pl.ds(pl.multiple_of(k * size + i * CHUNK, CHUNK), CHUNK)
            mix = total_of(sums, pl.multiple_of(k * size + i * CHUNK, CHUNK))
            values = times(mix, wide) + bias[...]
            mixed_buf[rows, :] = mix
            update_buf[rows, :] = values
            state_buf[rows, :] = (window[rows, :] + values * jax.nn.sigmoid(values)).astype(
                jnp.bfloat16
            )
            return carry

        lax.fori_loop(0, size // CHUNK, step, 0)
        rows = pl.ds(k * size, size)
        stores += fetch(
            [
                (state_buf.at[rows, :], state.at[rows, :]),
                (mixed_buf.at[rows, :], mixed.at[rows, :]),
                (update_buf.at[rows, :], update.at[rows, :]),
            ],
            sems.at[pl.ds(8 + 3 * k, 3)],
        )
    wait(stores)


def second_kernel(
    groups, ends, heads, head_rows, weight, bias, weight_back, source, target, rel, left, right, near,
    table, own, cotangent,
    state, grad_mixed, mixed, grad, to_left, to_right,
    source_buf, target_buf, rel_buf, left_buf, right_buf, table_buf, own_buf, cotangent_buf, window,
    mixed_buf, grad_buf, grad_mixed_buf, state_buf, left_out, right_out, sems, *sums,
):
    long = window.shape[0] // 2
    extra = fetch([(own, own_buf), (cotangent, cotangent_buf)], sems.at[pl.ds(7, 2)])
    far_sums(
        groups, long, ends, heads, (source, target, rel, left, right, near, table),
        (source_buf, target_buf, rel_buf, left_buf, right_buf, table_buf), head_rows, window, sems,
        sums,
    )
    wait(extra)
    spread(own_buf, window, 0)
    spread(cotangent_buf, window, long)
    wide = split_weight(weight[...])
    wide_back = split_weight(weight_back[...])

    def step(i, carry):
        at = pl.multiple_of(i * CHUNK, CHUNK)
        rows = pl.ds(at, CHUNK)
        mix = total_of(sums, at)
        values = times(mix, wide) + bias[...]
        sigma = jax.nn.sigmoid(values)
        window[rows, :] += values * sigma
        behind = pl.ds(long + at, CHUNK)
        slope = window[behind, :] * (sigma * (1.0 + values * (1.0 - sigma)))
        back = times(slope, wide_back).astype(jnp.bfloat16)
        mixed_buf[rows, :] = mix
        grad_buf[rows, :] = slope
        grad_mixed_buf[rows, :] = back
        window[behind, :] = back.astype(jnp.float32)
        for ref in sums:
            ref[rows, :] = jnp.zeros((CHUNK, LANES), jnp.float32)
            ref[behind, :] = jnp.zeros((CHUNK, LANES), jnp.float32)
        return carry

    lax.fori_loop(0, long // CHUNK, step, 0)
    size = CHUNK // groups

    def store(i, carry):
        at = pl.multiple_of(i * size, size)
        for j in range(groups):
            state_buf[pl.ds(at, size), j * LANES : (j + 1) * LANES] = window[
                pl.ds(at * groups + j, size, stride=groups), :
            ].astype(jnp.bfloat16)
        return carry

    lax.fori_loop(0, long // CHUNK, store, 0)
    stores = fetch(
        [(state_buf, state), (grad_mixed_buf, grad_mixed), (mixed_buf, mixed), (grad_buf, grad)],
        sems.at[pl.ds(9, 4)],
    )
    walk(
        groups, ends[1], ends[3], target_buf, source_buf, rel_buf, window.at[pl.ds(long, long), :],
        table_buf, sums,
    )

    for k, (buf, out) in enumerate(((left_out, to_left), (right_out, to_right))):

        def total(i, carry):
            at = pl.multiple_of(i * CHUNK, CHUNK)
            buf[pl.ds(at, CHUNK), :] = total_of(sums, k * long + at).astype(jnp.bfloat16)
            return carry

        lax.fori_loop(0, long // CHUNK, total, 0)
        stores += fetch([(buf, out)], sems.at[pl.ds(13 + k, 1)])
    wait(stores)


def adjoint_kernel(
    groups, ends, source, target, rel, grad_mixed, table, cotangent, mixed, grad,
    base, to_mirror, weight_sum, bias_sum,
    source_buf, target_buf, rel_buf, grad_mixed_buf, table_buf, cotangent_buf, mixed_buf, grad_buf,
    mirror_out, window, wide_sum, sems, *sums,
):
    long = window.shape[0]
    loads = fetch([(grad_mixed, grad_mixed_buf)], sems)
    lists = fetch(
        [(source, source_buf), (target, target_buf), (rel, rel_buf), (table, table_buf)],
        sems.at[pl.ds(1, 4)],
    )
    late = fetch(
        [(cotangent, cotangent_buf), (mixed, mixed_buf), (grad, grad_buf)], sems.at[pl.ds(5, 3)]
    )
    clear(sums)
    wait(loads)
    spread(grad_mixed_buf, window, 0)
    wait(lists)
    walk(groups, 0, ends[1], target_buf, source_buf, rel_buf, window, table_buf, sums)

    def total(i, carry):
        at = pl.multiple_of(i * CHUNK, CHUNK)
        mirror_out[pl.ds(at, CHUNK), :] = total_of(sums, long + at).astype(jnp.bfloat16)
        return carry

    lax.fori_loop(0, long // CHUNK, total, 0)
    stores = fetch([(mirror_out, to_mirror)], sems.at[pl.ds(8, 1)])
    wait(late)
    spread(cotangent_buf, window, 0)
    wide_sum[...] = jnp.zeros_like(wide_sum)
    bias_sum[...] = jnp.zeros_like(bias_sum)

    def step(i, carry):
        at = pl.multiple_of(i * CHUNK, CHUNK)
        rows = pl.ds(at, CHUNK)
        window[rows, :] += total_of(sums, at)
        values = grad_buf[rows, :]
        wide_sum[...] += outer(mixed_buf[rows, :], values)
        bias_sum[...] += jnp.sum(values, axis=0, keepdims=True)
        return carry

    lax.fori_loop(0, long // CHUNK, step, 0)
    stores += fetch([(window, base)], sems.at[pl.ds(9, 1)])
    weight_sum[...] = quarters(wide_sum[...])
    wait(stores)


def folded(wide):
    value = wide[:DIM, :DIM]
    for g in range(1, LANES // DIM):
        value = value + wide[g * DIM : (g + 1) * DIM, g * DIM : (g + 1) * DIM]
    return value


def folded_row(wide):
    value = wide[:, :DIM]
    for g in range(1, LANES // DIM):
        value = value + wide[:, g * DIM : (g + 1) * DIM]
    return value


def last_kernel(
    base, left, right, mirror, update, mixed, weight_one, bias_one, out, wide_sum, bias_sum
):
    @pl.when(pl.program_id(0) == 0)
    def _():
        wide_sum[...] = jnp.zeros_like(wide_sum)
        bias_sum[...] = jnp.zeros_like(bias_sum)

    state_grad = base[...]
    for ref in (left, right, mirror):
        state_grad = state_grad + ref[...].astype(jnp.float32)
    grad = state_grad * silu_slope(update[...])
    wide_sum[...] += outer(mixed[...], grad)
    bias_sum[...] += jnp.sum(grad, axis=0, keepdims=True)

    @pl.when(pl.program_id(0) == pl.num_programs(0) - 1)
    def _():
        out[...] = jnp.zeros_like(out)
        out[0:DIM, 0:DIM] = folded(quarters(wide_sum[...]))
        out[DIM : 2 * DIM, 0:DIM] = folded(weight_one[...])
        out[2 * DIM : 2 * DIM + 1, 0:DIM] = folded_row(bias_sum[...])
        out[2 * DIM + 1 : 2 * DIM + 2, 0:DIM] = folded_row(bias_one[...])


def edge_lists(edges, row_count, groups, rel_count):
    tile_count, slot_total = edges.shape[0], edges.shape[2]
    edge_count = tile_count * slot_total
    lines = edge_count // LANES
    slots = edges[:, 0, :].reshape(lines, LANES)
    rows = (edges[:, 1, :] + 64 * lax.iota(jnp.int32, tile_count)[:, None]).reshape(lines, LANES)
    rels = edges[:, 2, :].reshape(lines, LANES)
    quarter = slots // row_count
    local = slots % row_count
    kind = jnp.where(
        quarter == 1, 0, jnp.where(quarter == 3, 1, jnp.where(quarter == 0, 2, 3))
    )
    row_bits = (row_count - 1).bit_length()
    word = (rels << (2 * row_bits + 1)) | (rows << (row_bits + 1)) | ((kind & 1) * row_count + local)
    onehot = (kind[None] == lax.iota(jnp.int32, 4)[:, None, None]).astype(jnp.bfloat16)
    upto = (lax.iota(jnp.int32, LANES)[:, None] <= lax.iota(jnp.int32, LANES)[None, :]).astype(
        jnp.bfloat16
    )
    within = jnp.einsum("krl,lm->krm", onehot, upto, preferred_element_type=jnp.float32)
    per_line = within[:, :, -1]
    above = (lax.iota(jnp.int32, lines)[:, None] > lax.iota(jnp.int32, lines)[None, :]).astype(
        jnp.bfloat16
    )
    before = jnp.einsum(
        "rs,ks->kr", above, per_line.astype(jnp.bfloat16), preferred_element_type=jnp.float32
    )
    counts = jnp.sum(per_line, axis=1).astype(jnp.int32)
    padded = (counts + UNROLL - 1) // UNROLL * UNROLL
    ends = jnp.sum(
        jnp.where(lax.iota(jnp.int32, 4)[:, None] >= lax.iota(jnp.int32, 4)[None, :], padded[None], 0),
        axis=1,
    )
    begins = ends - padded
    place = begins.astype(jnp.float32)[:, None, None] + before[:, :, None] + within - 1.0
    pos = jnp.sum(jnp.where(onehot > 0, place, 0.0), axis=0).astype(jnp.int32)
    room = (edge_count + 4 * UNROLL + LANES - 1) // LANES * LANES
    words = pl.pallas_call(
        functools.partial(bucket_kernel, edges=edge_count, dummy=rel_count << (2 * row_bits + 1)),
        out_shape=jax.ShapeDtypeStruct((room,), jnp.int32),
        in_specs=[SMEM] * 3,
        out_specs=SMEM,
        name="bucket",
    )(pos.reshape(-1), word.reshape(-1), jnp.concatenate([begins + counts, ends]))
    source = (words & (2 * row_count - 1)) * groups
    target = ((words >> (row_bits + 1)) & (row_count - 1)) * groups
    return ends, source, target, words >> (2 * row_bits + 1)


def body(
    entity_state,
    edge_tiles,
    query_head,
    query_relation,
    query_table,
    rel_vectors,
    mix_weight,
    mix_bias,
    cotangent,
):
    row_count, col_count = entity_state.shape
    groups = col_count // LANES
    long = row_count * groups
    query_count = query_head.shape[0]
    rel_count = rel_vectors.shape[1]
    seats = Seats(lax.axis_size("node"), lax.axis_size("query"))

    def send(block, route):
        return lax.ppermute(block, AXES, route)

    def run(fn, args, specs, outs, out_specs, scratch):
        return pl.pallas_call(
            fn, out_shape=outs, in_specs=specs, out_specs=out_specs, scratch_shapes=scratch,
        )(*args)

    wide_f32 = jax.ShapeDtypeStruct((long, LANES), jnp.float32)
    wide_bf16 = jax.ShapeDtypeStruct((long, LANES), jnp.bfloat16)
    f32_buf = pltpu.VMEM((long, LANES), jnp.float32)
    bf16_buf = pltpu.VMEM((long, LANES), jnp.bfloat16)
    pair = pltpu.VMEM((2 * long, LANES), jnp.float32)
    sums = [f32_buf] * SUMS
    pair_sums = [pair] * SUMS
    square = jax.ShapeDtypeStruct((LANES, LANES), jnp.float32)
    line = jax.ShapeDtypeStruct((1, LANES), jnp.float32)

    state_zero = send(entity_state, seats.gather())
    flat = jnp.concatenate([edge_tiles.reshape(-1), query_head, query_relation])
    edge_total = edge_tiles.size
    flat = jnp.pad(flat, (0, -flat.shape[0] % (8 * LANES))).reshape(-1, LANES)
    flat = send(flat, seats.gather()).reshape(-1)
    edges = flat[:edge_total].reshape(edge_tiles.shape)
    own_head = flat[edge_total : edge_total + query_count]
    own_relation = flat[edge_total + query_count : edge_total + 2 * query_count]
    grad_out = send(cotangent, seats.gather())

    linear = lax.axis_index("node") * seats.queries + lax.axis_index("query")
    part = jnp.array(seats.parts(), jnp.int32)[linear]
    heads = own_head - part * row_count
    choose_rel = (own_relation[:, None] == lax.iota(jnp.int32, query_table.shape[0])[None, :]).astype(
        jnp.float32
    )
    query_vec = (
        jnp.dot(choose_rel, query_table, precision=HIGHEST, preferred_element_type=jnp.float32)
        .astype(jnp.bfloat16)
        .astype(jnp.float32)
    )
    repeat = LANES // DIM
    lane_group = lax.iota(jnp.int32, LANES) // DIM
    head_rows = jnp.where(
        lane_group[None, :] == (lax.iota(jnp.int32, query_count) % repeat)[:, None],
        jnp.tile(query_vec, (1, repeat)),
        0.0,
    )
    tables = jnp.tile(jnp.pad(rel_vectors, ((0, 0), (0, -rel_count % 8 or 8), (0, 0))), (1, 1, repeat))
    same = lane_group[:, None] == lane_group[None, :]
    weights = jnp.where(same[None], jnp.tile(mix_weight, (1, repeat, repeat)), 0.0)
    weight_back = weights[1].T
    biases = jnp.tile(mix_bias, (1, repeat))[:, None, :]
    ends, source, target, rel = edge_lists(edges, row_count, groups, rel_count)
    lists = [source, target, rel]
    list_bufs = [pltpu.SMEM(source.shape, jnp.int32)] * 3
    table_buf = pltpu.VMEM(tables.shape[1:], jnp.float32)

    def sems(count):
        return pltpu.SemaphoreType.DMA((count,))

    def halo(state, index):
        buf = pltpu.VMEM(state.shape, jnp.bfloat16)
        mirror = send(state, seats.mirror())
        left = send(state, seats.shift(1))
        right = send(state, seats.shift(-1))
        near = run(
            functools.partial(near_kernel, groups),
            [ends, *lists, state, mirror, tables[index]],
            [SMEM] + [ANY] * 6,
            wide_f32,
            ANY,
            [*list_bufs, buf, buf, table_buf, pair, sems(10), *sums],
        )
        return left, right, near

    left, right, near = halo(state_zero, 0)
    block_buf = pltpu.VMEM(state_zero.shape, jnp.bfloat16)
    state_one, mixed_zero, update_zero = run(
        functools.partial(first_kernel, groups),
        [ends, heads, head_rows, weights[0], biases[0], *lists, left, right, near, tables[0], state_zero],
        [SMEM] * 2 + [VMEM] * 3 + [ANY] * 8,
        [wide_bf16, wide_f32, wide_f32],
        [ANY] * 3,
        [*list_bufs, block_buf, block_buf, table_buf, block_buf, pair, f32_buf, f32_buf, bf16_buf, sems(20)]
        + sums,
    )
    left, right, near = halo(state_one, 1)
    state_two, grad_mixed, mixed_one, grad_one, to_left, to_right = run(
        functools.partial(second_kernel, groups),
        [ends, heads, head_rows, weights[1], biases[1], weight_back, *lists, left, right, near, tables[1]]
        + [state_one, grad_out],
        [SMEM] * 2 + [VMEM] * 4 + [ANY] * 9,
        [jax.ShapeDtypeStruct(entity_state.shape, jnp.bfloat16), wide_bf16, wide_f32, wide_f32]
        + [wide_bf16] * 2,
        [ANY] * 6,
        [*list_bufs, bf16_buf, bf16_buf, table_buf, bf16_buf, block_buf, pair, f32_buf, f32_buf, bf16_buf]
        + [block_buf, bf16_buf, bf16_buf, sems(15), *pair_sums],
    )
    from_right = send(to_left, seats.shift(-1))
    from_left = send(to_right, seats.shift(1))
    final_state = send(state_two, seats.give_back())
    base, to_mirror, weight_one, bias_one = run(
        functools.partial(adjoint_kernel, groups),
        [ends, *lists, grad_mixed, tables[1], grad_out, mixed_one, grad_one],
        [SMEM] + [ANY] * 8,
        [wide_f32, wide_bf16, square, line],
        [ANY] * 2 + [VMEM] * 2,
        [*list_bufs, bf16_buf, table_buf, block_buf, f32_buf, f32_buf, bf16_buf, f32_buf]
        + [pltpu.VMEM((2 * LANES, 2 * LANES), jnp.float32), sems(10), *pair_sums],
    )
    from_mirror = send(to_mirror, seats.mirror())
    steps = 8
    rows = pl.BlockSpec((long // steps, LANES), lambda i: (i, 0))
    whole = lambda shape: pl.BlockSpec(shape, lambda i: (0, 0))
    grads = pl.pallas_call(
        last_kernel,
        out_shape=jax.ShapeDtypeStruct((2 * DIM + 8, LANES), jnp.float32),
        grid=(steps,),
        in_specs=[rows] * 6 + [whole((LANES, LANES)), whole((1, LANES))],
        out_specs=whole((2 * DIM + 8, LANES)),
        scratch_shapes=[
            pltpu.VMEM((2 * LANES, 2 * LANES), jnp.float32),
            pltpu.VMEM((1, LANES), jnp.float32),
        ],
        name="last",
    )(base, from_left, from_right, from_mirror, update_zero, mixed_zero, weight_one, bias_one)
    devices = seats.nodes * seats.queries
    reach = 1
    while reach < devices:
        grads = grads + send(grads, [(i, i ^ reach) for i in range(devices)])
        reach *= 2
    weight_grads = grads[: 2 * DIM, :DIM].reshape(2, DIM, DIM)
    bias_grads = grads[2 * DIM : 2 * DIM + 2, :DIM]
    return (final_state, weight_grads, bias_grads)


def solution(mesh):
    placed = (
        P("node", "query"),
        P("node", None, None),
        P("query"),
        P("query"),
        P(),
        P(),
        P(),
        P(),
        P("node", "query"),
    )

    return jax.shard_map(
        body, mesh=mesh, in_specs=placed, out_specs=(P("node", "query"), P(), P()), check_vma=False
    )
```

```python
import functools

import jax
import jax.numpy as jnp
from jax import lax
from jax.experimental import pallas as pl
from jax.experimental.pallas import tpu as pltpu
from jax.sharding import PartitionSpec as P


DIM = 32
LANES = 128
UNROLL = 24
SUMS = 3
CHUNK = 256
AXES = ("node", "query")
HIGHEST = lax.Precision.HIGHEST
SMEM = pl.BlockSpec(memory_space=pltpu.SMEM)
VMEM = pl.BlockSpec(memory_space=pltpu.VMEM)
ANY = pl.BlockSpec(memory_space=pl.ANY)


def silu_slope(values):
    sigma = jax.nn.sigmoid(values)
    return sigma * (1.0 + values * (1.0 - sigma))


class Seats:
    def __init__(self, nodes, queries):
        self.nodes, self.queries = nodes, queries

    def home(self, part, column):
        return part * self.queries + column

    def seat(self, part, column):
        half = self.nodes // 2
        low = part % half
        node = (column & 1) * half + (low ^ (low >> 1))
        return node * self.queries + (column >> 1) * 2 + part // half

    def blocks(self):
        return [(p, c) for p in range(self.nodes) for c in range(self.queries)]

    def gather(self):
        return [(self.home(p, c), self.seat(p, c)) for p, c in self.blocks()]

    def give_back(self):
        return [(target, source) for source, target in self.gather()]

    def stays(self, part, column):
        return (column & 1) == part // (self.nodes // 2)

    def shift_from_home(self, step):
        return [
            (self.home(p, c), self.seat((p + step) % self.nodes, c))
            for p, c in self.blocks()
            if self.stays(p, c)
        ]

    def shift_from_seat(self, step):
        return [
            (self.seat(p, c), self.seat((p + step) % self.nodes, c))
            for p, c in self.blocks()
            if not self.stays(p, c)
        ]

    def near_table(self, step):
        table = [0] * (self.nodes * self.queries)
        for p, c in self.blocks():
            table[self.seat(p, c)] = int(self.stays((p - step) % self.nodes, c))
        return table

    def shift(self, step):
        return [
            (self.seat((p - step) % self.nodes, c), self.seat(p, c)) for p, c in self.blocks()
        ]

    def mirror(self):
        return [
            (self.seat(p, c), self.seat((p + self.nodes // 2) % self.nodes, c))
            for p, c in self.blocks()
        ]

    def parts(self):
        table = [0] * (self.nodes * self.queries)
        for p, c in self.blocks():
            table[self.seat(p, c)] = p
        return table


def spread(block_ref, window_ref, first):
    if block_ref.shape[1] == LANES:
        rows = block_ref.shape[0]

        def step(i, carry):
            at = pl.multiple_of(i * CHUNK, CHUNK)
            window_ref[pl.ds(first + at, CHUNK), :] = block_ref[pl.ds(at, CHUNK), :].astype(
                jnp.float32
            )
            return carry

        lax.fori_loop(0, rows // CHUNK, step, 0)
        return
    rows, cols = block_ref.shape
    groups = cols // LANES
    size = CHUNK // groups

    def step(i, carry):
        at = pl.multiple_of(i * size, size)
        for j in range(groups):
            window_ref[pl.ds(first + at * groups + j, size, stride=groups), :] = block_ref[
                pl.ds(at, size), j * LANES : (j + 1) * LANES
            ].astype(jnp.float32)
        return carry

    lax.fori_loop(0, rows // size, step, 0)


def clear(sums):
    def step(i, carry):
        at = pl.multiple_of(i * CHUNK, CHUNK)
        for ref in sums:
            ref[pl.ds(at, CHUNK), :] = jnp.zeros((CHUNK, LANES), jnp.float32)
        return carry

    lax.fori_loop(0, sums[0].shape[0] // CHUNK, step, 0)


def walk(groups, begin, end, from_ref, to_ref, rel_ref, window, table, sums):
    room = from_ref.shape[0] - UNROLL
    views = [[ref.at[pl.ds(u, room)] for ref in (from_ref, to_ref, rel_ref)] for u in range(UNROLL)]

    def step(i, carry):
        first = begin + i * UNROLL
        for u, (from_view, to_view, rel_view) in enumerate(views):
            source = pl.multiple_of(from_view[first], groups)
            target = pl.multiple_of(to_view[first], groups)
            scale = table[pl.ds(rel_view[first], groups, stride=0), :]
            sums[u % SUMS][pl.ds(target, groups), :] += (
                window[pl.ds(source, groups), :] * scale
            )
        return carry

    lax.fori_loop(0, (end - begin) // UNROLL, step, 0)


def total_of(sums, at):
    value = sums[0][pl.ds(at, CHUNK), :]
    for ref in sums[1:]:
        value = value + ref[pl.ds(at, CHUNK), :]
    return value


def fetch(pairs, sems):
    copies = [pltpu.make_async_copy(src, dst, sems.at[i]) for i, (src, dst) in enumerate(pairs)]
    for copy in copies:
        copy.start()
    return copies


def wait(copies):
    for copy in copies:
        copy.wait()


def bucket_kernel(
    edges_ref, out_ref, ends_ref, slots, rows, rels, pos, word, meta, pos_buf, word_buf, meta_buf,
    sems, *, tile_count, row_count, rel_count,
):
    lines = slots.shape[0]
    deep = lines // tile_count
    for t in range(tile_count):
        piece = slice(t * deep, (t + 1) * deep)
        at = 3 * t * deep
        slots[piece, :] = edges_ref[at : at + deep, :]
        rows[piece, :] = edges_ref[at + deep : at + 2 * deep, :] + 64 * t
        rels[piece, :] = edges_ref[at + 2 * deep : at + 3 * deep, :]
    slot = slots[...]
    quarter = sum(((slot >= k * row_count).astype(jnp.int32) for k in range(1, 4)))
    local = slot - quarter * row_count
    kind = jnp.where(
        quarter == 1, 0, jnp.where(quarter == 3, 1, jnp.where(quarter == 0, 2, 3))
    )
    second = jnp.where((kind == 1) | (kind == 3), row_count, 0)
    row_bits = (row_count - 1).bit_length()
    word[...] = (rels[...] << (2 * row_bits + 1)) | (rows[...] << (row_bits + 1)) | (second + local)
    shape = (LANES, LANES)
    upto = (lax.broadcasted_iota(jnp.int32, shape, 0) <= lax.broadcasted_iota(jnp.int32, shape, 1))
    upto = upto.astype(jnp.float32).astype(jnp.bfloat16)
    shape = (lines, lines)
    above = (lax.broadcasted_iota(jnp.int32, shape, 0) > lax.broadcasted_iota(jnp.int32, shape, 1))
    above = above.astype(jnp.float32).astype(jnp.bfloat16)
    ones = jnp.ones((LANES, LANES), jnp.bfloat16)
    place = jnp.zeros((lines, LANES), jnp.float32)
    begin = jnp.zeros((1, LANES), jnp.float32)
    for k in range(4):
        chosen = (kind == k).astype(jnp.float32)
        onehot = chosen.astype(jnp.bfloat16)
        within = jnp.dot(onehot, upto, preferred_element_type=jnp.float32)
        per_line = jnp.dot(onehot, ones, preferred_element_type=jnp.float32)
        before = jnp.dot(above, per_line.astype(jnp.bfloat16), preferred_element_type=jnp.float32)
        count = jnp.sum(per_line, axis=0, keepdims=True)
        place = place + chosen * (begin + before + within - 1.0)
        meta[k : k + 1, :] = (begin + count).astype(jnp.int32)
        begin = begin + jnp.floor((count + (UNROLL - 0.5)) / UNROLL) * UNROLL
        meta[k + 4 : k + 5, :] = begin.astype(jnp.int32)
    pos[...] = place.astype(jnp.int32)
    wait(fetch([(pos, pos_buf), (word, word_buf), (meta, meta_buf)], sems))

    def step(i, carry):
        for u in range(LANES):
            out_ref[pos_buf[i, u]] = word_buf[i, u]
        return carry

    lax.fori_loop(0, lines, step, 0)
    dummy = rel_count << (2 * row_bits + 1)

    def fill(i, carry):
        out_ref[i] = dummy
        return carry

    for k in range(4):
        lax.fori_loop(meta_buf[k, 0], meta_buf[k + 4, 0], fill, 0)
        ends_ref[k] = meta_buf[k + 4, 0]


def split(values):
    high = values.astype(jnp.bfloat16)
    low = (values - high.astype(jnp.float32)).astype(jnp.bfloat16)
    return jnp.concatenate([high, low], axis=1)


def split_weight(weight):
    wide = split(weight)
    return jnp.concatenate([wide, wide], axis=0)


def times(values, wide):
    both = jnp.dot(split(values), wide, preferred_element_type=jnp.float32)
    return both[:, :LANES] + both[:, LANES:]


def outer(left, right):
    return lax.dot_general(
        split(left), split(right), (((0,), (0,)), ((), ())), preferred_element_type=jnp.float32
    )


def quarters(wide):
    return (
        wide[:LANES, :LANES] + wide[LANES:, :LANES] + wide[:LANES, LANES:] + wide[LANES:, LANES:]
    )


def near_kernel(
    groups, index, ends, source, target, rel, own, mirror, tables, out,
    source_buf, target_buf, rel_buf, own_buf, mirror_buf, table_buf, window, sems, *sums,
):
    long = sums[0].shape[0]
    states = fetch([(own, own_buf), (mirror, mirror_buf)], sems)
    lists = fetch(
        [(source, source_buf), (target, target_buf), (rel, rel_buf), (tables.at[index], table_buf)],
        sems.at[pl.ds(2, 4)],
    )
    clear(sums)
    states[0].wait()
    spread(own_buf, window, 0)
    states[1].wait()
    spread(mirror_buf, window, long)
    wait(lists)
    walk(groups, 0, ends[1], source_buf, target_buf, rel_buf, window, table_buf, sums)
    parts = 4
    size = long // parts
    stores = []
    for k in range(parts):

        def step(i, carry):
            at = pl.multiple_of(k * size + i * CHUNK, CHUNK)
            sums[0][pl.ds(at, CHUNK), :] = total_of(sums, at)
            return carry

        lax.fori_loop(0, size // CHUNK, step, 0)
        piece = pl.ds(k * size, size)
        stores += fetch([(sums[0].at[piece, :], out.at[piece, :])], sems.at[pl.ds(6 + k, 1)])
    wait(stores)


def add_boundary(groups, heads, head_rows, ref, long):
    for q in range(head_rows.shape[0]):
        row = heads[q]

        @pl.when((row >= 0) & (row < long // groups))
        def _():
            at = row * groups + q * DIM // LANES
            ref[pl.ds(at, 1), :] += head_rows[q : q + 1, :]


def far_sums(groups, long, ends, heads, inputs, bufs, head_rows, window, sems, sums):
    source, target, rel, left, right, near, table = inputs
    source_buf, target_buf, rel_buf, left_buf, right_buf, table_buf = bufs
    states = []
    for k, (sides, buf) in enumerate(((left, left_buf), (right, right_buf))):
        if isinstance(sides, tuple):
            flag, early, late = sides
            for at, ref in ((1, early), (0, late)):

                @pl.when(flag == at)
                def _():
                    pltpu.make_async_copy(ref, buf, sems.at[k]).start()

            states.append(pltpu.make_async_copy(early, buf, sems.at[k]))
        else:
            states += fetch([(sides, buf)], sems.at[pl.ds(k, 1)])
    states += fetch([(near, sums[0].at[pl.ds(0, long), :])], sems.at[pl.ds(2, 1)])
    lists = fetch(
        [(source, source_buf), (target, target_buf), (rel, rel_buf), (table, table_buf)],
        sems.at[pl.ds(3, 4)],
    )
    clear([ref.at[pl.ds(0, long), :] for ref in sums[1:]])
    states[0].wait()
    spread(left_buf, window, 0)
    states[1].wait()
    spread(right_buf, window, long)
    states[2].wait()
    add_boundary(groups, heads, head_rows, sums[0], long)
    wait(lists)
    walk(groups, ends[1], ends[3], source_buf, target_buf, rel_buf, window, table_buf, sums)


def first_kernel(
    groups, ends, heads, flags, head_rows, weights, biases, source, target, rel, left_early, left_late,
    right_early, right_late, near, tables, own, state, mixed, update,
    source_buf, target_buf, rel_buf, left_buf, right_buf, table_buf, own_buf, window, mixed_buf,
    update_buf, state_buf, sems, *sums,
):
    long = sums[0].shape[0]
    extra = fetch([(own, own_buf)], sems.at[pl.ds(7, 1)])
    far_sums(
        groups, long, ends, heads,
        (source, target, rel, (flags[0], left_early, left_late), (flags[1], right_early, right_late))
        + (near, tables.at[0]),
        (source_buf, target_buf, rel_buf, left_buf, right_buf, table_buf), head_rows, window, sems,
        sums,
    )
    wait(extra)
    spread(own_buf, window, 0)
    wide = split_weight(weights[0])
    bias = biases[0]
    parts = 4
    size = long // parts
    stores = []
    for k in range(parts):

        def step(i, carry):
            rows = pl.ds(pl.multiple_of(k * size + i * CHUNK, CHUNK), CHUNK)
            mix = total_of(sums, pl.multiple_of(k * size + i * CHUNK, CHUNK))
            values = times(mix, wide) + bias
            mixed_buf[rows, :] = mix
            update_buf[rows, :] = values
            state_buf[rows, :] = (window[rows, :] + values * jax.nn.sigmoid(values)).astype(
                jnp.bfloat16
            )
            return carry

        lax.fori_loop(0, size // CHUNK, step, 0)
        rows = pl.ds(k * size, size)
        stores += fetch(
            [
                (state_buf.at[rows, :], state.at[rows, :]),
                (mixed_buf.at[rows, :], mixed.at[rows, :]),
                (update_buf.at[rows, :], update.at[rows, :]),
            ],
            sems.at[pl.ds(8 + 3 * k, 3)],
        )
    wait(stores)


def second_kernel(
    groups, ends, heads, head_rows, weights, biases, source, target, rel, left, right, near, tables, own,
    cotangent,
    state, grad_mixed, mixed, grad, to_left, to_right,
    source_buf, target_buf, rel_buf, left_buf, right_buf, table_buf, own_buf, cotangent_buf, window,
    mixed_buf, grad_buf, grad_mixed_buf, state_buf, left_out, right_out, sems, *sums,
):
    long = window.shape[0] // 2
    extra = fetch([(own, own_buf), (cotangent, cotangent_buf)], sems.at[pl.ds(7, 2)])
    far_sums(
        groups, long, ends, heads, (source, target, rel, left, right, near, tables.at[1]),
        (source_buf, target_buf, rel_buf, left_buf, right_buf, table_buf), head_rows, window, sems,
        sums,
    )
    wait(extra)
    spread(own_buf, window, 0)
    spread(cotangent_buf, window, long)
    wide = split_weight(weights[1])
    wide_back = split_weight(weights[1].T)
    bias = biases[1]

    def step(i, carry):
        at = pl.multiple_of(i * CHUNK, CHUNK)
        rows = pl.ds(at, CHUNK)
        mix = total_of(sums, at)
        values = times(mix, wide) + bias
        sigma = jax.nn.sigmoid(values)
        window[rows, :] += values * sigma
        behind = pl.ds(long + at, CHUNK)
        slope = window[behind, :] * (sigma * (1.0 + values * (1.0 - sigma)))
        back = times(slope, wide_back).astype(jnp.bfloat16)
        mixed_buf[rows, :] = mix
        grad_buf[rows, :] = slope
        grad_mixed_buf[rows, :] = back
        window[behind, :] = back.astype(jnp.float32)
        for ref in sums:
            ref[rows, :] = jnp.zeros((CHUNK, LANES), jnp.float32)
            ref[behind, :] = jnp.zeros((CHUNK, LANES), jnp.float32)
        return carry

    lax.fori_loop(0, long // CHUNK, step, 0)
    size = CHUNK // groups

    def store(i, carry):
        at = pl.multiple_of(i * size, size)
        for j in range(groups):
            state_buf[pl.ds(at, size), j * LANES : (j + 1) * LANES] = window[
                pl.ds(at * groups + j, size, stride=groups), :
            ].astype(jnp.bfloat16)
        return carry

    lax.fori_loop(0, long // CHUNK, store, 0)
    stores = fetch(
        [(state_buf, state), (grad_mixed_buf, grad_mixed), (mixed_buf, mixed), (grad_buf, grad)],
        sems.at[pl.ds(9, 4)],
    )
    walk(
        groups, ends[1], ends[3], target_buf, source_buf, rel_buf, window.at[pl.ds(long, long), :],
        table_buf, sums,
    )

    for k, (buf, out) in enumerate(((left_out, to_left), (right_out, to_right))):

        def total(i, carry):
            at = pl.multiple_of(i * CHUNK, CHUNK)
            buf[pl.ds(at, CHUNK), :] = total_of(sums, k * long + at).astype(jnp.bfloat16)
            return carry

        lax.fori_loop(0, long // CHUNK, total, 0)
        stores += fetch([(buf, out)], sems.at[pl.ds(13 + k, 1)])
    wait(stores)


def adjoint_kernel(
    groups, ends, source, target, rel, grad_mixed, tables, cotangent, mixed, grad,
    base, to_mirror, weight_sum, bias_sum,
    source_buf, target_buf, rel_buf, grad_mixed_buf, table_buf, cotangent_buf, mixed_buf, grad_buf,
    mirror_out, window, wide_sum, sems, *sums,
):
    long = window.shape[0]
    loads = fetch([(grad_mixed, grad_mixed_buf)], sems)
    lists = fetch(
        [(source, source_buf), (target, target_buf), (rel, rel_buf), (tables.at[1], table_buf)],
        sems.at[pl.ds(1, 4)],
    )
    late = fetch(
        [(cotangent, cotangent_buf), (mixed, mixed_buf), (grad, grad_buf)], sems.at[pl.ds(5, 3)]
    )
    clear(sums)
    wait(loads)
    spread(grad_mixed_buf, window, 0)
    wait(lists)
    walk(groups, 0, ends[1], target_buf, source_buf, rel_buf, window, table_buf, sums)

    def total(i, carry):
        at = pl.multiple_of(i * CHUNK, CHUNK)
        mirror_out[pl.ds(at, CHUNK), :] = total_of(sums, long + at).astype(jnp.bfloat16)
        return carry

    lax.fori_loop(0, long // CHUNK, total, 0)
    stores = fetch([(mirror_out, to_mirror)], sems.at[pl.ds(8, 1)])
    wait(late)
    spread(cotangent_buf, window, 0)
    wide_sum[...] = jnp.zeros_like(wide_sum)
    bias_sum[...] = jnp.zeros_like(bias_sum)

    def step(i, carry):
        at = pl.multiple_of(i * CHUNK, CHUNK)
        rows = pl.ds(at, CHUNK)
        window[rows, :] += total_of(sums, at)
        values = grad_buf[rows, :]
        wide_sum[...] += outer(mixed_buf[rows, :], values)
        bias_sum[...] += jnp.sum(values, axis=0, keepdims=True)
        return carry

    lax.fori_loop(0, long // CHUNK, step, 0)
    stores += fetch([(window, base)], sems.at[pl.ds(9, 1)])
    weight_sum[...] = quarters(wide_sum[...])
    wait(stores)


def folded(wide):
    value = wide[:DIM, :DIM]
    for g in range(1, LANES // DIM):
        value = value + wide[g * DIM : (g + 1) * DIM, g * DIM : (g + 1) * DIM]
    return value


def folded_row(wide):
    value = wide[:, :DIM]
    for g in range(1, LANES // DIM):
        value = value + wide[:, g * DIM : (g + 1) * DIM]
    return value


def last_kernel(
    base, left, right, mirror, update, mixed, weight_one, bias_one, out, wide_sum, bias_sum
):
    @pl.when(pl.program_id(0) == 0)
    def _():
        wide_sum[...] = jnp.zeros_like(wide_sum)
        bias_sum[...] = jnp.zeros_like(bias_sum)

    state_grad = base[...]
    for ref in (left, right, mirror):
        state_grad = state_grad + ref[...].astype(jnp.float32)
    grad = state_grad * silu_slope(update[...])
    wide_sum[...] += outer(mixed[...], grad)
    bias_sum[...] += jnp.sum(grad, axis=0, keepdims=True)

    @pl.when(pl.program_id(0) == pl.num_programs(0) - 1)
    def _():
        out[...] = jnp.zeros_like(out)
        out[0:DIM, 0:DIM] = folded(quarters(wide_sum[...]))
        out[DIM : 2 * DIM, 0:DIM] = folded(weight_one[...])
        out[2 * DIM : 2 * DIM + 1, 0:DIM] = folded_row(bias_sum[...])
        out[2 * DIM + 1 : 2 * DIM + 2, 0:DIM] = folded_row(bias_one[...])


def edge_lists(edges, tile_count, slot_total, row_count, groups, rel_count):
    edge_count = tile_count * slot_total
    lines = edge_count // LANES
    row_bits = (row_count - 1).bit_length()
    room = (edge_count + 5 * UNROLL + LANES - 1) // LANES * LANES
    flat = pltpu.VMEM((lines, LANES), jnp.int32)
    flat_smem = pltpu.SMEM((lines, LANES), jnp.int32)
    words, ends = pl.pallas_call(
        functools.partial(
            bucket_kernel, tile_count=tile_count, row_count=row_count, rel_count=rel_count
        ),
        out_shape=[jax.ShapeDtypeStruct((room,), jnp.int32), jax.ShapeDtypeStruct((4,), jnp.int32)],
        in_specs=[VMEM],
        out_specs=[SMEM] * 2,
        scratch_shapes=[flat] * 5
        + [pltpu.VMEM((8, LANES), jnp.int32), flat_smem, flat_smem]
        + [pltpu.SMEM((8, LANES), jnp.int32), pltpu.SemaphoreType.DMA((3,))],
        name="bucket",
    )(edges)
    source = (words & (2 * row_count - 1)) * groups
    target = ((words >> (row_bits + 1)) & (row_count - 1)) * groups
    return ends, source, target, words >> (2 * row_bits + 1)


def body(
    entity_state,
    edge_tiles,
    query_head,
    query_relation,
    query_table,
    rel_vectors,
    mix_weight,
    mix_bias,
    cotangent,
):
    row_count, col_count = entity_state.shape
    groups = col_count // LANES
    long = row_count * groups
    query_count = query_head.shape[0]
    rel_count = rel_vectors.shape[1]
    seats = Seats(lax.axis_size("node"), lax.axis_size("query"))

    def send(block, route):
        return lax.ppermute(block, AXES, route)

    def run(fn, args, specs, outs, out_specs, scratch):
        return pl.pallas_call(
            fn, out_shape=outs, in_specs=specs, out_specs=out_specs, scratch_shapes=scratch,
        )(*args)

    wide_f32 = jax.ShapeDtypeStruct((long, LANES), jnp.float32)
    wide_bf16 = jax.ShapeDtypeStruct((long, LANES), jnp.bfloat16)
    f32_buf = pltpu.VMEM((long, LANES), jnp.float32)
    bf16_buf = pltpu.VMEM((long, LANES), jnp.bfloat16)
    pair = pltpu.VMEM((2 * long, LANES), jnp.float32)
    sums = [f32_buf] * SUMS
    pair_sums = [pair] * SUMS
    square = jax.ShapeDtypeStruct((LANES, LANES), jnp.float32)
    line = jax.ShapeDtypeStruct((1, LANES), jnp.float32)

    flat = jnp.concatenate([edge_tiles.reshape(-1), query_head, query_relation])
    edge_total = edge_tiles.size
    flat = jnp.pad(flat, (0, -flat.shape[0] % (8 * LANES))).reshape(-1, LANES)
    edges = send(flat, seats.gather())
    flat = edges.reshape(-1)
    state_zero = send(entity_state, seats.gather())
    left_early = send(entity_state, seats.shift_from_home(1))
    right_early = send(entity_state, seats.shift_from_home(-1))
    own_head = flat[edge_total : edge_total + query_count]
    own_relation = flat[edge_total + query_count : edge_total + 2 * query_count]
    grad_out = send(cotangent, seats.gather())

    linear = lax.axis_index("node") * seats.queries + lax.axis_index("query")
    part = jnp.array(seats.parts(), jnp.int32)[linear]
    heads = own_head - part * row_count
    flags = jnp.array([seats.near_table(1), seats.near_table(-1)], jnp.int32)[:, linear]
    choose_rel = (own_relation[:, None] == lax.iota(jnp.int32, query_table.shape[0])[None, :]).astype(
        jnp.float32
    )
    query_vec = (
        jnp.dot(choose_rel, query_table, precision=HIGHEST, preferred_element_type=jnp.float32)
        .astype(jnp.bfloat16)
        .astype(jnp.float32)
    )
    repeat = LANES // DIM
    lane_group = lax.iota(jnp.int32, LANES) // DIM
    head_rows = jnp.where(
        lane_group[None, :] == (lax.iota(jnp.int32, query_count) % repeat)[:, None],
        jnp.tile(query_vec, (1, repeat)),
        0.0,
    )
    tables = jnp.tile(jnp.pad(rel_vectors, ((0, 0), (0, -rel_count % 8 or 8), (0, 0))), (1, 1, repeat))
    same = lane_group[:, None] == lane_group[None, :]
    weights = jnp.where(same[None], jnp.tile(mix_weight, (1, repeat, repeat)), 0.0)
    biases = jnp.tile(mix_bias, (1, repeat))[:, None, :]
    ends, source, target, rel = edge_lists(
        edges, edge_tiles.shape[0], edge_tiles.shape[2], row_count, groups, rel_count
    )
    lists = [source, target, rel]
    list_bufs = [pltpu.SMEM(source.shape, jnp.int32)] * 3
    table_buf = pltpu.VMEM(tables.shape[1:], jnp.float32)

    def sems(count):
        return pltpu.SemaphoreType.DMA((count,))

    def halo(state, index):
        buf = pltpu.VMEM(state.shape, jnp.bfloat16)
        mirror = send(state, seats.mirror())
        left = send(state, seats.shift(1) if index else seats.shift_from_seat(1))
        right = send(state, seats.shift(-1) if index else seats.shift_from_seat(-1))
        near = run(
            functools.partial(near_kernel, groups, index),
            [ends, *lists, state, mirror, tables],
            [SMEM] + [ANY] * 6,
            wide_f32,
            ANY,
            [*list_bufs, buf, buf, table_buf, pair, sems(10), *sums],
        )
        return left, right, near

    left, right, near = halo(state_zero, 0)
    block_buf = pltpu.VMEM(state_zero.shape, jnp.bfloat16)
    state_one, mixed_zero, update_zero = run(
        functools.partial(first_kernel, groups),
        [ends, heads, flags, head_rows, weights, biases, *lists, left_early, left, right_early, right]
        + [near, tables, state_zero],
        [SMEM] * 3 + [VMEM] * 3 + [ANY] * 10,
        [wide_bf16, wide_f32, wide_f32],
        [ANY] * 3,
        [*list_bufs, block_buf, block_buf, table_buf, block_buf, pair, f32_buf, f32_buf, bf16_buf, sems(20)]
        + sums,
    )
    left, right, near = halo(state_one, 1)
    state_two, grad_mixed, mixed_one, grad_one, to_left, to_right = run(
        functools.partial(second_kernel, groups),
        [ends, heads, head_rows, weights, biases, *lists, left, right, near, tables, state_one, grad_out],
        [SMEM] * 2 + [VMEM] * 3 + [ANY] * 9,
        [jax.ShapeDtypeStruct(entity_state.shape, jnp.bfloat16), wide_bf16, wide_f32, wide_f32]
        + [wide_bf16] * 2,
        [ANY] * 6,
        [*list_bufs, bf16_buf, bf16_buf, table_buf, bf16_buf, block_buf, pair, f32_buf, f32_buf, bf16_buf]
        + [block_buf, bf16_buf, bf16_buf, sems(15), *pair_sums],
    )
    from_right = send(to_left, seats.shift(-1))
    from_left = send(to_right, seats.shift(1))
    final_state = send(state_two, seats.give_back())
    base, to_mirror, weight_one, bias_one = run(
        functools.partial(adjoint_kernel, groups),
        [ends, *lists, grad_mixed, tables, grad_out, mixed_one, grad_one],
        [SMEM] + [ANY] * 8,
        [wide_f32, wide_bf16, square, line],
        [ANY] * 2 + [VMEM] * 2,
        [*list_bufs, bf16_buf, table_buf, block_buf, f32_buf, f32_buf, bf16_buf, f32_buf]
        + [pltpu.VMEM((2 * LANES, 2 * LANES), jnp.float32), sems(10), *pair_sums],
    )
    from_mirror = send(to_mirror, seats.mirror())
    steps = 8
    rows = pl.BlockSpec((long // steps, LANES), lambda i: (i, 0))
    whole = lambda shape: pl.BlockSpec(shape, lambda i: (0, 0))
    grads = pl.pallas_call(
        last_kernel,
        out_shape=jax.ShapeDtypeStruct((2 * DIM + 8, LANES), jnp.float32),
        grid=(steps,),
        in_specs=[rows] * 6 + [whole((LANES, LANES)), whole((1, LANES))],
        out_specs=whole((2 * DIM + 8, LANES)),
        scratch_shapes=[
            pltpu.VMEM((2 * LANES, 2 * LANES), jnp.float32),
            pltpu.VMEM((1, LANES), jnp.float32),
        ],
        name="last",
    )(base, from_left, from_right, from_mirror, update_zero, mixed_zero, weight_one, bias_one)
    devices = seats.nodes * seats.queries
    reach = 1
    while reach < devices:
        grads = grads + send(grads, [(i, i ^ reach) for i in range(devices)])
        reach *= 2
    weight_grads = grads[: 2 * DIM, :DIM].reshape(2, DIM, DIM)
    bias_grads = grads[2 * DIM : 2 * DIM + 2, :DIM]
    return (final_state, weight_grads, bias_grads)


def solution(mesh):
    placed = (
        P("node", "query"),
        P("node", None, None),
        P("query"),
        P("query"),
        P(),
        P(),
        P(),
        P(),
        P("node", "query"),
    )

    return jax.shard_map(
        body, mesh=mesh, in_specs=placed, out_specs=(P("node", "query"), P(), P()), check_vma=False
    )
```

```python
import functools

import jax
import jax.numpy as jnp
from jax import lax
from jax.experimental import pallas as pl
from jax.experimental.pallas import tpu as pltpu
from jax.sharding import PartitionSpec as P


DIM = 32
LANES = 128
UNROLL = 48
SUMS = 3
CHUNK = 256
DENSE = 512
LINE = 1024
AXES = ("node", "query")
HIGHEST = lax.Precision.HIGHEST
SMEM = pl.BlockSpec(memory_space=pltpu.SMEM)
VMEM = pl.BlockSpec(memory_space=pltpu.VMEM)
ANY = pl.BlockSpec(memory_space=pl.ANY)


def silu_slope(values):
    sigma = jax.nn.sigmoid(values)
    return sigma * (1.0 + values * (1.0 - sigma))


class Seats:
    def __init__(self, nodes, queries):
        self.nodes, self.queries = nodes, queries

    def home(self, part, column):
        return part * self.queries + column

    def seat(self, part, column):
        half = self.nodes // 2
        low = part % half
        node = (column & 1) * half + (low ^ (low >> 1))
        return node * self.queries + (column >> 1) * 2 + part // half

    def blocks(self):
        return [(p, c) for p in range(self.nodes) for c in range(self.queries)]

    def gather(self):
        return [(self.home(p, c), self.seat(p, c)) for p, c in self.blocks()]

    def give_back(self):
        return [(target, source) for source, target in self.gather()]

    def shift(self, step):
        return [
            (self.seat((p - step) % self.nodes, c), self.seat(p, c)) for p, c in self.blocks()
        ]

    def mirror(self):
        return [
            (self.seat(p, c), self.seat((p + self.nodes // 2) % self.nodes, c))
            for p, c in self.blocks()
        ]

    def parts(self):
        table = [0] * (self.nodes * self.queries)
        for p, c in self.blocks():
            table[self.seat(p, c)] = p
        return table


def spread(block_ref, window_ref, first):
    if block_ref.shape[1] == LANES:
        rows = block_ref.shape[0]

        def step(i, carry):
            at = pl.multiple_of(i * CHUNK, CHUNK)
            window_ref[pl.ds(first + at, CHUNK), :] = block_ref[pl.ds(at, CHUNK), :].astype(
                jnp.float32
            )
            return carry

        lax.fori_loop(0, rows // CHUNK, step, 0)
        return
    rows, cols = block_ref.shape
    groups = cols // LANES
    size = CHUNK // groups

    def step(i, carry):
        at = pl.multiple_of(i * size, size)
        for j in range(groups):
            window_ref[pl.ds(first + at * groups + j, size, stride=groups), :] = block_ref[
                pl.ds(at, size), j * LANES : (j + 1) * LANES
            ].astype(jnp.float32)
        return carry

    lax.fori_loop(0, rows // size, step, 0)


def clear(sums):
    def step(i, carry):
        at = pl.multiple_of(i * CHUNK, CHUNK)
        for ref in sums:
            ref[pl.ds(at, CHUNK), :] = jnp.zeros((CHUNK, LANES), jnp.float32)
        return carry

    lax.fori_loop(0, sums[0].shape[0] // CHUNK, step, 0)


def walk(groups, begin, end, from_ref, to_ref, rel_ref, window, table, sums):
    room = from_ref.shape[0] - UNROLL
    views = [[ref.at[pl.ds(u, room)] for ref in (from_ref, to_ref, rel_ref)] for u in range(UNROLL)]

    def step(i, carry):
        first = begin + i * UNROLL
        for u, (from_view, to_view, rel_view) in enumerate(views):
            source = pl.multiple_of(from_view[first], groups)
            target = pl.multiple_of(to_view[first], groups)
            scale = table[pl.ds(rel_view[first], groups, stride=0), :]
            sums[u % SUMS][pl.ds(target, groups), :] += (
                window[pl.ds(source, groups), :] * scale
            )
        return carry

    lax.fori_loop(0, (end - begin) // UNROLL, step, 0)


def total_of(sums, at, size=CHUNK):
    value = sums[0][pl.ds(at, size), :]
    for ref in sums[1:]:
        value = value + ref[pl.ds(at, size), :]
    return value


def fetch(pairs, sems):
    copies = [pltpu.make_async_copy(src, dst, sems.at[i]) for i, (src, dst) in enumerate(pairs)]
    for copy in copies:
        copy.start()
    return copies


def wait(copies):
    for copy in copies:
        copy.wait()


def bucket_kernel(
    edges_ref, out_ref, ends_ref, slots, rows, rels, pos, word, meta, pos_buf, word_buf, meta_buf,
    sems, *, tile_count, row_count, rel_count,
):
    lines = slots.shape[0]
    first = 64 * lax.broadcasted_iota(jnp.int32, (tile_count, LANES), 0)
    for j in range(lines // tile_count):
        piece = slice(j * tile_count, (j + 1) * tile_count)
        lanes = slice(j * LANES, (j + 1) * LANES)
        slots[piece, :] = edges_ref[0, :, lanes]
        rows[piece, :] = edges_ref[1, :, lanes] + first
        rels[piece, :] = edges_ref[2, :, lanes]
    slot = slots[...]
    quarter = sum(((slot >= k * row_count).astype(jnp.int32) for k in range(1, 4)))
    local = slot - quarter * row_count
    kind = jnp.where(
        quarter == 1, 0, jnp.where(quarter == 3, 1, jnp.where(quarter == 0, 2, 3))
    )
    second = jnp.where((kind == 1) | (kind == 3), row_count, 0)
    row_bits = (row_count - 1).bit_length()
    word[...] = (rels[...] << (2 * row_bits + 1)) | (rows[...] << (row_bits + 1)) | (second + local)
    shape = (LANES, LANES)
    upto = (lax.broadcasted_iota(jnp.int32, shape, 0) <= lax.broadcasted_iota(jnp.int32, shape, 1))
    upto = upto.astype(jnp.float32).astype(jnp.bfloat16)
    shape = (lines, lines)
    above = (lax.broadcasted_iota(jnp.int32, shape, 0) > lax.broadcasted_iota(jnp.int32, shape, 1))
    above = above.astype(jnp.float32).astype(jnp.bfloat16)
    ones = jnp.ones((LANES, LANES), jnp.bfloat16)
    place = jnp.zeros((lines, LANES), jnp.float32)
    begin = jnp.zeros((1, LANES), jnp.float32)
    for k in range(4):
        chosen = (kind == k).astype(jnp.float32)
        onehot = chosen.astype(jnp.bfloat16)
        within = jnp.dot(onehot, upto, preferred_element_type=jnp.float32)
        per_line = jnp.dot(onehot, ones, preferred_element_type=jnp.float32)
        before = jnp.dot(above, per_line.astype(jnp.bfloat16), preferred_element_type=jnp.float32)
        count = jnp.sum(per_line, axis=0, keepdims=True)
        place = place + chosen * (begin + before + within - 1.0)
        meta[k : k + 1, :] = (begin + count).astype(jnp.int32)
        begin = begin + jnp.floor((count + (UNROLL - 0.5)) / UNROLL) * UNROLL
        meta[k + 4 : k + 5, :] = begin.astype(jnp.int32)
    pos[...] = place.astype(jnp.int32)
    wait(fetch([(pos, pos_buf), (word, word_buf), (meta, meta_buf)], sems))

    def step(i, carry):
        for u in range(LANES):
            out_ref[pos_buf[i, u]] = word_buf[i, u]
        return carry

    lax.fori_loop(0, lines, step, 0)
    dummy = rel_count << (2 * row_bits + 1)

    def fill(i, carry):
        out_ref[i] = dummy
        return carry

    for k in range(4):
        lax.fori_loop(meta_buf[k, 0], meta_buf[k + 4, 0], fill, 0)
        ends_ref[k] = meta_buf[k + 4, 0]


def split(values):
    high = values.astype(jnp.bfloat16)
    low = (values - high.astype(jnp.float32)).astype(jnp.bfloat16)
    return jnp.concatenate([high, low], axis=1)


def split_weight(weight):
    wide = split(weight)
    return jnp.concatenate([wide, wide], axis=0)


def times(values, wide):
    both = jnp.dot(split(values), wide, preferred_element_type=jnp.float32)
    return both[:, :LANES] + both[:, LANES:]


def outer(left, right):
    return lax.dot_general(
        split(left), split(right), (((0,), (0,)), ((), ())), preferred_element_type=jnp.float32
    )


def quarters(wide):
    return (
        wide[:LANES, :LANES] + wide[LANES:, :LANES] + wide[:LANES, LANES:] + wide[LANES:, LANES:]
    )


def near_kernel(
    groups, index, flat, own, mirror, tables, out,
    source, target, rel, tail, own_buf, mirror_buf, table_buf, window, sems, *sums,
):
    long = sums[0].shape[0]
    lists = fetch_lists(flat, (source, target, rel, tail), tables, index, table_buf, sems)
    states = fetch([(own, own_buf), (mirror, mirror_buf)], sems.at[pl.ds(5, 2)])
    clear(sums)
    states[0].wait()
    spread(own_buf, window, 0)
    states[1].wait()
    spread(mirror_buf, window, long)
    wait(lists)
    walk(groups, 0, tail[1], source, target, rel, window, table_buf, sums)
    parts = 4
    size = long // parts
    stores = []
    for k in range(parts):

        def step(i, carry):
            at = pl.multiple_of(k * size + i * CHUNK, CHUNK)
            sums[0][pl.ds(at, CHUNK), :] = total_of(sums, at)
            return carry

        lax.fori_loop(0, size // CHUNK, step, 0)
        piece = pl.ds(k * size, size)
        stores += fetch([(sums[0].at[piece, :], out.at[piece, :])], sems.at[pl.ds(7 + k, 1)])
    wait(stores)


def add_boundary(groups, heads, head_rows, ref, long):
    for q in range(head_rows.shape[0]):
        row = heads[4 + q]

        @pl.when((row >= 0) & (row < long // groups))
        def _():
            at = row * groups + q * DIM // LANES
            ref[pl.ds(at, 1), :] += head_rows[q : q + 1, :]


def fetch_lists(flat, bufs, tables, index, table_buf, sems):
    room = bufs[0].shape[0]
    pairs = [(flat.at[pl.ds(k * room, buf.shape[0])], buf) for k, buf in enumerate(bufs)]
    return fetch(pairs + [(tables.at[index], table_buf)], sems)


def far_sums(groups, long, index, flat, tables, states, list_bufs, bufs, head_rows, window, sems, sums):
    left, right, near = states
    left_buf, right_buf, table_buf = bufs
    lists = fetch_lists(flat, list_bufs, tables, index, table_buf, sems)
    states = fetch(
        [(left, left_buf), (right, right_buf), (near, sums[0].at[pl.ds(0, long), :])],
        sems.at[pl.ds(5, 3)],
    )
    clear([ref.at[pl.ds(0, long), :] for ref in sums[1:]])
    states[0].wait()
    spread(left_buf, window, 0)
    states[1].wait()
    spread(right_buf, window, long)
    states[2].wait()
    wait(lists)
    _, _, _, tail = list_bufs
    add_boundary(groups, tail, head_rows, sums[0], long)


def first_kernel(
    groups, head_rows, weights, biases, flat, left, right, near, tables, own, state, mixed, update,
    source, target, rel, tail, left_buf, right_buf, table_buf, own_buf, window, mixed_buf, update_buf,
    state_buf, sems, *sums,
):
    long = sums[0].shape[0]
    far_sums(
        groups, long, 0, flat, tables, (left, right, near), (source, target, rel, tail),
        (left_buf, right_buf, table_buf), head_rows, window, sems, sums,
    )
    extra = fetch([(own, own_buf)], sems.at[pl.ds(8, 1)])
    walk(groups, tail[1], tail[3], source, target, rel, window, table_buf, sums)
    wait(extra)
    spread(own_buf, window, 0)
    wide = split_weight(weights[0])
    bias = biases[0]
    parts = 4
    size = long // parts
    stores = []
    for k in range(parts):

        def step(i, carry):
            at = pl.multiple_of(k * size + i * DENSE, DENSE)
            rows = pl.ds(at, DENSE)
            mix = total_of(sums, at, DENSE)
            values = times(mix, wide) + bias
            mixed_buf[rows, :] = mix
            update_buf[rows, :] = values
            state_buf[rows, :] = (window[rows, :] + values * jax.nn.sigmoid(values)).astype(
                jnp.bfloat16
            )
            return carry

        lax.fori_loop(0, size // DENSE, step, 0)
        rows = pl.ds(k * size, size)
        stores += fetch(
            [
                (state_buf.at[rows, :], state.at[rows, :]),
                (mixed_buf.at[rows, :], mixed.at[rows, :]),
                (update_buf.at[rows, :], update.at[rows, :]),
            ],
            sems.at[pl.ds(9 + 3 * k, 3)],
        )
    wait(stores)


def second_kernel(
    groups, head_rows, weights, biases, flat, left, right, near, tables, own, cotangent,
    state, grad_mixed, mixed, grad, to_left, to_right,
    source, target, rel, tail, left_buf, right_buf, table_buf, own_buf, cotangent_buf, window,
    mixed_buf, grad_buf, grad_mixed_buf, state_buf, left_out, right_out, sems, *sums,
):
    long = window.shape[0] // 2
    far_sums(
        groups, long, 1, flat, tables, (left, right, near), (source, target, rel, tail),
        (left_buf, right_buf, table_buf), head_rows, window, sems, sums,
    )
    extra = fetch([(own, own_buf), (cotangent, cotangent_buf)], sems.at[pl.ds(8, 2)])
    walk(groups, tail[1], tail[3], source, target, rel, window, table_buf, sums)
    wait(extra)
    spread(own_buf, window, 0)
    spread(cotangent_buf, window, long)
    wide = split_weight(weights[1])
    wide_back = split_weight(weights[1].T)
    bias = biases[1]

    def step(i, carry):
        at = pl.multiple_of(i * DENSE, DENSE)
        rows = pl.ds(at, DENSE)
        mix = total_of(sums, at, DENSE)
        values = times(mix, wide) + bias
        sigma = jax.nn.sigmoid(values)
        window[rows, :] += values * sigma
        behind = pl.ds(long + at, DENSE)
        slope = window[behind, :] * (sigma * (1.0 + values * (1.0 - sigma)))
        back = times(slope, wide_back).astype(jnp.bfloat16)
        mixed_buf[rows, :] = mix
        grad_buf[rows, :] = slope
        grad_mixed_buf[rows, :] = back
        window[behind, :] = back.astype(jnp.float32)
        for ref in sums:
            ref[rows, :] = jnp.zeros((DENSE, LANES), jnp.float32)
            ref[behind, :] = jnp.zeros((DENSE, LANES), jnp.float32)
        return carry

    lax.fori_loop(0, long // DENSE, step, 0)
    size = CHUNK // groups

    def store(i, carry):
        at = pl.multiple_of(i * size, size)
        for j in range(groups):
            state_buf[pl.ds(at, size), j * LANES : (j + 1) * LANES] = window[
                pl.ds(at * groups + j, size, stride=groups), :
            ].astype(jnp.bfloat16)
        return carry

    lax.fori_loop(0, long // CHUNK, store, 0)
    stores = fetch(
        [(state_buf, state), (grad_mixed_buf, grad_mixed), (mixed_buf, mixed), (grad_buf, grad)],
        sems.at[pl.ds(10, 4)],
    )
    walk(
        groups, tail[1], tail[3], target, source, rel, window.at[pl.ds(long, long), :], table_buf, sums,
    )

    for k, (buf, out) in enumerate(((left_out, to_left), (right_out, to_right))):

        def total(i, carry):
            at = pl.multiple_of(i * CHUNK, CHUNK)
            buf[pl.ds(at, CHUNK), :] = total_of(sums, k * long + at).astype(jnp.bfloat16)
            return carry

        lax.fori_loop(0, long // CHUNK, total, 0)
        stores += fetch([(buf, out)], sems.at[pl.ds(14 + k, 1)])
    wait(stores)


def adjoint_kernel(
    groups, flat, grad_mixed, tables, cotangent, mixed, grad,
    base, to_mirror, weight_sum, bias_sum,
    source, target, rel, tail, grad_mixed_buf, table_buf, cotangent_buf, mixed_buf, grad_buf,
    mirror_out, window, wide_sum, sems, *sums,
):
    long = window.shape[0]
    lists = fetch_lists(flat, (source, target, rel, tail), tables, 1, table_buf, sems)
    loads = fetch([(grad_mixed, grad_mixed_buf)], sems.at[pl.ds(5, 1)])
    clear(sums)
    wait(loads)
    spread(grad_mixed_buf, window, 0)
    wait(lists)
    late = fetch(
        [(cotangent, cotangent_buf), (mixed, mixed_buf), (grad, grad_buf)], sems.at[pl.ds(6, 3)]
    )
    walk(groups, 0, tail[1], target, source, rel, window, table_buf, sums)

    def total(i, carry):
        at = pl.multiple_of(i * CHUNK, CHUNK)
        mirror_out[pl.ds(at, CHUNK), :] = total_of(sums, long + at).astype(jnp.bfloat16)
        return carry

    lax.fori_loop(0, long // CHUNK, total, 0)
    stores = fetch([(mirror_out, to_mirror)], sems.at[pl.ds(9, 1)])
    wait(late)
    spread(cotangent_buf, window, 0)
    wide_sum[...] = jnp.zeros_like(wide_sum)
    bias_sum[...] = jnp.zeros_like(bias_sum)

    def step(i, carry):
        at = pl.multiple_of(i * DENSE, DENSE)
        rows = pl.ds(at, DENSE)
        window[rows, :] += total_of(sums, at, DENSE)
        values = grad_buf[rows, :]
        wide_sum[...] += outer(mixed_buf[rows, :], values)
        bias_sum[...] += jnp.sum(values, axis=0, keepdims=True)
        return carry

    lax.fori_loop(0, long // DENSE, step, 0)
    stores += fetch([(window, base)], sems.at[pl.ds(10, 1)])
    weight_sum[...] = quarters(wide_sum[...])
    wait(stores)


def copy_kernel(source, out, sems):
    wait(fetch([(source, out)], sems))


def folded(wide):
    value = wide[:DIM, :DIM]
    for g in range(1, LANES // DIM):
        value = value + wide[g * DIM : (g + 1) * DIM, g * DIM : (g + 1) * DIM]
    return value


def folded_row(wide):
    value = wide[:, :DIM]
    for g in range(1, LANES // DIM):
        value = value + wide[:, g * DIM : (g + 1) * DIM]
    return value


def last_kernel(
    base, left, right, mirror, update, mixed, weight_one, bias_one, out, wide_sum, bias_sum
):
    @pl.when(pl.program_id(0) == 0)
    def _():
        wide_sum[...] = jnp.zeros_like(wide_sum)
        bias_sum[...] = jnp.zeros_like(bias_sum)

    state_grad = base[...]
    for ref in (left, right, mirror):
        state_grad = state_grad + ref[...].astype(jnp.float32)
    grad = state_grad * silu_slope(update[...])
    wide_sum[...] += outer(mixed[...], grad)
    bias_sum[...] += jnp.sum(grad, axis=0, keepdims=True)

    @pl.when(pl.program_id(0) == pl.num_programs(0) - 1)
    def _():
        out[...] = jnp.zeros_like(out)
        out[0:DIM, 0:DIM] = folded(quarters(wide_sum[...]))
        out[DIM : 2 * DIM, 0:DIM] = folded(weight_one[...])
        out[2 * DIM : 2 * DIM + 1, 0:DIM] = folded_row(bias_sum[...])
        out[2 * DIM + 1 : 2 * DIM + 2, 0:DIM] = folded_row(bias_one[...])


def edge_lists(edge_tiles, row_count, groups, rel_count):
    tile_count, _, slot_total = edge_tiles.shape
    lines = tile_count * slot_total // LANES
    row_bits = (row_count - 1).bit_length()
    room = (tile_count * slot_total + 5 * UNROLL + LINE - 1) // LINE * LINE
    flat = pltpu.VMEM((lines, LANES), jnp.int32)
    flat_smem = pltpu.SMEM((lines, LANES), jnp.int32)
    words, ends = pl.pallas_call(
        functools.partial(
            bucket_kernel, tile_count=tile_count, row_count=row_count, rel_count=rel_count
        ),
        out_shape=[jax.ShapeDtypeStruct((room,), jnp.int32), jax.ShapeDtypeStruct((4,), jnp.int32)],
        in_specs=[VMEM],
        out_specs=[SMEM] * 2,
        scratch_shapes=[flat] * 5
        + [pltpu.VMEM((8, LANES), jnp.int32), flat_smem, flat_smem]
        + [pltpu.SMEM((8, LANES), jnp.int32), pltpu.SemaphoreType.DMA((3,))],
        name="bucket",
    )(edge_tiles.transpose(1, 0, 2))
    source = (words & (2 * row_count - 1)) * groups
    target = ((words >> (row_bits + 1)) & (row_count - 1)) * groups
    return room, ends, source, target, words >> (2 * row_bits + 1)


def body(
    entity_state,
    edge_tiles,
    query_head,
    query_relation,
    query_table,
    rel_vectors,
    mix_weight,
    mix_bias,
    cotangent,
):
    row_count, col_count = entity_state.shape
    groups = col_count // LANES
    long = row_count * groups
    query_count = query_head.shape[0]
    rel_count = rel_vectors.shape[1]
    seats = Seats(lax.axis_size("node"), lax.axis_size("query"))

    def send(block, route):
        return lax.ppermute(block, AXES, route)

    def run(fn, args, specs, outs, out_specs, scratch):
        return pl.pallas_call(
            fn, out_shape=outs, in_specs=specs, out_specs=out_specs, scratch_shapes=scratch,
        )(*args)

    wide_f32 = jax.ShapeDtypeStruct((long, LANES), jnp.float32)
    wide_bf16 = jax.ShapeDtypeStruct((long, LANES), jnp.bfloat16)
    f32_buf = pltpu.VMEM((long, LANES), jnp.float32)
    bf16_buf = pltpu.VMEM((long, LANES), jnp.bfloat16)
    pair = pltpu.VMEM((2 * long, LANES), jnp.float32)
    sums = [f32_buf] * SUMS
    pair_sums = [pair] * SUMS
    square = jax.ShapeDtypeStruct((LANES, LANES), jnp.float32)
    line = jax.ShapeDtypeStruct((1, LANES), jnp.float32)

    state_zero = send(entity_state, seats.gather())
    room, ends, source, target, rel = edge_lists(edge_tiles, row_count, groups, rel_count)
    heads = query_head - lax.axis_index("node") * row_count
    tail = jnp.concatenate([ends, heads, query_relation])
    tail_room = -(-tail.shape[0] // LINE) * LINE
    tail = jnp.pad(tail, (0, tail_room - tail.shape[0]))
    flat = send(jnp.concatenate([source, target, rel, tail]), seats.gather())
    own_relation = flat[3 * room + 4 + query_count : 3 * room + 4 + 2 * query_count]
    grad_out = send(cotangent, seats.gather())

    choose_rel = (own_relation[:, None] == lax.iota(jnp.int32, query_table.shape[0])[None, :]).astype(
        jnp.float32
    )
    query_vec = (
        jnp.dot(choose_rel, query_table, precision=HIGHEST, preferred_element_type=jnp.float32)
        .astype(jnp.bfloat16)
        .astype(jnp.float32)
    )
    repeat = LANES // DIM
    lane_group = lax.iota(jnp.int32, LANES) // DIM
    head_rows = jnp.where(
        lane_group[None, :] == (lax.iota(jnp.int32, query_count) % repeat)[:, None],
        jnp.tile(query_vec, (1, repeat)),
        0.0,
    )
    tables = jnp.tile(jnp.pad(rel_vectors, ((0, 0), (0, -rel_count % 8 or 8), (0, 0))), (1, 1, repeat))
    same = lane_group[:, None] == lane_group[None, :]
    weights = jnp.where(same[None], jnp.tile(mix_weight, (1, repeat, repeat)), 0.0)
    biases = jnp.tile(mix_bias, (1, repeat))[:, None, :]
    list_bufs = [pltpu.SMEM((room,), jnp.int32)] * 3 + [pltpu.SMEM((tail_room,), jnp.int32)]
    table_buf = pltpu.VMEM(tables.shape[1:], jnp.float32)

    def sems(count):
        return pltpu.SemaphoreType.DMA((count,))

    def halo(state, index):
        buf = pltpu.VMEM(state.shape, jnp.bfloat16)
        mirror = send(state, seats.mirror())
        left = send(state, seats.shift(1))
        right = send(state, seats.shift(-1))
        near = run(
            functools.partial(near_kernel, groups, index),
            [flat, state, mirror, tables],
            [ANY] * 4,
            wide_f32,
            ANY,
            [*list_bufs, buf, buf, table_buf, pair, sems(11), *sums],
        )
        return left, right, near

    left, right, near = halo(state_zero, 0)
    block_buf = pltpu.VMEM(state_zero.shape, jnp.bfloat16)
    state_one, mixed_zero, update_zero = run(
        functools.partial(first_kernel, groups),
        [head_rows, weights, biases, flat, left, right, near, tables, state_zero],
        [VMEM] * 3 + [ANY] * 6,
        [wide_bf16, wide_f32, wide_f32],
        [ANY] * 3,
        [*list_bufs, block_buf, block_buf, table_buf, block_buf, pair, f32_buf, f32_buf, bf16_buf, sems(21)]
        + sums,
    )
    left, right, near = halo(state_one, 1)
    state_two, grad_mixed, mixed_one, grad_one, to_left, to_right = run(
        functools.partial(second_kernel, groups),
        [head_rows, weights, biases, flat, left, right, near, tables, state_one, grad_out],
        [VMEM] * 3 + [ANY] * 7,
        [jax.ShapeDtypeStruct(entity_state.shape, jnp.bfloat16), wide_bf16, wide_f32, wide_f32]
        + [wide_bf16] * 2,
        [ANY] * 6,
        [*list_bufs, bf16_buf, bf16_buf, table_buf, bf16_buf, block_buf, pair, f32_buf, f32_buf, bf16_buf]
        + [block_buf, bf16_buf, bf16_buf, sems(16), *pair_sums],
    )
    from_right = send(to_left, seats.shift(-1))
    from_left = send(to_right, seats.shift(1))
    final_state = run(
        copy_kernel, [send(state_two, seats.give_back())], [ANY],
        jax.ShapeDtypeStruct(entity_state.shape, jnp.bfloat16), VMEM, [sems(1)],
    )
    base, to_mirror, weight_one, bias_one = run(
        functools.partial(adjoint_kernel, groups),
        [flat, grad_mixed, tables, grad_out, mixed_one, grad_one],
        [ANY] * 6,
        [wide_f32, wide_bf16, square, line],
        [ANY] * 2 + [VMEM] * 2,
        [*list_bufs, bf16_buf, table_buf, block_buf, f32_buf, f32_buf, bf16_buf, f32_buf]
        + [pltpu.VMEM((2 * LANES, 2 * LANES), jnp.float32), sems(11), *pair_sums],
    )
    from_mirror = send(to_mirror, seats.mirror())
    steps = 4
    rows = pl.BlockSpec((long // steps, LANES), lambda i: (i, 0))
    whole = lambda shape: pl.BlockSpec(shape, lambda i: (0, 0))
    grads = pl.pallas_call(
        last_kernel,
        out_shape=jax.ShapeDtypeStruct((2 * DIM + 8, LANES), jnp.float32),
        grid=(steps,),
        in_specs=[rows] * 6 + [whole((LANES, LANES)), whole((1, LANES))],
        out_specs=whole((2 * DIM + 8, LANES)),
        scratch_shapes=[
            pltpu.VMEM((2 * LANES, 2 * LANES), jnp.float32),
            pltpu.VMEM((1, LANES), jnp.float32),
        ],
        name="last",
    )(base, from_left, from_right, from_mirror, update_zero, mixed_zero, weight_one, bias_one)
    devices = seats.nodes * seats.queries
    reach = 1
    while reach < devices:
        grads = grads + send(grads, [(i, i ^ reach) for i in range(devices)])
        reach *= 2
    weight_grads = grads[: 2 * DIM, :DIM].reshape(2, DIM, DIM)
    bias_grads = grads[2 * DIM : 2 * DIM + 2, :DIM]
    return (final_state, weight_grads, bias_grads)


def solution(mesh):
    placed = (
        P("node", "query"),
        P("node", None, None),
        P("query"),
        P("query"),
        P(),
        P(),
        P(),
        P(),
        P("node", "query"),
    )

    return jax.shard_map(
        body, mesh=mesh, in_specs=placed, out_specs=(P("node", "query"), P(), P()), check_vma=False
    )
```

```python
import functools

import jax
import jax.numpy as jnp
from jax import lax
from jax.experimental import pallas as pl
from jax.experimental.pallas import tpu as pltpu
from jax.sharding import PartitionSpec as P


DIM = 32
LANES = 128
UNROLL = 48
SUMS = 3
CHUNK = 256
DENSE = 512
LINE = 1024
AXES = ("node", "query")
HIGHEST = lax.Precision.HIGHEST
SMEM = pl.BlockSpec(memory_space=pltpu.SMEM)
VMEM = pl.BlockSpec(memory_space=pltpu.VMEM)
ANY = pl.BlockSpec(memory_space=pl.ANY)


def silu_slope(values):
    sigma = jax.nn.sigmoid(values)
    return sigma * (1.0 + values * (1.0 - sigma))


class Seats:
    def __init__(self, nodes, queries):
        self.nodes, self.queries = nodes, queries

    def home(self, part, column):
        return part * self.queries + column

    def seat(self, part, column):
        half = self.nodes // 2
        low = part % half
        node = (column & 1) * half + (low ^ (low >> 1))
        return node * self.queries + (column >> 1) * 2 + part // half

    def blocks(self):
        return [(p, c) for p in range(self.nodes) for c in range(self.queries)]

    def gather(self):
        return [(self.home(p, c), self.seat(p, c)) for p, c in self.blocks()]

    def give_back(self):
        return [(target, source) for source, target in self.gather()]

    def shift(self, step):
        return [
            (self.seat((p - step) % self.nodes, c), self.seat(p, c)) for p, c in self.blocks()
        ]

    def mirror(self):
        return [
            (self.seat(p, c), self.seat((p + self.nodes // 2) % self.nodes, c))
            for p, c in self.blocks()
        ]

    def parts(self):
        table = [0] * (self.nodes * self.queries)
        for p, c in self.blocks():
            table[self.seat(p, c)] = p
        return table


def spread(block_ref, window_ref, first):
    if block_ref.shape[1] == LANES:
        rows = block_ref.shape[0]

        def step(i, carry):
            at = pl.multiple_of(i * CHUNK, CHUNK)
            window_ref[pl.ds(first + at, CHUNK), :] = block_ref[pl.ds(at, CHUNK), :].astype(
                jnp.float32
            )
            return carry

        lax.fori_loop(0, rows // CHUNK, step, 0)
        return
    rows, cols = block_ref.shape
    groups = cols // LANES
    size = CHUNK // groups

    def step(i, carry):
        at = pl.multiple_of(i * size, size)
        for j in range(groups):
            window_ref[pl.ds(first + at * groups + j, size, stride=groups), :] = block_ref[
                pl.ds(at, size), j * LANES : (j + 1) * LANES
            ].astype(jnp.float32)
        return carry

    lax.fori_loop(0, rows // size, step, 0)


def clear(sums):
    def step(i, carry):
        at = pl.multiple_of(i * CHUNK, CHUNK)
        for ref in sums:
            ref[pl.ds(at, CHUNK), :] = jnp.zeros((CHUNK, LANES), jnp.float32)
        return carry

    lax.fori_loop(0, sums[0].shape[0] // CHUNK, step, 0)


def walk(groups, begin, end, from_ref, to_ref, rel_ref, window, table, sums):
    room = from_ref.shape[0] - UNROLL
    views = [[ref.at[pl.ds(u, room)] for ref in (from_ref, to_ref, rel_ref)] for u in range(UNROLL)]

    def step(i, carry):
        first = begin + i * UNROLL
        for u, (from_view, to_view, rel_view) in enumerate(views):
            source = pl.multiple_of(from_view[first], groups)
            target = pl.multiple_of(to_view[first], groups)
            scale = table[pl.ds(rel_view[first], groups, stride=0), :]
            sums[u % SUMS][pl.ds(target, groups), :] += (
                window[pl.ds(source, groups), :] * scale
            )
        return carry

    lax.fori_loop(0, (end - begin) // UNROLL, step, 0)


def total_of(sums, at, size=CHUNK):
    value = sums[0][pl.ds(at, size), :]
    for ref in sums[1:]:
        value = value + ref[pl.ds(at, size), :]
    return value


def fetch(pairs, sems):
    copies = [pltpu.make_async_copy(src, dst, sems.at[i]) for i, (src, dst) in enumerate(pairs)]
    for copy in copies:
        copy.start()
    return copies


def wait(copies):
    for copy in copies:
        copy.wait()


def bucket_kernel(
    edges_ref, out_ref, ends_ref, slots, rows, rels, pos, word, meta, pos_buf, word_buf, meta_buf,
    sems, *, tile_count, row_count, rel_count,
):
    lines = slots.shape[0]
    first = 64 * lax.broadcasted_iota(jnp.int32, (tile_count, LANES), 0)
    for j in range(lines // tile_count):
        piece = slice(j * tile_count, (j + 1) * tile_count)
        lanes = slice(j * LANES, (j + 1) * LANES)
        slots[piece, :] = edges_ref[0, :, lanes]
        rows[piece, :] = edges_ref[1, :, lanes] + first
        rels[piece, :] = edges_ref[2, :, lanes]
    slot = slots[...]
    quarter = sum(((slot >= k * row_count).astype(jnp.int32) for k in range(1, 4)))
    local = slot - quarter * row_count
    kind = jnp.where(
        quarter == 1, 0, jnp.where(quarter == 3, 1, jnp.where(quarter == 0, 2, 3))
    )
    second = jnp.where((kind == 1) | (kind == 3), row_count, 0)
    row_bits = (row_count - 1).bit_length()
    word[...] = (rels[...] << (2 * row_bits + 1)) | (rows[...] << (row_bits + 1)) | (second + local)
    shape = (LANES, LANES)
    upto = (lax.broadcasted_iota(jnp.int32, shape, 0) <= lax.broadcasted_iota(jnp.int32, shape, 1))
    upto = upto.astype(jnp.float32).astype(jnp.bfloat16)
    shape = (lines, lines)
    above = (lax.broadcasted_iota(jnp.int32, shape, 0) > lax.broadcasted_iota(jnp.int32, shape, 1))
    above = above.astype(jnp.float32).astype(jnp.bfloat16)
    ones = jnp.ones((LANES, LANES), jnp.bfloat16)
    place = jnp.zeros((lines, LANES), jnp.float32)
    begin = jnp.zeros((1, LANES), jnp.float32)
    for k in range(4):
        chosen = (kind == k).astype(jnp.float32)
        onehot = chosen.astype(jnp.bfloat16)
        within = jnp.dot(onehot, upto, preferred_element_type=jnp.float32)
        per_line = jnp.dot(onehot, ones, preferred_element_type=jnp.float32)
        before = jnp.dot(above, per_line.astype(jnp.bfloat16), preferred_element_type=jnp.float32)
        count = jnp.sum(per_line, axis=0, keepdims=True)
        place = place + chosen * (begin + before + within - 1.0)
        meta[k : k + 1, :] = (begin + count).astype(jnp.int32)
        begin = begin + jnp.floor((count + (UNROLL - 0.5)) / UNROLL) * UNROLL
        meta[k + 4 : k + 5, :] = begin.astype(jnp.int32)
    pos[...] = place.astype(jnp.int32)
    wait(fetch([(pos, pos_buf), (word, word_buf), (meta, meta_buf)], sems))

    def step(i, carry):
        for u in range(LANES):
            out_ref[pos_buf[i, u]] = word_buf[i, u]
        return carry

    lax.fori_loop(0, lines, step, 0)
    dummy = rel_count << (2 * row_bits + 1)

    def fill(i, carry):
        out_ref[i] = dummy
        return carry

    for k in range(4):
        lax.fori_loop(meta_buf[k, 0], meta_buf[k + 4, 0], fill, 0)
        ends_ref[k] = meta_buf[k + 4, 0]


def split(values):
    high = values.astype(jnp.bfloat16)
    low = (values - high.astype(jnp.float32)).astype(jnp.bfloat16)
    return jnp.concatenate([high, low], axis=1)


def split_weight(weight):
    wide = split(weight)
    return jnp.concatenate([wide, wide], axis=0)


def times(values, wide):
    both = jnp.dot(split(values), wide, preferred_element_type=jnp.float32)
    return both[:, :LANES] + both[:, LANES:]


def outer(left, right):
    return lax.dot_general(
        split(left), split(right), (((0,), (0,)), ((), ())), preferred_element_type=jnp.float32
    )


def quarters(wide):
    return (
        wide[:LANES, :LANES] + wide[LANES:, :LANES] + wide[:LANES, LANES:] + wide[LANES:, LANES:]
    )


def update_of(mixed, wide, bias):
    both = jnp.dot(mixed, wide, preferred_element_type=jnp.float32)
    return both[:, :LANES] + both[:, LANES:] + bias


def advance(state_buf, mixed_buf, window, first, wide, bias):
    spread(state_buf, window, first)

    def step(i, carry):
        at = pl.multiple_of(i * DENSE, DENSE)
        values = update_of(mixed_buf[pl.ds(at, DENSE), :], wide, bias)
        window[pl.ds(first + at, DENSE), :] += values * jax.nn.sigmoid(values)
        return carry

    lax.fori_loop(0, mixed_buf.shape[0] // DENSE, step, 0)


def send_total(sums, out, sems):
    parts = 4
    size = sums[0].shape[0] // parts
    stores = []
    for k in range(parts):

        def step(i, carry):
            at = pl.multiple_of(k * size + i * CHUNK, CHUNK)
            sums[0][pl.ds(at, CHUNK), :] = total_of(sums, at)
            return carry

        lax.fori_loop(0, size // CHUNK, step, 0)
        piece = pl.ds(k * size, size)
        stores += fetch([(sums[0].at[piece, :], out.at[piece, :])], sems.at[pl.ds(k, 1)])
    wait(stores)


def near_zero_kernel(
    groups, flat, own, mirror, tables, out,
    source, target, rel, tail, own_buf, mirror_buf, table_buf, window, sems, *sums,
):
    long = sums[0].shape[0]
    lists = fetch_lists(flat, (source, target, rel, tail), tables, 0, table_buf, sems)
    states = fetch([(own, own_buf), (mirror, mirror_buf)], sems.at[pl.ds(5, 2)])
    clear(sums)
    states[0].wait()
    spread(own_buf, window, 0)
    states[1].wait()
    spread(mirror_buf, window, long)
    wait(lists)
    walk(groups, 0, tail[1], source, target, rel, window, table_buf, sums)
    send_total(sums, out, sems.at[pl.ds(7, 4)])


def near_one_kernel(
    groups, weights, biases, flat, own, mirror, mirror_mixed, tables, out,
    source, target, rel, tail, own_buf, mirror_buf, mixed_buf, table_buf, window, sems, *sums,
):
    long = sums[0].shape[0]
    lists = fetch_lists(flat, (source, target, rel, tail), tables, 1, table_buf, sems)
    states = fetch(
        [(own, own_buf), (mirror, mirror_buf), (mirror_mixed, mixed_buf)], sems.at[pl.ds(5, 3)]
    )
    clear(sums)
    wait(states)
    spread(own_buf, window, 0)
    advance(mirror_buf, mixed_buf, window, long, split(weights[0]), biases[0])
    wait(lists)
    walk(groups, 0, tail[1], source, target, rel, window, table_buf, sums)
    send_total(sums, out, sems.at[pl.ds(8, 4)])


def add_boundary(groups, heads, head_rows, ref, long):
    for q in range(head_rows.shape[0]):
        row = heads[4 + q]

        @pl.when((row >= 0) & (row < long // groups))
        def _():
            at = row * groups + q * DIM // LANES
            ref[pl.ds(at, 1), :] += head_rows[q : q + 1, :]


def fetch_lists(flat, bufs, tables, index, table_buf, sems):
    room = bufs[0].shape[0]
    pairs = [(flat.at[pl.ds(k * room, buf.shape[0])], buf) for k, buf in enumerate(bufs)]
    return fetch(pairs + [(tables.at[index], table_buf)], sems)


def first_kernel(
    groups, head_rows, weights, biases, flat, left, right, near, tables, own, state, mixed,
    source, target, rel, tail, left_buf, right_buf, table_buf, own_buf, window, mixed_buf, state_buf,
    sems, *sums,
):
    long = sums[0].shape[0]
    lists = fetch_lists(flat, (source, target, rel, tail), tables, 0, table_buf, sems)
    states = fetch([(left, left_buf), (right, right_buf), (near, sums[0])], sems.at[pl.ds(5, 3)])
    clear(sums[1:])
    states[0].wait()
    spread(left_buf, window, 0)
    states[1].wait()
    spread(right_buf, window, long)
    states[2].wait()
    wait(lists)
    extra = fetch([(own, own_buf)], sems.at[pl.ds(8, 1)])
    add_boundary(groups, tail, head_rows, sums[0], long)
    walk(groups, tail[1], tail[3], source, target, rel, window, table_buf, sums)
    wait(extra)
    spread(own_buf, window, 0)
    wide = split_weight(weights[0])
    bias = biases[0]
    parts = 4
    size = long // parts
    stores = []
    for k in range(parts):

        def step(i, carry):
            at = pl.multiple_of(k * size + i * DENSE, DENSE)
            rows = pl.ds(at, DENSE)
            mix = total_of(sums, at, DENSE)
            values = times(mix, wide) + bias
            mixed_buf[rows, :] = mix.astype(jnp.bfloat16)
            state_buf[rows, :] = (window[rows, :] + values * jax.nn.sigmoid(values)).astype(
                jnp.bfloat16
            )
            return carry

        lax.fori_loop(0, size // DENSE, step, 0)
        rows = pl.ds(k * size, size)
        stores += fetch(
            [(state_buf.at[rows, :], state.at[rows, :]), (mixed_buf.at[rows, :], mixed.at[rows, :])],
            sems.at[pl.ds(9 + 2 * k, 2)],
        )
    wait(stores)


def second_kernel(
    groups, head_rows, weights, biases, flat, left, right, left_mixed, right_mixed, near, tables, own,
    cotangent, state, grad_mixed, weight_sum, bias_sum,
    source, target, rel, tail, left_buf, right_buf, left_mixed_buf, right_mixed_buf, table_buf, own_buf,
    cotangent_buf, window, grad_mixed_buf, state_buf, wide_sum, sems, *sums,
):
    long = sums[0].shape[0]
    states = fetch(
        [(left, left_buf), (left_mixed, left_mixed_buf), (right, right_buf)]
        + [(right_mixed, right_mixed_buf), (near, sums[0])],
        sems.at[pl.ds(5, 5)],
    )
    lists = fetch_lists(flat, (source, target, rel, tail), tables, 1, table_buf, sems)
    clear(sums[1:])
    first = split(weights[0])
    wait(states[:2])
    advance(left_buf, left_mixed_buf, window, 0, first, biases[0])
    wait(states[2:])
    advance(right_buf, right_mixed_buf, window, long, first, biases[0])
    wait(lists)
    extra = fetch([(own, own_buf), (cotangent, cotangent_buf)], sems.at[pl.ds(10, 2)])
    add_boundary(groups, tail, head_rows, sums[0], long)
    walk(groups, tail[1], tail[3], source, target, rel, window, table_buf, sums)
    wait(extra)
    spread(own_buf, window, 0)
    spread(cotangent_buf, window, long)
    wide = split_weight(weights[1])
    wide_back = split_weight(weights[1].T)
    bias = biases[1]
    wide_sum[...] = jnp.zeros_like(wide_sum)
    bias_sum[...] = jnp.zeros_like(bias_sum)

    def step(i, carry):
        at = pl.multiple_of(i * DENSE, DENSE)
        rows = pl.ds(at, DENSE)
        mix = total_of(sums, at, DENSE)
        values = times(mix, wide) + bias
        sigma = jax.nn.sigmoid(values)
        window[rows, :] += values * sigma
        grad = window[pl.ds(long + at, DENSE), :] * (sigma * (1.0 + values * (1.0 - sigma)))
        grad_mixed_buf[rows, :] = times(grad, wide_back).astype(jnp.bfloat16)
        wide_sum[...] += outer(mix, grad)
        bias_sum[...] += jnp.sum(grad, axis=0, keepdims=True)
        return carry

    lax.fori_loop(0, long // DENSE, step, 0)
    stores = fetch([(grad_mixed_buf, grad_mixed)], sems.at[pl.ds(12, 1)])
    size = CHUNK // groups

    def store(i, carry):
        at = pl.multiple_of(i * size, size)
        for j in range(groups):
            state_buf[pl.ds(at, size), j * LANES : (j + 1) * LANES] = window[
                pl.ds(at * groups + j, size, stride=groups), :
            ].astype(jnp.bfloat16)
        return carry

    lax.fori_loop(0, long // CHUNK, store, 0)
    stores += fetch([(state_buf, state)], sems.at[pl.ds(13, 1)])
    weight_sum[...] = quarters(wide_sum[...])
    wait(stores)


def folded(wide):
    value = wide[:DIM, :DIM]
    for g in range(1, LANES // DIM):
        value = value + wide[g * DIM : (g + 1) * DIM, g * DIM : (g + 1) * DIM]
    return value


def folded_row(wide):
    value = wide[:, :DIM]
    for g in range(1, LANES // DIM):
        value = value + wide[:, g * DIM : (g + 1) * DIM]
    return value


def adjoint_kernel(
    groups, weights, biases, weight_one, bias_one, flat, grad_mixed, tables, cotangent, own, mirror, left,
    right, out,
    source, target, rel, tail, grad_mixed_buf, table_buf, cotangent_buf, own_buf, mirror_buf, left_buf,
    right_buf, window, wide_sum, bias_sum, sems, *sums,
):
    long = window.shape[0]
    lists = fetch_lists(flat, (source, target, rel, tail), tables, 1, table_buf, sems)
    loads = fetch([(grad_mixed, grad_mixed_buf)], sems.at[pl.ds(5, 1)])
    clear(sums)
    wide_sum[...] = jnp.zeros_like(wide_sum)
    bias_sum[...] = jnp.zeros_like(bias_sum)
    wide = split(weights[0])
    bias = biases[0]
    wait(loads)
    spread(grad_mixed_buf, window, 0)
    wait(lists)
    late = fetch(
        [(left, left_buf), (right, right_buf), (mirror, mirror_buf), (own, own_buf)]
        + [(cotangent, cotangent_buf)],
        sems.at[pl.ds(6, 5)],
    )

    def add_products(mixed_buf, first, extra, again):
        def step(i, carry):
            at = pl.multiple_of(i * DENSE, DENSE)
            terms = total_of(sums, first + at, DENSE)
            if extra is not None:
                terms = terms + extra[pl.ds(at, DENSE), :]
            if again:
                for ref in sums:
                    ref[pl.ds(first + at, DENSE), :] = jnp.zeros((DENSE, LANES), jnp.float32)
            mixed = mixed_buf[pl.ds(at, DENSE), :]
            grad = terms * silu_slope(update_of(mixed, wide, bias))
            wide_sum[...] += lax.dot_general(
                mixed, split(grad), (((0,), (0,)), ((), ())), preferred_element_type=jnp.float32
            )
            bias_sum[...] += jnp.sum(grad, axis=0, keepdims=True)
            return carry

        lax.fori_loop(0, long // DENSE, step, 0)

    walk(groups, tail[1], tail[3], target, source, rel, window, table_buf, sums)
    wait(late)
    add_products(left_buf, 0, None, True)
    add_products(right_buf, long, None, True)
    walk(groups, 0, tail[1], target, source, rel, window, table_buf, sums)
    add_products(mirror_buf, long, None, False)
    spread(cotangent_buf, window, 0)
    add_products(own_buf, 0, window, False)
    out[...] = jnp.zeros_like(out)
    out[0:DIM, 0:DIM] = folded(wide_sum[:, :LANES] + wide_sum[:, LANES:])
    out[DIM : 2 * DIM, 0:DIM] = folded(weight_one[...])
    out[2 * DIM : 2 * DIM + 1, 0:DIM] = folded_row(bias_sum[...])
    out[2 * DIM + 1 : 2 * DIM + 2, 0:DIM] = folded_row(bias_one[...])


def copy_kernel(source, out, sems):
    wait(fetch([(source, out)], sems))


def edge_lists(edge_tiles, row_count, groups, rel_count):
    tile_count, _, slot_total = edge_tiles.shape
    lines = tile_count * slot_total // LANES
    row_bits = (row_count - 1).bit_length()
    room = (tile_count * slot_total + 5 * UNROLL + LINE - 1) // LINE * LINE
    flat = pltpu.VMEM((lines, LANES), jnp.int32)
    flat_smem = pltpu.SMEM((lines, LANES), jnp.int32)
    words, ends = pl.pallas_call(
        functools.partial(
            bucket_kernel, tile_count=tile_count, row_count=row_count, rel_count=rel_count
        ),
        out_shape=[
            jax.ShapeDtypeStruct((room,), jnp.int32), jax.ShapeDtypeStruct((4,), jnp.int32)
        ],
        in_specs=[VMEM],
        out_specs=[SMEM] * 2,
        scratch_shapes=[flat] * 5
        + [pltpu.VMEM((8, LANES), jnp.int32), flat_smem, flat_smem]
        + [pltpu.SMEM((8, LANES), jnp.int32), pltpu.SemaphoreType.DMA((3,))],
        name="bucket",
    )(edge_tiles.transpose(1, 0, 2))
    source = (words & (2 * row_count - 1)) * groups
    target = ((words >> (row_bits + 1)) & (row_count - 1)) * groups
    return room, ends, source, target, words >> (2 * row_bits + 1)


def body(
    entity_state,
    edge_tiles,
    query_head,
    query_relation,
    query_table,
    rel_vectors,
    mix_weight,
    mix_bias,
    cotangent,
):
    row_count, col_count = entity_state.shape
    groups = col_count // LANES
    long = row_count * groups
    query_count = query_head.shape[0]
    rel_count = rel_vectors.shape[1]
    seats = Seats(lax.axis_size("node"), lax.axis_size("query"))

    def send(block, route):
        return lax.ppermute(block, AXES, route)

    def run(fn, args, specs, outs, out_specs, scratch):
        return pl.pallas_call(fn, out_shape=outs, in_specs=specs, out_specs=out_specs, scratch_shapes=scratch)(*args)

    wide_f32 = jax.ShapeDtypeStruct((long, LANES), jnp.float32)
    wide_bf16 = jax.ShapeDtypeStruct((long, LANES), jnp.bfloat16)
    f32_buf = pltpu.VMEM((long, LANES), jnp.float32)
    bf16_buf = pltpu.VMEM((long, LANES), jnp.bfloat16)
    pair = pltpu.VMEM((2 * long, LANES), jnp.float32)
    sums = [f32_buf] * SUMS
    pair_sums = [pair] * SUMS
    square = jax.ShapeDtypeStruct((LANES, LANES), jnp.float32)
    line = jax.ShapeDtypeStruct((1, LANES), jnp.float32)

    state_zero = send(entity_state, seats.gather())
    room, ends, source, target, rel = edge_lists(edge_tiles, row_count, groups, rel_count)
    heads = query_head - lax.axis_index("node") * row_count
    tail = jnp.concatenate([ends, heads, query_relation])
    tail_room = -(-tail.shape[0] // LINE) * LINE
    tail = jnp.pad(tail, (0, tail_room - tail.shape[0]))
    flat = send(jnp.concatenate([source, target, rel, tail]), seats.gather())
    own_relation = flat[3 * room + 4 + query_count : 3 * room + 4 + 2 * query_count]
    grad_out = send(cotangent, seats.gather())

    choose_rel = (own_relation[:, None] == lax.iota(jnp.int32, query_table.shape[0])[None, :]).astype(
        jnp.float32
    )
    query_vec = (
        jnp.dot(choose_rel, query_table, precision=HIGHEST, preferred_element_type=jnp.float32)
        .astype(jnp.bfloat16)
        .astype(jnp.float32)
    )
    repeat = LANES // DIM
    lane_group = lax.iota(jnp.int32, LANES) // DIM
    head_rows = jnp.where(
        lane_group[None, :] == (lax.iota(jnp.int32, query_count) % repeat)[:, None],
        jnp.tile(query_vec, (1, repeat)),
        0.0,
    )
    tables = jnp.tile(jnp.pad(rel_vectors, ((0, 0), (0, -rel_count % 8 or 8), (0, 0))), (1, 1, repeat))
    same = lane_group[:, None] == lane_group[None, :]
    weights = jnp.where(same[None], jnp.tile(mix_weight, (1, repeat, repeat)), 0.0)
    biases = jnp.tile(mix_bias, (1, repeat))[:, None, :]
    list_bufs = [pltpu.SMEM((room,), jnp.int32)] * 3 + [pltpu.SMEM((tail_room,), jnp.int32)]
    table_buf = pltpu.VMEM(tables.shape[1:], jnp.float32)

    def sems(count):
        return pltpu.SemaphoreType.DMA((count,))

    def halo(block):
        mirror = send(block, seats.mirror())
        left = send(block, seats.shift(1))
        right = send(block, seats.shift(-1))
        return mirror, left, right

    block_buf = pltpu.VMEM(state_zero.shape, jnp.bfloat16)
    mirror, left, right = halo(state_zero)
    near = run(
        functools.partial(near_zero_kernel, groups),
        [flat, state_zero, mirror, tables],
        [ANY] * 4,
        wide_f32,
        ANY,
        [*list_bufs, block_buf, block_buf, table_buf, pair, sems(11), *sums],
    )
    state_one, mixed = run(
        functools.partial(first_kernel, groups),
        [head_rows, weights, biases, flat, left, right, near, tables, state_zero],
        [VMEM] * 3 + [ANY] * 6,
        [wide_bf16, wide_bf16],
        [ANY] * 2,
        [*list_bufs, block_buf, block_buf, table_buf, block_buf, pair, bf16_buf, bf16_buf, sems(17), *sums],
    )
    mirror_mixed, left_mixed, right_mixed = halo(mixed)
    near = run(
        functools.partial(near_one_kernel, groups),
        [weights, biases, flat, state_one, mirror, mirror_mixed, tables],
        [VMEM] * 2 + [ANY] * 5,
        wide_f32,
        ANY,
        [*list_bufs, bf16_buf, block_buf, bf16_buf, table_buf, pair, sems(12), *sums],
    )
    state_two, grad_mixed, weight_one, bias_one = run(
        functools.partial(second_kernel, groups),
        [head_rows, weights, biases, flat, left, right, left_mixed, right_mixed, near, tables, state_one]
        + [grad_out],
        [VMEM] * 3 + [ANY] * 9,
        [jax.ShapeDtypeStruct(entity_state.shape, jnp.bfloat16), wide_bf16, square, line],
        [ANY] * 2 + [VMEM] * 2,
        [*list_bufs, block_buf, block_buf, bf16_buf, bf16_buf, table_buf, bf16_buf, block_buf, pair]
        + [bf16_buf, block_buf, pltpu.VMEM((2 * LANES, 2 * LANES), jnp.float32), sems(14), *sums],
    )
    final_state = run(
        copy_kernel, [send(state_two, seats.give_back())], [ANY],
        jax.ShapeDtypeStruct(entity_state.shape, jnp.bfloat16), VMEM, [sems(1)],
    )
    grads = run(
        functools.partial(adjoint_kernel, groups),
        [weights, biases, weight_one, bias_one, flat, grad_mixed, tables, grad_out, mixed, mirror_mixed]
        + [left_mixed, right_mixed],
        [VMEM] * 4 + [ANY] * 8,
        jax.ShapeDtypeStruct((2 * DIM + 8, LANES), jnp.float32),
        VMEM,
        [*list_bufs, bf16_buf, table_buf, block_buf, bf16_buf, bf16_buf, bf16_buf, bf16_buf, f32_buf]
        + [pltpu.VMEM((LANES, 2 * LANES), jnp.float32), pltpu.VMEM((1, LANES), jnp.float32), sems(11)]
        + pair_sums,
    )
    devices = seats.nodes * seats.queries
    reach = 1
    while reach < devices:
        grads = grads + send(grads, [(i, i ^ reach) for i in range(devices)])
        reach *= 2
    weight_grads = grads[: 2 * DIM, :DIM].reshape(2, DIM, DIM)
    bias_grads = grads[2 * DIM : 2 * DIM + 2, :DIM]
    return (final_state, weight_grads, bias_grads)


def solution(mesh):
    placed = (
        P("node", "query"),
        P("node", None, None),
        P("query"),
        P("query"),
        P(),
        P(),
        P(),
        P(),
        P("node", "query"),
    )

    return jax.shard_map(body, mesh=mesh, in_specs=placed, out_specs=(P("node", "query"), P(), P()), check_vma=False)
```

```python
import functools

import jax
import jax.numpy as jnp
from jax import lax
from jax.experimental import pallas as pl
from jax.experimental.pallas import tpu as pltpu
from jax.sharding import PartitionSpec as P


DIM = 32
LANES = 128
UNROLL = 48
SUMS = 3
CHUNK = 256
DENSE = 1024
LINE = 1024
AXES = ("node", "query")
HIGHEST = lax.Precision.HIGHEST
SMEM = pl.BlockSpec(memory_space=pltpu.SMEM)
VMEM = pl.BlockSpec(memory_space=pltpu.VMEM)
ANY = pl.BlockSpec(memory_space=pl.ANY)


class Seats:
    def __init__(self, nodes, queries):
        self.nodes, self.queries = nodes, queries

    def home(self, part, column):
        return part * self.queries + column

    def seat(self, part, column):
        half = self.nodes // 2
        low = part % half
        node = (column & 1) * half + (low ^ (low >> 1))
        return node * self.queries + (column >> 1) * 2 + part // half

    def blocks(self):
        return [(p, c) for p in range(self.nodes) for c in range(self.queries)]

    def gather(self):
        return [(self.home(p, c), self.seat(p, c)) for p, c in self.blocks()]

    def give_back(self):
        return [(target, source) for source, target in self.gather()]

    def shift(self, step):
        return [
            (self.seat((p - step) % self.nodes, c), self.seat(p, c)) for p, c in self.blocks()
        ]

    def mirror(self):
        return [
            (self.seat(p, c), self.seat((p + self.nodes // 2) % self.nodes, c))
            for p, c in self.blocks()
        ]

    def parts(self):
        table = [0] * (self.nodes * self.queries)
        for p, c in self.blocks():
            table[self.seat(p, c)] = p
        return table


def spread(block_ref, window_ref, first):
    if block_ref.shape[1] == LANES:
        rows = block_ref.shape[0]

        def step(i, carry):
            at = pl.multiple_of(i * CHUNK, CHUNK)
            window_ref[pl.ds(first + at, CHUNK), :] = block_ref[pl.ds(at, CHUNK), :].astype(
                jnp.float32
            )
            return carry

        lax.fori_loop(0, rows // CHUNK, step, 0)
        return
    rows, cols = block_ref.shape
    groups = cols // LANES
    size = CHUNK // groups

    def step(i, carry):
        at = pl.multiple_of(i * size, size)
        for j in range(groups):
            window_ref[pl.ds(first + at * groups + j, size, stride=groups), :] = block_ref[
                pl.ds(at, size), j * LANES : (j + 1) * LANES
            ].astype(jnp.float32)
        return carry

    lax.fori_loop(0, rows // size, step, 0)


def clear(sums):
    def step(i, carry):
        at = pl.multiple_of(i * CHUNK, CHUNK)
        for ref in sums:
            ref[pl.ds(at, CHUNK), :] = jnp.zeros((CHUNK, LANES), jnp.float32)
        return carry

    lax.fori_loop(0, sums[0].shape[0] // CHUNK, step, 0)


def walk(groups, begin, end, from_ref, to_ref, rel_ref, window, table, sums):
    room = from_ref.shape[0] - UNROLL
    views = [[ref.at[pl.ds(u, room)] for ref in (from_ref, to_ref, rel_ref)] for u in range(UNROLL)]

    def step(i, carry):
        first = begin + i * UNROLL
        for u, (from_view, to_view, rel_view) in enumerate(views):
            source = pl.multiple_of(from_view[first], groups)
            target = pl.multiple_of(to_view[first], groups)
            scale = table[pl.ds(rel_view[first], groups, stride=0), :]
            sums[u % SUMS][pl.ds(target, groups), :] += (
                window[pl.ds(source, groups), :] * scale
            )
        return carry

    lax.fori_loop(0, (end - begin) // UNROLL, step, 0)


def total_of(sums, at, size=CHUNK):
    value = sums[0][pl.ds(at, size), :]
    for ref in sums[1:]:
        value = value + ref[pl.ds(at, size), :]
    return value


def fetch(pairs, sems):
    copies = [pltpu.make_async_copy(src, dst, sems.at[i]) for i, (src, dst) in enumerate(pairs)]
    for copy in copies:
        copy.start()
    return copies


def wait(copies):
    for copy in copies:
        copy.wait()


def bucket_kernel(
    edges_ref, out_ref, ends_ref, slots, rows, rels, pos, word, meta, pos_buf, word_buf, meta_buf,
    sems, *, tile_count, row_count, rel_count,
):
    lines = slots.shape[0]
    first = 64 * lax.broadcasted_iota(jnp.int32, (tile_count, LANES), 0)
    for j in range(lines // tile_count):
        piece = slice(j * tile_count, (j + 1) * tile_count)
        lanes = slice(j * LANES, (j + 1) * LANES)
        slots[piece, :] = edges_ref[0, :, lanes]
        rows[piece, :] = edges_ref[1, :, lanes] + first
        rels[piece, :] = edges_ref[2, :, lanes]
    slot = slots[...]
    quarter = sum(((slot >= k * row_count).astype(jnp.int32) for k in range(1, 4)))
    local = slot - quarter * row_count
    kind = jnp.where(
        quarter == 1, 0, jnp.where(quarter == 3, 1, jnp.where(quarter == 0, 2, 3))
    )
    second = jnp.where((kind == 1) | (kind == 3), row_count, 0)
    row_bits = (row_count - 1).bit_length()
    word[...] = (rels[...] << (2 * row_bits + 1)) | (rows[...] << (row_bits + 1)) | (second + local)
    shape = (LANES, LANES)
    upto = (lax.broadcasted_iota(jnp.int32, shape, 0) <= lax.broadcasted_iota(jnp.int32, shape, 1))
    upto = upto.astype(jnp.float32).astype(jnp.bfloat16)
    shape = (lines, lines)
    above = (lax.broadcasted_iota(jnp.int32, shape, 0) > lax.broadcasted_iota(jnp.int32, shape, 1))
    above = above.astype(jnp.float32).astype(jnp.bfloat16)
    ones = jnp.ones((LANES, LANES), jnp.bfloat16)
    place = jnp.zeros((lines, LANES), jnp.float32)
    begin = jnp.zeros((1, LANES), jnp.float32)
    for k in range(4):
        chosen = (kind == k).astype(jnp.float32)
        onehot = chosen.astype(jnp.bfloat16)
        within = jnp.dot(onehot, upto, preferred_element_type=jnp.float32)
        per_line = jnp.dot(onehot, ones, preferred_element_type=jnp.float32)
        before = jnp.dot(above, per_line.astype(jnp.bfloat16), preferred_element_type=jnp.float32)
        count = jnp.sum(per_line, axis=0, keepdims=True)
        place = place + chosen * (begin + before + within - 1.0)
        meta[k : k + 1, :] = (begin + count).astype(jnp.int32)
        begin = begin + jnp.floor((count + (UNROLL - 0.5)) / UNROLL) * UNROLL
        meta[k + 4 : k + 5, :] = begin.astype(jnp.int32)
    pos[...] = place.astype(jnp.int32)
    wait(fetch([(pos, pos_buf), (word, word_buf), (meta, meta_buf)], sems))

    def step(i, carry):
        for u in range(LANES):
            out_ref[pos_buf[i, u]] = word_buf[i, u]
        return carry

    lax.fori_loop(0, lines, step, 0)
    dummy = rel_count << (2 * row_bits + 1)

    def fill(i, carry):
        out_ref[i] = dummy
        return carry

    for k in range(4):
        lax.fori_loop(meta_buf[k, 0], meta_buf[k + 4, 0], fill, 0)
        ends_ref[k] = meta_buf[k + 4, 0]


def split(values):
    high = values.astype(jnp.bfloat16)
    low = (values - high.astype(jnp.float32)).astype(jnp.bfloat16)
    return jnp.concatenate([high, low], axis=1)


def split_weight(weight):
    wide = split(weight)
    return jnp.concatenate([wide, wide], axis=0)


def times(values, wide):
    both = jnp.dot(split(values), wide, preferred_element_type=jnp.float32)
    return both[:, :LANES] + both[:, LANES:]


def outer(left, right):
    return lax.dot_general(
        split(left), split(right), (((0,), (0,)), ((), ())), preferred_element_type=jnp.float32
    )


def outer_rounded(left, right):
    return lax.dot_general(
        left, split(right), (((0,), (0,)), ((), ())), preferred_element_type=jnp.float32
    )


def quarters(wide):
    return (
        wide[:LANES, :LANES] + wide[LANES:, :LANES] + wide[:LANES, LANES:] + wide[LANES:, LANES:]
    )


def make_table(rels, index, table):
    count = rels.shape[2]
    for at in range(0, table.shape[0], LANES):
        size = min(LANES, count - at)
        piece = rels[index, :, at : at + size]
        if size < LANES:
            piece = jnp.concatenate([piece, jnp.zeros((DIM, LANES - size), jnp.float32)], axis=1)
        table[at : at + LANES, :] = jnp.concatenate([piece] * (LANES // DIM), axis=0).T


def block_weight(weight):
    repeat = LANES // DIM
    wide = jnp.concatenate([jnp.concatenate([weight] * repeat, axis=1)] * repeat, axis=0)
    row = lax.broadcasted_iota(jnp.int32, wide.shape, 0)
    lane = lax.broadcasted_iota(jnp.int32, wide.shape, 1)
    return jnp.where((row & -DIM) == (lane & -DIM), wide, 0.0)


def block_bias(bias):
    return jnp.concatenate([bias] * (LANES // DIM), axis=1)


def update_of(mixed, wide, bias):
    both = jnp.dot(mixed, wide, preferred_element_type=jnp.float32)
    return both[:, :LANES] + both[:, LANES:] + bias


def slope_from(values, sigma):
    return sigma * (1.0 + values * (1.0 - sigma))


def advance(state_buf, mixed_buf, window, first, wide, bias, slope_buf=None):
    spread(state_buf, window, first)

    def step(i, carry):
        at = pl.multiple_of(i * DENSE, DENSE)
        values = update_of(mixed_buf[pl.ds(at, DENSE), :], wide, bias)
        sigma = jax.nn.sigmoid(values)
        window[pl.ds(first + at, DENSE), :] += values * sigma
        if slope_buf is not None:
            slope_buf[pl.ds(at, DENSE), :] = slope_from(values, sigma)
        return carry

    lax.fori_loop(0, mixed_buf.shape[0] // DENSE, step, 0)


def send_total(sums, out, sems):
    parts = 4
    size = sums[0].shape[0] // parts
    stores = []
    for k in range(parts):

        def step(i, carry):
            at = pl.multiple_of(k * size + i * CHUNK, CHUNK)
            sums[0][pl.ds(at, CHUNK), :] = total_of(sums, at)
            return carry

        lax.fori_loop(0, size // CHUNK, step, 0)
        piece = pl.ds(k * size, size)
        stores += fetch([(sums[0].at[piece, :], out.at[piece, :])], sems.at[pl.ds(k, 1)])
    wait(stores)


def near_zero_kernel(
    groups, rels, flat, own, mirror, out,
    source, target, rel, tail, own_buf, mirror_buf, table_buf, window, sems, *sums,
):
    long = sums[0].shape[0]
    lists = fetch_lists(flat, (source, target, rel, tail), sems)
    states = fetch([(own, own_buf), (mirror, mirror_buf)], sems.at[pl.ds(5, 2)])
    make_table(rels, 0, table_buf)
    clear(sums)
    states[0].wait()
    spread(own_buf, window, 0)
    states[1].wait()
    spread(mirror_buf, window, long)
    wait(lists)
    walk(groups, 0, tail[1], source, target, rel, window, table_buf, sums)
    send_total(sums, out, sems.at[pl.ds(7, 4)])


def near_one_kernel(
    groups, rels, weights, biases, flat, own, mirror, mirror_mixed, out,
    source, target, rel, tail, own_buf, mirror_buf, mixed_buf, table_buf, window, sems, *sums,
):
    long = sums[0].shape[0]
    lists = fetch_lists(flat, (source, target, rel, tail), sems)
    states = fetch(
        [(own, own_buf), (mirror, mirror_buf), (mirror_mixed, mixed_buf)], sems.at[pl.ds(5, 3)]
    )
    make_table(rels, 1, table_buf)
    clear(sums)
    wait(states)
    spread(own_buf, window, 0)
    advance(mirror_buf, mixed_buf, window, long, split(block_weight(weights[0])), block_bias(biases[0:1, :]))
    wait(lists)
    walk(groups, 0, tail[1], source, target, rel, window, table_buf, sums)
    send_total(sums, out, sems.at[pl.ds(8, 4)])


def add_boundary(groups, heads, head_rows, ref, long):
    for q in range(head_rows.shape[0]):
        row = heads[4 + q]

        @pl.when((row >= 0) & (row < long // groups))
        def _():
            at = row * groups + q * DIM // LANES
            ref[pl.ds(at, 1), :] += head_rows[q : q + 1, :]


def fetch_lists(flat, bufs, sems):
    room = bufs[0].shape[0]
    pairs = [(flat.at[pl.ds(k * room, buf.shape[0])], buf) for k, buf in enumerate(bufs)]
    return fetch(pairs, sems)


def first_kernel(
    groups, rels, head_rows, weights, biases, flat, left, right, near, own, state, mixed,
    source, target, rel, tail, left_buf, right_buf, table_buf, own_buf, window, mixed_buf, state_buf,
    sems, *sums,
):
    long = sums[0].shape[0]
    lists = fetch_lists(flat, (source, target, rel, tail), sems)
    states = fetch([(left, left_buf), (right, right_buf), (near, sums[0])], sems.at[pl.ds(5, 3)])
    make_table(rels, 0, table_buf)
    clear(sums[1:])
    states[0].wait()
    spread(left_buf, window, 0)
    states[1].wait()
    spread(right_buf, window, long)
    states[2].wait()
    wait(lists)
    extra = fetch([(own, own_buf)], sems.at[pl.ds(8, 1)])
    add_boundary(groups, tail, head_rows, sums[0], long)
    walk(groups, tail[1], tail[3], source, target, rel, window, table_buf, sums)
    wait(extra)
    spread(own_buf, window, 0)
    wide = split_weight(block_weight(weights[0]))
    bias = block_bias(biases[0:1, :])
    parts = 4
    size = long // parts
    stores = []
    for k in range(parts):

        def step(i, carry):
            at = pl.multiple_of(k * size + i * DENSE, DENSE)
            rows = pl.ds(at, DENSE)
            mix = total_of(sums, at, DENSE)
            values = times(mix, wide) + bias
            mixed_buf[rows, :] = mix.astype(jnp.bfloat16)
            state_buf[rows, :] = (window[rows, :] + values * jax.nn.sigmoid(values)).astype(
                jnp.bfloat16
            )
            return carry

        lax.fori_loop(0, size // DENSE, step, 0)
        rows = pl.ds(k * size, size)
        stores += fetch(
            [(state_buf.at[rows, :], state.at[rows, :]), (mixed_buf.at[rows, :], mixed.at[rows, :])],
            sems.at[pl.ds(9 + 2 * k, 2)],
        )
    wait(stores)


def second_kernel(
    groups, rels, head_rows, weights, biases, flat, left, right, left_mixed, right_mixed, near, own,
    cotangent, state, grad_mixed, left_slope, right_slope, weight_sum, bias_sum,
    source, target, rel, tail, left_buf, right_buf, left_mixed_buf, right_mixed_buf, table_buf, own_buf,
    cotangent_buf, window, grad_mixed_buf, state_buf, left_slope_buf, right_slope_buf, wide_sum, sems, *sums,
):
    long = sums[0].shape[0]
    states = fetch(
        [(left, left_buf), (left_mixed, left_mixed_buf), (right, right_buf)]
        + [(right_mixed, right_mixed_buf), (near, sums[0])],
        sems.at[pl.ds(5, 5)],
    )
    lists = fetch_lists(flat, (source, target, rel, tail), sems)
    make_table(rels, 1, table_buf)
    clear(sums[1:])
    first = split(block_weight(weights[0]))
    first_bias = block_bias(biases[0:1, :])
    wait(states[:2])
    advance(left_buf, left_mixed_buf, window, 0, first, first_bias, left_slope_buf)
    wait(states[2:])
    advance(right_buf, right_mixed_buf, window, long, first, first_bias, right_slope_buf)
    stores = fetch(
        [(left_slope_buf, left_slope), (right_slope_buf, right_slope)], sems.at[pl.ds(14, 2)]
    )
    wait(lists)
    extra = fetch([(own, own_buf), (cotangent, cotangent_buf)], sems.at[pl.ds(10, 2)])
    add_boundary(groups, tail, head_rows, sums[0], long)
    walk(groups, tail[1], tail[3], source, target, rel, window, table_buf, sums)
    wait(extra)
    spread(own_buf, window, 0)
    spread(cotangent_buf, window, long)
    weight = block_weight(weights[1])
    wide = split_weight(weight)
    wide_back = split_weight(weight.T)
    bias = block_bias(biases[1:2, :])
    wide_sum[...] = jnp.zeros_like(wide_sum)
    bias_sum[...] = jnp.zeros_like(bias_sum)

    def step(i, carry):
        at = pl.multiple_of(i * DENSE, DENSE)
        rows = pl.ds(at, DENSE)
        mix = total_of(sums, at, DENSE)
        values = times(mix, wide) + bias
        sigma = jax.nn.sigmoid(values)
        window[rows, :] += values * sigma
        grad = window[pl.ds(long + at, DENSE), :] * slope_from(values, sigma)
        grad_mixed_buf[rows, :] = times(grad, wide_back).astype(jnp.bfloat16)
        wide_sum[...] += outer(mix, grad)
        bias_sum[...] += jnp.sum(grad, axis=0, keepdims=True)
        return carry

    lax.fori_loop(0, long // DENSE, step, 0)
    stores += fetch([(grad_mixed_buf, grad_mixed)], sems.at[pl.ds(12, 1)])
    size = CHUNK // groups

    def store(i, carry):
        at = pl.multiple_of(i * size, size)
        for j in range(groups):
            state_buf[pl.ds(at, size), j * LANES : (j + 1) * LANES] = window[
                pl.ds(at * groups + j, size, stride=groups), :
            ].astype(jnp.bfloat16)
        return carry

    lax.fori_loop(0, long // CHUNK, store, 0)
    stores += fetch([(state_buf, state)], sems.at[pl.ds(13, 1)])
    weight_sum[...] = quarters(wide_sum[...])
    wait(stores)


def folded(wide):
    value = wide[:DIM, :DIM]
    for g in range(1, LANES // DIM):
        value = value + wide[g * DIM : (g + 1) * DIM, g * DIM : (g + 1) * DIM]
    return value


def folded_row(wide):
    value = wide[:, :DIM]
    for g in range(1, LANES // DIM):
        value = value + wide[:, g * DIM : (g + 1) * DIM]
    return value


def prepare_kernel(
    weights, biases, cotangent, own, mirror, own_slope, mirror_slope, weight_sum, bias_sum, window, wide_sum
):
    spread(cotangent, window, 0)
    wide = split(block_weight(weights[0]))
    bias = block_bias(biases[0:1, :])
    wide_sum[...] = jnp.zeros_like(wide_sum)
    bias_sum[...] = jnp.zeros_like(bias_sum)

    def step(i, carry):
        rows = pl.ds(pl.multiple_of(i * DENSE, DENSE), DENSE)
        values = update_of(mirror[rows, :], wide, bias)
        mirror_slope[rows, :] = slope_from(values, jax.nn.sigmoid(values))
        mixed = own[rows, :]
        values = update_of(mixed, wide, bias)
        slope = slope_from(values, jax.nn.sigmoid(values))
        own_slope[rows, :] = slope
        grad = window[rows, :] * slope
        wide_sum[...] += outer_rounded(mixed, grad)
        bias_sum[...] += jnp.sum(grad, axis=0, keepdims=True)
        return carry

    lax.fori_loop(0, window.shape[0] // DENSE, step, 0)
    weight_sum[...] = wide_sum[:, :LANES] + wide_sum[:, LANES:]


def adjoint_kernel(
    groups, rels, weight_zero, bias_zero, weight_one, bias_one, flat, grad_mixed, *refs
):
    parts, refs = refs[:8], refs[8:]
    out, source, target, rel, tail, grad_mixed_buf, table_buf = refs[:7]
    bufs, refs = refs[7:15], refs[15:]
    window, wide_sum, bias_sum, sems = refs[:4]
    sums = refs[4:]
    long = window.shape[0]
    lists = fetch_lists(flat, (source, target, rel, tail), sems)
    loads = fetch([(grad_mixed, grad_mixed_buf)], sems.at[pl.ds(5, 1)])
    make_table(rels, 1, table_buf)
    clear(sums)
    wide_sum[...] = jnp.zeros_like(wide_sum)
    bias_sum[...] = bias_zero[...]
    wait(loads)
    spread(grad_mixed_buf, window, 0)
    wait(lists)
    late = fetch(list(zip(parts, bufs)), sems.at[pl.ds(6, 8)])

    def add_products(mixed_buf, slope_buf, first, again):
        def step(i, carry):
            at = pl.multiple_of(i * DENSE, DENSE)
            grad = total_of(sums, first + at, DENSE) * slope_buf[pl.ds(at, DENSE), :]
            if again:
                for ref in sums:
                    ref[pl.ds(first + at, DENSE), :] = jnp.zeros((DENSE, LANES), jnp.float32)
            wide_sum[...] += outer_rounded(mixed_buf[pl.ds(at, DENSE), :], grad)
            bias_sum[...] += jnp.sum(grad, axis=0, keepdims=True)
            return carry

        lax.fori_loop(0, long // DENSE, step, 0)

    walk(groups, tail[1], tail[3], target, source, rel, window, table_buf, sums)
    wait(late)
    add_products(bufs[0], bufs[1], 0, True)
    add_products(bufs[2], bufs[3], long, True)
    walk(groups, 0, tail[1], target, source, rel, window, table_buf, sums)
    add_products(bufs[4], bufs[5], 0, False)
    add_products(bufs[6], bufs[7], long, False)
    out[...] = jnp.zeros_like(out)
    out[0:DIM, 0:DIM] = folded(wide_sum[:, :LANES] + wide_sum[:, LANES:] + weight_zero[...])
    out[DIM : 2 * DIM, 0:DIM] = folded(weight_one[...])
    out[2 * DIM : 2 * DIM + 1, 0:DIM] = folded_row(bias_sum[...])
    out[2 * DIM + 1 : 2 * DIM + 2, 0:DIM] = folded_row(bias_one[...])


def copy_kernel(source, out, sems):
    wait(fetch([(source, out)], sems))


def edge_lists(edge_tiles, row_count, groups, rel_count):
    tile_count, _, slot_total = edge_tiles.shape
    lines = tile_count * slot_total // LANES
    row_bits = (row_count - 1).bit_length()
    room = (tile_count * slot_total + 5 * UNROLL + LINE - 1) // LINE * LINE
    flat = pltpu.VMEM((lines, LANES), jnp.int32)
    flat_smem = pltpu.SMEM((lines, LANES), jnp.int32)
    words, ends = pl.pallas_call(
        functools.partial(
            bucket_kernel, tile_count=tile_count, row_count=row_count, rel_count=rel_count
        ),
        out_shape=[
            jax.ShapeDtypeStruct((room,), jnp.int32), jax.ShapeDtypeStruct((4,), jnp.int32)
        ],
        in_specs=[VMEM],
        out_specs=[SMEM] * 2,
        scratch_shapes=[flat] * 5
        + [pltpu.VMEM((8, LANES), jnp.int32), flat_smem, flat_smem]
        + [pltpu.SMEM((8, LANES), jnp.int32), pltpu.SemaphoreType.DMA((3,))],
        name="bucket",
    )(edge_tiles.transpose(1, 0, 2))
    source = (words & (2 * row_count - 1)) * groups
    target = ((words >> (row_bits + 1)) & (row_count - 1)) * groups
    return room, ends, source, target, words >> (2 * row_bits + 1)


def body(
    entity_state,
    edge_tiles,
    query_head,
    query_relation,
    query_table,
    rel_vectors,
    mix_weight,
    mix_bias,
    cotangent,
):
    row_count, col_count = entity_state.shape
    groups = col_count // LANES
    long = row_count * groups
    query_count = query_head.shape[0]
    rel_count = rel_vectors.shape[1]
    seats = Seats(lax.axis_size("node"), lax.axis_size("query"))

    def send(block, route):
        return lax.ppermute(block, AXES, route)

    def run(fn, args, specs, outs, out_specs, scratch):
        return pl.pallas_call(fn, out_shape=outs, in_specs=specs, out_specs=out_specs, scratch_shapes=scratch)(*args)

    wide_f32 = jax.ShapeDtypeStruct((long, LANES), jnp.float32)
    wide_bf16 = jax.ShapeDtypeStruct((long, LANES), jnp.bfloat16)
    f32_buf = pltpu.VMEM((long, LANES), jnp.float32)
    bf16_buf = pltpu.VMEM((long, LANES), jnp.bfloat16)
    pair = pltpu.VMEM((2 * long, LANES), jnp.float32)
    sums = [f32_buf] * SUMS
    pair_sums = [pair] * SUMS
    square = jax.ShapeDtypeStruct((LANES, LANES), jnp.float32)
    line = jax.ShapeDtypeStruct((1, LANES), jnp.float32)

    state_zero = send(entity_state, seats.gather())
    room, ends, source, target, rel = edge_lists(edge_tiles, row_count, groups, rel_count)
    heads = query_head - lax.axis_index("node") * row_count
    tail = jnp.concatenate([ends, heads, query_relation])
    tail_room = -(-tail.shape[0] // LINE) * LINE
    tail = jnp.pad(tail, (0, tail_room - tail.shape[0]))
    flat = send(jnp.concatenate([source, target, rel, tail]), seats.gather())
    own_relation = flat[3 * room + 4 + query_count : 3 * room + 4 + 2 * query_count]
    grad_out = send(cotangent, seats.gather())

    choose_rel = (own_relation[:, None] == lax.iota(jnp.int32, query_table.shape[0])[None, :]).astype(
        jnp.float32
    )
    query_vec = (
        jnp.dot(choose_rel, query_table, precision=HIGHEST, preferred_element_type=jnp.float32)
        .astype(jnp.bfloat16)
        .astype(jnp.float32)
    )
    repeat = LANES // DIM
    lane_group = lax.iota(jnp.int32, LANES) // DIM
    head_rows = jnp.where(
        lane_group[None, :] == (lax.iota(jnp.int32, query_count) % repeat)[:, None],
        jnp.tile(query_vec, (1, repeat)),
        0.0,
    )
    rels = rel_vectors.transpose(0, 2, 1)
    list_bufs = [pltpu.SMEM((room,), jnp.int32)] * 3 + [pltpu.SMEM((tail_room,), jnp.int32)]
    table_buf = pltpu.VMEM(((rel_count // LANES + 1) * LANES, LANES), jnp.float32)

    def sems(count):
        return pltpu.SemaphoreType.DMA((count,))

    def halo(block):
        mirror = send(block, seats.mirror())
        left = send(block, seats.shift(1))
        right = send(block, seats.shift(-1))
        return mirror, left, right

    block_buf = pltpu.VMEM(state_zero.shape, jnp.bfloat16)
    mirror, left, right = halo(state_zero)
    near = run(
        functools.partial(near_zero_kernel, groups),
        [rels, flat, state_zero, mirror],
        [VMEM] + [ANY] * 3,
        wide_f32,
        ANY,
        [*list_bufs, block_buf, block_buf, table_buf, pair, sems(11), *sums],
    )
    state_one, mixed = run(
        functools.partial(first_kernel, groups),
        [rels, head_rows, mix_weight, mix_bias, flat, left, right, near, state_zero],
        [VMEM] * 4 + [ANY] * 5,
        [wide_bf16, wide_bf16],
        [ANY] * 2,
        [*list_bufs, block_buf, block_buf, table_buf, block_buf, pair, bf16_buf, bf16_buf, sems(17), *sums],
    )
    mirror_mixed, left_mixed, right_mixed = halo(mixed)
    near = run(
        functools.partial(near_one_kernel, groups),
        [rels, mix_weight, mix_bias, flat, state_one, mirror, mirror_mixed],
        [VMEM] * 3 + [ANY] * 4,
        wide_f32,
        ANY,
        [*list_bufs, bf16_buf, block_buf, bf16_buf, table_buf, pair, sems(12), *sums],
    )
    own_slope, mirror_slope, weight_zero, bias_zero = run(
        prepare_kernel,
        [mix_weight, mix_bias, grad_out, mixed, mirror_mixed],
        [VMEM] * 5,
        [wide_f32, wide_f32, square, line],
        [VMEM] * 4,
        [f32_buf, pltpu.VMEM((LANES, 2 * LANES), jnp.float32)],
    )
    state_two, grad_mixed, left_slope, right_slope, weight_one, bias_one = run(
        functools.partial(second_kernel, groups),
        [rels, head_rows, mix_weight, mix_bias, flat, left, right, left_mixed, right_mixed, near, state_one]
        + [grad_out],
        [VMEM] * 4 + [ANY] * 8,
        [jax.ShapeDtypeStruct(entity_state.shape, jnp.bfloat16), wide_bf16, wide_f32, wide_f32]
        + [square, line],
        [ANY] * 4 + [VMEM] * 2,
        [*list_bufs, block_buf, block_buf, bf16_buf, bf16_buf, table_buf, bf16_buf, block_buf, pair]
        + [bf16_buf, block_buf, f32_buf, f32_buf, pltpu.VMEM((2 * LANES, 2 * LANES), jnp.float32)]
        + [sems(16), *sums],
    )
    final_state = run(
        copy_kernel, [send(state_two, seats.give_back())], [ANY],
        jax.ShapeDtypeStruct(entity_state.shape, jnp.bfloat16), VMEM, [sems(1)],
    )
    grads = run(
        functools.partial(adjoint_kernel, groups),
        [rels, weight_zero, bias_zero, weight_one, bias_one, flat, grad_mixed, left_mixed, left_slope]
        + [right_mixed, right_slope, mixed, own_slope, mirror_mixed, mirror_slope],
        [VMEM] * 5 + [ANY] * 10,
        jax.ShapeDtypeStruct((2 * DIM + 8, LANES), jnp.float32),
        VMEM,
        [*list_bufs, bf16_buf, table_buf, *([bf16_buf, f32_buf] * 4), f32_buf]
        + [pltpu.VMEM((LANES, 2 * LANES), jnp.float32), pltpu.VMEM((1, LANES), jnp.float32), sems(14)]
        + pair_sums,
    )
    devices = seats.nodes * seats.queries
    reach = 1
    while reach < devices:
        grads = grads + send(grads, [(i, i ^ reach) for i in range(devices)])
        reach *= 2
    weight_grads = grads[: 2 * DIM, :DIM].reshape(2, DIM, DIM)
    bias_grads = grads[2 * DIM : 2 * DIM + 2, :DIM]
    return (final_state, weight_grads, bias_grads)


def solution(mesh):
    placed = (
        P("node", "query"),
        P("node", None, None),
        P("query"),
        P("query"),
        P(),
        P(),
        P(),
        P(),
        P("node", "query"),
    )

    return jax.shard_map(body, mesh=mesh, in_specs=placed, out_specs=(P("node", "query"), P(), P()), check_vma=False)
```

```python
import functools

import jax
import jax.numpy as jnp
from jax import lax
from jax.experimental import pallas as pl
from jax.experimental.pallas import tpu as pltpu
from jax.sharding import PartitionSpec as P


DIM = 32
LANES = 128
UNROLL = 48
SUMS = 3
CHUNK = 256
DENSE = 1024
LINE = 1024
AXES = ("node", "query")
HIGHEST = lax.Precision.HIGHEST
SMEM = pl.BlockSpec(memory_space=pltpu.SMEM)
VMEM = pl.BlockSpec(memory_space=pltpu.VMEM)
HBM = pl.BlockSpec(memory_space=pltpu.HBM)


class Seats:
    def __init__(self, nodes, queries):
        self.nodes, self.queries = nodes, queries

    def home(self, part, column):
        return part * self.queries + column

    def seat(self, part, column):
        half = self.nodes // 2
        low = part % half
        node = (column & 1) * half + (low ^ (low >> 1))
        return node * self.queries + (column >> 1) * 2 + part // half

    def blocks(self):
        return [(p, c) for p in range(self.nodes) for c in range(self.queries)]

    def gather(self):
        return [(self.home(p, c), self.seat(p, c)) for p, c in self.blocks()]

    def give_back(self):
        return [(target, source) for source, target in self.gather()]

    def shift(self, step):
        return [
            (self.seat((p - step) % self.nodes, c), self.seat(p, c)) for p, c in self.blocks()
        ]

    def mirror(self):
        return [
            (self.seat(p, c), self.seat((p + self.nodes // 2) % self.nodes, c))
            for p, c in self.blocks()
        ]

    def parts(self):
        table = [0] * (self.nodes * self.queries)
        for p, c in self.blocks():
            table[self.seat(p, c)] = p
        return table


def spread(block_ref, window_ref, first):
    if block_ref.shape[1] == LANES:
        rows = block_ref.shape[0]

        def step(i, carry):
            at = pl.multiple_of(i * CHUNK, CHUNK)
            window_ref[pl.ds(first + at, CHUNK), :] = block_ref[pl.ds(at, CHUNK), :].astype(
                jnp.float32
            )
            return carry

        lax.fori_loop(0, rows // CHUNK, step, 0)
        return
    rows, cols = block_ref.shape
    groups = cols // LANES
    size = CHUNK // groups

    def step(i, carry):
        at = pl.multiple_of(i * size, size)
        for j in range(groups):
            window_ref[pl.ds(first + at * groups + j, size, stride=groups), :] = block_ref[
                pl.ds(at, size), j * LANES : (j + 1) * LANES
            ].astype(jnp.float32)
        return carry

    lax.fori_loop(0, rows // size, step, 0)


def clear(sums):
    def step(i, carry):
        at = pl.multiple_of(i * CHUNK, CHUNK)
        for ref in sums:
            ref[pl.ds(at, CHUNK), :] = jnp.zeros((CHUNK, LANES), jnp.float32)
        return carry

    lax.fori_loop(0, sums[0].shape[0] // CHUNK, step, 0)


def walk(groups, begin, end, from_ref, to_ref, rel_ref, window, table, sums):
    room = from_ref.shape[0] - UNROLL
    views = [[ref.at[pl.ds(u, room)] for ref in (from_ref, to_ref, rel_ref)] for u in range(UNROLL)]

    def step(i, carry):
        first = begin + i * UNROLL
        for u, (from_view, to_view, rel_view) in enumerate(views):
            source = pl.multiple_of(from_view[first], groups)
            target = pl.multiple_of(to_view[first], groups)
            scale = table[pl.ds(rel_view[first], groups, stride=0), :]
            sums[u % SUMS][pl.ds(target, groups), :] += (
                window[pl.ds(source, groups), :] * scale
            )
        return carry

    lax.fori_loop(0, (end - begin) // UNROLL, step, 0)


def total_of(sums, at, size=CHUNK):
    value = sums[0][pl.ds(at, size), :]
    for ref in sums[1:]:
        value = value + ref[pl.ds(at, size), :]
    return value


def fetch(pairs, sems):
    copies = [pltpu.make_async_copy(src, dst, sems.at[i]) for i, (src, dst) in enumerate(pairs)]
    for copy in copies:
        copy.start()
    return copies


def wait(copies):
    for copy in copies:
        copy.wait()


def bucket_kernel(
    edges_ref, out_ref, ends_ref, slots, rows, rels, pos, word, meta, pos_buf, word_buf, meta_buf,
    sems, *, tile_count, row_count, rel_count,
):
    lines = slots.shape[0]
    first = 64 * lax.broadcasted_iota(jnp.int32, (tile_count, LANES), 0)
    for j in range(lines // tile_count):
        piece = slice(j * tile_count, (j + 1) * tile_count)
        lanes = slice(j * LANES, (j + 1) * LANES)
        slots[piece, :] = edges_ref[0, :, lanes]
        rows[piece, :] = edges_ref[1, :, lanes] + first
        rels[piece, :] = edges_ref[2, :, lanes]
    slot = slots[...]
    quarter = sum(((slot >= k * row_count).astype(jnp.int32) for k in range(1, 4)))
    local = slot - quarter * row_count
    kind = jnp.where(
        quarter == 1, 0, jnp.where(quarter == 3, 1, jnp.where(quarter == 0, 2, 3))
    )
    second = jnp.where((kind == 1) | (kind == 3), row_count, 0)
    row_bits = (row_count - 1).bit_length()
    word[...] = (rels[...] << (2 * row_bits + 1)) | (rows[...] << (row_bits + 1)) | (second + local)
    shape = (LANES, LANES)
    upto = (lax.broadcasted_iota(jnp.int32, shape, 0) <= lax.broadcasted_iota(jnp.int32, shape, 1))
    upto = upto.astype(jnp.float32).astype(jnp.bfloat16)
    shape = (lines, lines)
    above = (lax.broadcasted_iota(jnp.int32, shape, 0) > lax.broadcasted_iota(jnp.int32, shape, 1))
    above = above.astype(jnp.float32).astype(jnp.bfloat16)
    ones = jnp.ones((LANES, LANES), jnp.bfloat16)
    place = jnp.zeros((lines, LANES), jnp.float32)
    begin = jnp.zeros((1, LANES), jnp.float32)
    for k in range(4):
        chosen = (kind == k).astype(jnp.float32)
        onehot = chosen.astype(jnp.bfloat16)
        within = jnp.dot(onehot, upto, preferred_element_type=jnp.float32)
        per_line = jnp.dot(onehot, ones, preferred_element_type=jnp.float32)
        before = jnp.dot(above, per_line.astype(jnp.bfloat16), preferred_element_type=jnp.float32)
        count = jnp.sum(per_line, axis=0, keepdims=True)
        place = place + chosen * (begin + before + within - 1.0)
        meta[k : k + 1, :] = (begin + count).astype(jnp.int32)
        begin = begin + jnp.floor((count + (UNROLL - 0.5)) / UNROLL) * UNROLL
        meta[k + 4 : k + 5, :] = begin.astype(jnp.int32)
    pos[...] = place.astype(jnp.int32)
    wait(fetch([(pos, pos_buf), (word, word_buf), (meta, meta_buf)], sems))

    def step(i, carry):
        for u in range(LANES):
            out_ref[pos_buf[i, u]] = word_buf[i, u]
        return carry

    lax.fori_loop(0, lines, step, 0)
    dummy = rel_count << (2 * row_bits + 1)

    def fill(i, carry):
        out_ref[i] = dummy
        return carry

    for k in range(4):
        lax.fori_loop(meta_buf[k, 0], meta_buf[k + 4, 0], fill, 0)
        ends_ref[k] = meta_buf[k + 4, 0]


def split(values):
    high = values.astype(jnp.bfloat16)
    low = (values - high.astype(jnp.float32)).astype(jnp.bfloat16)
    return jnp.concatenate([high, low], axis=1)


def split_weight(weight):
    wide = split(weight)
    return jnp.concatenate([wide, wide], axis=0)


def times(values, wide):
    both = jnp.dot(split(values), wide, preferred_element_type=jnp.float32)
    return both[:, :LANES] + both[:, LANES:]


def outer(left, right):
    return lax.dot_general(
        split(left), split(right), (((0,), (0,)), ((), ())), preferred_element_type=jnp.float32
    )


def outer_rounded(left, right):
    return lax.dot_general(
        left, split(right), (((0,), (0,)), ((), ())), preferred_element_type=jnp.float32
    )


def quarters(wide):
    return (
        wide[:LANES, :LANES] + wide[LANES:, :LANES] + wide[:LANES, LANES:] + wide[LANES:, LANES:]
    )


def make_table(rels, index, table):
    count = rels.shape[2]
    for at in range(0, table.shape[0], LANES):
        size = min(LANES, count - at)
        piece = rels[index, :, at : at + size]
        if size < LANES:
            piece = jnp.concatenate([piece, jnp.zeros((DIM, LANES - size), jnp.float32)], axis=1)
        table[at : at + LANES, :] = jnp.concatenate([piece] * (LANES // DIM), axis=0).T


def block_weight(weight):
    repeat = LANES // DIM
    wide = jnp.concatenate([jnp.concatenate([weight] * repeat, axis=1)] * repeat, axis=0)
    row = lax.broadcasted_iota(jnp.int32, wide.shape, 0)
    lane = lax.broadcasted_iota(jnp.int32, wide.shape, 1)
    return jnp.where((row & -DIM) == (lane & -DIM), wide, 0.0)


def block_bias(bias):
    return jnp.concatenate([bias] * (LANES // DIM), axis=1)


def update_of(mixed, wide, bias):
    both = jnp.dot(mixed, wide, preferred_element_type=jnp.float32)
    return both[:, :LANES] + both[:, LANES:] + bias


def slope_from(values, sigma):
    return sigma * (1.0 + values * (1.0 - sigma))


def advance(state_buf, mixed_buf, window, first, wide, bias, slope_buf=None):
    spread(state_buf, window, first)

    def step(i, carry):
        at = pl.multiple_of(i * DENSE, DENSE)
        values = update_of(mixed_buf[pl.ds(at, DENSE), :], wide, bias)
        sigma = jax.nn.sigmoid(values)
        window[pl.ds(first + at, DENSE), :] += values * sigma
        if slope_buf is not None:
            slope_buf[pl.ds(at, DENSE), :] = slope_from(values, sigma)
        return carry

    lax.fori_loop(0, mixed_buf.shape[0] // DENSE, step, 0)


def send_total(sums, out, sems):
    parts = 4
    size = sums[0].shape[0] // parts
    stores = []
    for k in range(parts):

        def step(i, carry):
            at = pl.multiple_of(k * size + i * CHUNK, CHUNK)
            sums[0][pl.ds(at, CHUNK), :] = total_of(sums, at)
            return carry

        lax.fori_loop(0, size // CHUNK, step, 0)
        piece = pl.ds(k * size, size)
        stores += fetch([(sums[0].at[piece, :], out.at[piece, :])], sems.at[pl.ds(k, 1)])
    wait(stores)


def near_zero_kernel(
    groups, rels, flat, own, mirror, out,
    source, target, rel, tail, own_buf, mirror_buf, table_buf, window, sems, *sums,
):
    long = sums[0].shape[0]
    lists = fetch_lists(flat, (source, target, rel, tail), sems)
    states = fetch([(own, own_buf), (mirror, mirror_buf)], sems.at[pl.ds(5, 2)])
    make_table(rels, 0, table_buf)
    clear(sums)
    states[0].wait()
    spread(own_buf, window, 0)
    states[1].wait()
    spread(mirror_buf, window, long)
    wait(lists)
    walk(groups, 0, tail[1], source, target, rel, window, table_buf, sums)
    send_total(sums, out, sems.at[pl.ds(7, 4)])


def near_one_kernel(
    groups, rels, weights, biases, flat, own, mirror, mirror_mixed, out,
    source, target, rel, tail, own_buf, mirror_buf, mixed_buf, table_buf, window, sems, *sums,
):
    long = sums[0].shape[0]
    lists = fetch_lists(flat, (source, target, rel, tail), sems)
    states = fetch(
        [(own, own_buf), (mirror, mirror_buf), (mirror_mixed, mixed_buf)], sems.at[pl.ds(5, 3)]
    )
    make_table(rels, 1, table_buf)
    clear(sums)
    wait(states)
    spread(own_buf, window, 0)
    advance(mirror_buf, mixed_buf, window, long, split(block_weight(weights[0])), block_bias(biases[0:1, :]))
    wait(lists)
    walk(groups, 0, tail[1], source, target, rel, window, table_buf, sums)
    send_total(sums, out, sems.at[pl.ds(8, 4)])


def add_boundary(groups, heads, head_rows, ref, long):
    for q in range(head_rows.shape[0]):
        row = heads[4 + q]

        @pl.when((row >= 0) & (row < long // groups))
        def _():
            at = row * groups + q * DIM // LANES
            ref[pl.ds(at, 1), :] += head_rows[q : q + 1, :]


def fetch_lists(flat, bufs, sems):
    room = bufs[0].shape[0]
    pairs = [(flat.at[pl.ds(k * room, buf.shape[0])], buf) for k, buf in enumerate(bufs)]
    return fetch(pairs, sems)


def first_kernel(
    groups, rels, head_rows, weights, biases, flat, left, right, near, own, state, mixed,
    source, target, rel, tail, left_buf, right_buf, table_buf, own_buf, window, mixed_buf, state_buf,
    sems, *sums,
):
    long = sums[0].shape[0]
    lists = fetch_lists(flat, (source, target, rel, tail), sems)
    states = fetch([(left, left_buf), (right, right_buf), (near, sums[0])], sems.at[pl.ds(5, 3)])
    make_table(rels, 0, table_buf)
    clear(sums[1:])
    states[0].wait()
    spread(left_buf, window, 0)
    states[1].wait()
    spread(right_buf, window, long)
    states[2].wait()
    wait(lists)
    extra = fetch([(own, own_buf)], sems.at[pl.ds(8, 1)])
    add_boundary(groups, tail, head_rows, sums[0], long)
    walk(groups, tail[1], tail[3], source, target, rel, window, table_buf, sums)
    wait(extra)
    spread(own_buf, window, 0)
    wide = split_weight(block_weight(weights[0]))
    bias = block_bias(biases[0:1, :])
    parts = 4
    size = long // parts
    stores = []
    for k in range(parts):

        def step(i, carry):
            at = pl.multiple_of(k * size + i * DENSE, DENSE)
            rows = pl.ds(at, DENSE)
            mix = total_of(sums, at, DENSE)
            values = times(mix, wide) + bias
            mixed_buf[rows, :] = mix.astype(jnp.bfloat16)
            state_buf[rows, :] = (window[rows, :] + values * jax.nn.sigmoid(values)).astype(
                jnp.bfloat16
            )
            return carry

        lax.fori_loop(0, size // DENSE, step, 0)
        rows = pl.ds(k * size, size)
        stores += fetch(
            [(state_buf.at[rows, :], state.at[rows, :]), (mixed_buf.at[rows, :], mixed.at[rows, :])],
            sems.at[pl.ds(9 + 2 * k, 2)],
        )
    wait(stores)


def second_kernel(
    groups, rels, head_rows, weights, biases, flat, left, right, left_mixed, right_mixed, near, own,
    cotangent, state, grad_mixed, left_slope, right_slope, weight_sum, bias_sum,
    source, target, rel, tail, left_buf, right_buf, left_mixed_buf, right_mixed_buf, table_buf, own_buf,
    cotangent_buf, window, grad_mixed_buf, state_buf, left_slope_buf, right_slope_buf, wide_sum, sems, *sums,
):
    long = sums[0].shape[0]
    states = fetch(
        [(left, left_buf), (left_mixed, left_mixed_buf), (right, right_buf)]
        + [(right_mixed, right_mixed_buf), (near, sums[0])],
        sems.at[pl.ds(5, 5)],
    )
    lists = fetch_lists(flat, (source, target, rel, tail), sems)
    make_table(rels, 1, table_buf)
    clear(sums[1:])
    first = split(block_weight(weights[0]))
    first_bias = block_bias(biases[0:1, :])
    wait(states[:2])
    advance(left_buf, left_mixed_buf, window, 0, first, first_bias, left_slope_buf)
    wait(states[2:])
    advance(right_buf, right_mixed_buf, window, long, first, first_bias, right_slope_buf)
    stores = fetch(
        [(left_slope_buf, left_slope), (right_slope_buf, right_slope)], sems.at[pl.ds(14, 2)]
    )
    wait(lists)
    extra = fetch([(own, own_buf), (cotangent, cotangent_buf)], sems.at[pl.ds(10, 2)])
    add_boundary(groups, tail, head_rows, sums[0], long)
    walk(groups, tail[1], tail[3], source, target, rel, window, table_buf, sums)
    wait(extra)
    spread(own_buf, window, 0)
    spread(cotangent_buf, window, long)
    weight = block_weight(weights[1])
    wide = split_weight(weight)
    wide_back = split_weight(weight.T)
    bias = block_bias(biases[1:2, :])
    wide_sum[...] = jnp.zeros_like(wide_sum)
    bias_sum[...] = jnp.zeros_like(bias_sum)

    def step(i, carry):
        at = pl.multiple_of(i * DENSE, DENSE)
        rows = pl.ds(at, DENSE)
        mix = total_of(sums, at, DENSE)
        values = times(mix, wide) + bias
        sigma = jax.nn.sigmoid(values)
        window[rows, :] += values * sigma
        grad = window[pl.ds(long + at, DENSE), :] * slope_from(values, sigma)
        grad_mixed_buf[rows, :] = times(grad, wide_back).astype(jnp.bfloat16)
        wide_sum[...] += outer(mix, grad)
        bias_sum[...] += jnp.sum(grad, axis=0, keepdims=True)
        return carry

    lax.fori_loop(0, long // DENSE, step, 0)
    stores += fetch([(grad_mixed_buf, grad_mixed)], sems.at[pl.ds(12, 1)])
    size = CHUNK // groups

    def store(i, carry):
        at = pl.multiple_of(i * size, size)
        for j in range(groups):
            state_buf[pl.ds(at, size), j * LANES : (j + 1) * LANES] = window[
                pl.ds(at * groups + j, size, stride=groups), :
            ].astype(jnp.bfloat16)
        return carry

    lax.fori_loop(0, long // CHUNK, store, 0)
    stores += fetch([(state_buf, state)], sems.at[pl.ds(13, 1)])
    weight_sum[...] = quarters(wide_sum[...])
    wait(stores)


def folded(wide):
    value = wide[:DIM, :DIM]
    for g in range(1, LANES // DIM):
        value = value + wide[g * DIM : (g + 1) * DIM, g * DIM : (g + 1) * DIM]
    return value


def folded_row(wide):
    value = wide[:, :DIM]
    for g in range(1, LANES // DIM):
        value = value + wide[:, g * DIM : (g + 1) * DIM]
    return value


def prepare_kernel(
    weights, biases, cotangent, own, mirror, own_slope, mirror_slope, weight_sum, bias_sum, window, wide_sum
):
    spread(cotangent, window, 0)
    wide = split(block_weight(weights[0]))
    bias = block_bias(biases[0:1, :])
    wide_sum[...] = jnp.zeros_like(wide_sum)
    bias_sum[...] = jnp.zeros_like(bias_sum)

    def step(i, carry):
        rows = pl.ds(pl.multiple_of(i * DENSE, DENSE), DENSE)
        values = update_of(mirror[rows, :], wide, bias)
        mirror_slope[rows, :] = slope_from(values, jax.nn.sigmoid(values))
        mixed = own[rows, :]
        values = update_of(mixed, wide, bias)
        slope = slope_from(values, jax.nn.sigmoid(values))
        own_slope[rows, :] = slope
        grad = window[rows, :] * slope
        wide_sum[...] += outer_rounded(mixed, grad)
        bias_sum[...] += jnp.sum(grad, axis=0, keepdims=True)
        return carry

    lax.fori_loop(0, window.shape[0] // DENSE, step, 0)
    weight_sum[...] = wide_sum[:, :LANES] + wide_sum[:, LANES:]


def adjoint_kernel(
    groups, rels, weight_zero, bias_zero, weight_one, bias_one, flat, grad_mixed, *refs
):
    parts, refs = refs[:8], refs[8:]
    out, source, target, rel, tail, grad_mixed_buf, table_buf = refs[:7]
    bufs, refs = refs[7:15], refs[15:]
    window, wide_sum, bias_sum, sems = refs[:4]
    sums = refs[4:]
    long = window.shape[0]
    lists = fetch_lists(flat, (source, target, rel, tail), sems)
    loads = fetch([(grad_mixed, grad_mixed_buf)], sems.at[pl.ds(5, 1)])
    make_table(rels, 1, table_buf)
    clear(sums)
    wide_sum[...] = jnp.zeros_like(wide_sum)
    bias_sum[...] = bias_zero[...]
    wait(loads)
    spread(grad_mixed_buf, window, 0)
    wait(lists)
    late = fetch(list(zip(parts, bufs)), sems.at[pl.ds(6, 8)])

    def add_products(mixed_buf, slope_buf, first, again):
        def step(i, carry):
            at = pl.multiple_of(i * DENSE, DENSE)
            grad = total_of(sums, first + at, DENSE) * slope_buf[pl.ds(at, DENSE), :]
            if again:
                for ref in sums:
                    ref[pl.ds(first + at, DENSE), :] = jnp.zeros((DENSE, LANES), jnp.float32)
            wide_sum[...] += outer_rounded(mixed_buf[pl.ds(at, DENSE), :], grad)
            bias_sum[...] += jnp.sum(grad, axis=0, keepdims=True)
            return carry

        lax.fori_loop(0, long // DENSE, step, 0)

    walk(groups, tail[1], tail[3], target, source, rel, window, table_buf, sums)
    wait(late)
    add_products(bufs[0], bufs[1], 0, True)
    add_products(bufs[2], bufs[3], long, True)
    walk(groups, 0, tail[1], target, source, rel, window, table_buf, sums)
    add_products(bufs[4], bufs[5], 0, False)
    add_products(bufs[6], bufs[7], long, False)
    out[...] = jnp.zeros_like(out)
    out[0:DIM, 0:DIM] = folded(wide_sum[:, :LANES] + wide_sum[:, LANES:] + weight_zero[...])
    out[DIM : 2 * DIM, 0:DIM] = folded(weight_one[...])
    out[2 * DIM : 2 * DIM + 1, 0:DIM] = folded_row(bias_sum[...])
    out[2 * DIM + 1 : 2 * DIM + 2, 0:DIM] = folded_row(bias_one[...])


def copy_kernel(source, out, sems):
    wait(fetch([(source, out)], sems))


def edge_lists(edge_tiles, row_count, groups, rel_count):
    tile_count, _, slot_total = edge_tiles.shape
    lines = tile_count * slot_total // LANES
    row_bits = (row_count - 1).bit_length()
    room = (tile_count * slot_total + 5 * UNROLL + LINE - 1) // LINE * LINE
    flat = pltpu.VMEM((lines, LANES), jnp.int32)
    flat_smem = pltpu.SMEM((lines, LANES), jnp.int32)
    words, ends = pl.pallas_call(
        functools.partial(
            bucket_kernel, tile_count=tile_count, row_count=row_count, rel_count=rel_count
        ),
        out_shape=[
            jax.ShapeDtypeStruct((room,), jnp.int32), jax.ShapeDtypeStruct((4,), jnp.int32)
        ],
        in_specs=[VMEM],
        out_specs=[SMEM] * 2,
        scratch_shapes=[flat] * 5
        + [pltpu.VMEM((8, LANES), jnp.int32), flat_smem, flat_smem]
        + [pltpu.SMEM((8, LANES), jnp.int32), pltpu.SemaphoreType.DMA((3,))],
        name="bucket",
    )(edge_tiles.transpose(1, 0, 2))
    source = (words & (2 * row_count - 1)) * groups
    target = ((words >> (row_bits + 1)) & (row_count - 1)) * groups
    return room, ends, source, target, words >> (2 * row_bits + 1)


def body(
    entity_state,
    edge_tiles,
    query_head,
    query_relation,
    query_table,
    rel_vectors,
    mix_weight,
    mix_bias,
    cotangent,
):
    row_count, col_count = entity_state.shape
    groups = col_count // LANES
    long = row_count * groups
    query_count = query_head.shape[0]
    rel_count = rel_vectors.shape[1]
    seats = Seats(lax.axis_size("node"), lax.axis_size("query"))

    def send(block, route):
        return lax.ppermute(block, AXES, route)

    def run(fn, args, specs, outs, out_specs, scratch):
        return pl.pallas_call(fn, out_shape=outs, in_specs=specs, out_specs=out_specs, scratch_shapes=scratch)(*args)

    wide_f32 = jax.ShapeDtypeStruct((long, LANES), jnp.float32)
    wide_bf16 = jax.ShapeDtypeStruct((long, LANES), jnp.bfloat16)
    f32_buf = pltpu.VMEM((long, LANES), jnp.float32)
    bf16_buf = pltpu.VMEM((long, LANES), jnp.bfloat16)
    pair = pltpu.VMEM((2 * long, LANES), jnp.float32)
    sums = [f32_buf] * SUMS
    pair_sums = [pair] * SUMS
    square = jax.ShapeDtypeStruct((LANES, LANES), jnp.float32)
    line = jax.ShapeDtypeStruct((1, LANES), jnp.float32)

    state_zero = send(entity_state, seats.gather())
    room, ends, source, target, rel = edge_lists(edge_tiles, row_count, groups, rel_count)
    heads = query_head - lax.axis_index("node") * row_count
    tail = jnp.concatenate([ends, heads, query_relation])
    tail_room = -(-tail.shape[0] // LINE) * LINE
    tail = jnp.pad(tail, (0, tail_room - tail.shape[0]))
    flat = send(jnp.concatenate([source, target, rel, tail]), seats.gather())
    own_relation = flat[3 * room + 4 + query_count : 3 * room + 4 + 2 * query_count]
    grad_out = send(cotangent, seats.gather())

    choose_rel = (own_relation[:, None] == lax.iota(jnp.int32, query_table.shape[0])[None, :]).astype(
        jnp.float32
    )
    query_vec = (
        jnp.dot(choose_rel, query_table, precision=HIGHEST, preferred_element_type=jnp.float32)
        .astype(jnp.bfloat16)
        .astype(jnp.float32)
    )
    repeat = LANES // DIM
    lane_group = lax.iota(jnp.int32, LANES) // DIM
    head_rows = jnp.where(
        lane_group[None, :] == (lax.iota(jnp.int32, query_count) % repeat)[:, None],
        jnp.tile(query_vec, (1, repeat)),
        0.0,
    )
    rels = rel_vectors.transpose(0, 2, 1)
    list_bufs = [pltpu.SMEM((room,), jnp.int32)] * 3 + [pltpu.SMEM((tail_room,), jnp.int32)]
    table_buf = pltpu.VMEM(((rel_count // LANES + 1) * LANES, LANES), jnp.float32)

    def sems(count):
        return pltpu.SemaphoreType.DMA((count,))

    def halo(block):
        mirror = send(block, seats.mirror())
        left = send(block, seats.shift(1))
        right = send(block, seats.shift(-1))
        return mirror, left, right

    block_buf = pltpu.VMEM(state_zero.shape, jnp.bfloat16)
    mirror, left, right = halo(state_zero)
    near = run(
        functools.partial(near_zero_kernel, groups),
        [rels, flat, state_zero, mirror],
        [VMEM] + [HBM] * 3,
        wide_f32,
        HBM,
        [*list_bufs, block_buf, block_buf, table_buf, pair, sems(11), *sums],
    )
    state_one, mixed = run(
        functools.partial(first_kernel, groups),
        [rels, head_rows, mix_weight, mix_bias, flat, left, right, near, state_zero],
        [VMEM] * 4 + [HBM] * 5,
        [wide_bf16, wide_bf16],
        [HBM] * 2,
        [*list_bufs, block_buf, block_buf, table_buf, block_buf, pair, bf16_buf, bf16_buf, sems(17), *sums],
    )
    mirror_mixed, left_mixed, right_mixed = halo(mixed)
    near = run(
        functools.partial(near_one_kernel, groups),
        [rels, mix_weight, mix_bias, flat, state_one, mirror, mirror_mixed],
        [VMEM] * 3 + [HBM] * 4,
        wide_f32,
        HBM,
        [*list_bufs, bf16_buf, block_buf, bf16_buf, table_buf, pair, sems(12), *sums],
    )
    own_slope, mirror_slope, weight_zero, bias_zero = run(
        prepare_kernel,
        [mix_weight, mix_bias, grad_out, mixed, mirror_mixed],
        [VMEM] * 5,
        [wide_f32, wide_f32, square, line],
        [VMEM] * 4,
        [f32_buf, pltpu.VMEM((LANES, 2 * LANES), jnp.float32)],
    )
    state_two, grad_mixed, left_slope, right_slope, weight_one, bias_one = run(
        functools.partial(second_kernel, groups),
        [rels, head_rows, mix_weight, mix_bias, flat, left, right, left_mixed, right_mixed, near, state_one]
        + [grad_out],
        [VMEM] * 4 + [HBM] * 8,
        [jax.ShapeDtypeStruct(entity_state.shape, jnp.bfloat16), wide_bf16, wide_f32, wide_f32]
        + [square, line],
        [HBM] * 4 + [VMEM] * 2,
        [*list_bufs, block_buf, block_buf, bf16_buf, bf16_buf, table_buf, bf16_buf, block_buf, pair]
        + [bf16_buf, block_buf, f32_buf, f32_buf, pltpu.VMEM((2 * LANES, 2 * LANES), jnp.float32)]
        + [sems(16), *sums],
    )
    final_state = run(
        copy_kernel, [send(state_two, seats.give_back())], [HBM],
        jax.ShapeDtypeStruct(entity_state.shape, jnp.bfloat16), VMEM, [sems(1)],
    )
    grads = run(
        functools.partial(adjoint_kernel, groups),
        [rels, weight_zero, bias_zero, weight_one, bias_one, flat, grad_mixed, left_mixed, left_slope]
        + [right_mixed, right_slope, mixed, own_slope, mirror_mixed, mirror_slope],
        [VMEM] * 5 + [HBM] * 10,
        jax.ShapeDtypeStruct((2 * DIM + 8, LANES), jnp.float32),
        VMEM,
        [*list_bufs, bf16_buf, table_buf, *([bf16_buf, f32_buf] * 4), f32_buf]
        + [pltpu.VMEM((LANES, 2 * LANES), jnp.float32), pltpu.VMEM((1, LANES), jnp.float32), sems(14)]
        + pair_sums,
    )
    devices = seats.nodes * seats.queries
    reach = 1
    while reach < devices:
        grads = grads + send(grads, [(i, i ^ reach) for i in range(devices)])
        reach *= 2
    weight_grads = grads[: 2 * DIM, :DIM].reshape(2, DIM, DIM)
    bias_grads = grads[2 * DIM : 2 * DIM + 2, :DIM]
    return (final_state, weight_grads, bias_grads)


def solution(mesh):
    placed = (
        P("node", "query"),
        P("node", None, None),
        P("query"),
        P("query"),
        P(),
        P(),
        P(),
        P(),
        P("node", "query"),
    )

    return jax.shard_map(body, mesh=mesh, in_specs=placed, out_specs=(P("node", "query"), P(), P()), check_vma=False)
```

```python
import functools

import jax
import jax.numpy as jnp
from jax import lax
from jax.experimental import pallas as pl
from jax.experimental.pallas import tpu as pltpu
from jax.sharding import PartitionSpec as P


DIM = 32
LANES = 128
UNROLL = 96
SUMS = 3
CHUNK = 256
DENSE = 1024
LINE = 1024
VMEM_LIMIT = 65400 * 1024
AXES = ("node", "query")
HIGHEST = lax.Precision.HIGHEST
SMEM = pl.BlockSpec(memory_space=pltpu.SMEM)
VMEM = pl.BlockSpec(memory_space=pltpu.VMEM)
HBM = pl.BlockSpec(memory_space=pltpu.HBM)


class Seats:
    def __init__(self, nodes, queries):
        self.nodes, self.queries = nodes, queries

    def home(self, part, column):
        return part * self.queries + column

    def seat(self, part, column):
        half = self.nodes // 2
        low = part % half
        node = (column & 1) * half + (low ^ (low >> 1))
        return node * self.queries + (column >> 1) * 2 + 1 - part // half

    def blocks(self):
        return [(p, c) for p in range(self.nodes) for c in range(self.queries)]

    def gather(self):
        return [(self.home(p, c), self.seat(p, c)) for p, c in self.blocks()]

    def give_back(self):
        return [(target, source) for source, target in self.gather()]

    def shift(self, step):
        return [
            (self.seat((p - step) % self.nodes, c), self.seat(p, c)) for p, c in self.blocks()
        ]

    def mirror(self):
        return [
            (self.seat(p, c), self.seat((p + self.nodes // 2) % self.nodes, c))
            for p, c in self.blocks()
        ]

    def parts(self):
        table = [0] * (self.nodes * self.queries)
        for p, c in self.blocks():
            table[self.seat(p, c)] = p
        return table


def spread(block_ref, window_ref, first):
    if block_ref.shape[1] == LANES:
        rows = block_ref.shape[0]

        def step(i, carry):
            at = pl.multiple_of(i * CHUNK, CHUNK)
            window_ref[pl.ds(first + at, CHUNK), :] = block_ref[pl.ds(at, CHUNK), :].astype(
                jnp.float32
            )
            return carry

        lax.fori_loop(0, rows // CHUNK, step, 0)
        return
    rows, cols = block_ref.shape
    groups = cols // LANES
    size = CHUNK // groups

    def step(i, carry):
        at = pl.multiple_of(i * size, size)
        for j in range(groups):
            window_ref[pl.ds(first + at * groups + j, size, stride=groups), :] = block_ref[
                pl.ds(at, size), j * LANES : (j + 1) * LANES
            ].astype(jnp.float32)
        return carry

    lax.fori_loop(0, rows // size, step, 0)


def clear(sums):
    def step(i, carry):
        at = pl.multiple_of(i * CHUNK, CHUNK)
        for ref in sums:
            ref[pl.ds(at, CHUNK), :] = jnp.zeros((CHUNK, LANES), jnp.float32)
        return carry

    lax.fori_loop(0, sums[0].shape[0] // CHUNK, step, 0)


def walk(groups, begin, end, from_ref, to_ref, rel_ref, window, table, sums):
    room = from_ref.shape[0] - UNROLL
    views = [[ref.at[pl.ds(u, room)] for ref in (from_ref, to_ref, rel_ref)] for u in range(UNROLL)]

    def step(i, carry):
        first = begin + i * UNROLL
        for u, (from_view, to_view, rel_view) in enumerate(views):
            source = pl.multiple_of(from_view[first], groups)
            target = pl.multiple_of(to_view[first], groups)
            scale = table[pl.ds(rel_view[first], groups, stride=0), :]
            sums[u % SUMS][pl.ds(target, groups), :] += (
                window[pl.ds(source, groups), :] * scale
            )
        return carry

    lax.fori_loop(0, (end - begin) // UNROLL, step, 0)


def total_of(sums, at, size=CHUNK):
    value = sums[0][pl.ds(at, size), :]
    for ref in sums[1:]:
        value = value + ref[pl.ds(at, size), :]
    return value


def fetch(pairs, sems):
    copies = [pltpu.make_async_copy(src, dst, sems.at[i]) for i, (src, dst) in enumerate(pairs)]
    for copy in copies:
        copy.start()
    return copies


def wait(copies):
    for copy in copies:
        copy.wait()


def bucket_kernel(
    edges_ref, out_ref, ends_ref, slots, rows, rels, pos, word, meta, pos_buf, word_buf, meta_buf,
    sems, *, tile_count, row_count, rel_count,
):
    lines = slots.shape[0]
    first = 64 * lax.broadcasted_iota(jnp.int32, (tile_count, LANES), 0)
    for j in range(lines // tile_count):
        piece = slice(j * tile_count, (j + 1) * tile_count)
        lanes = slice(j * LANES, (j + 1) * LANES)
        slots[piece, :] = edges_ref[0, :, lanes]
        rows[piece, :] = edges_ref[1, :, lanes] + first
        rels[piece, :] = edges_ref[2, :, lanes]
    slot = slots[...]
    quarter = sum(((slot >= k * row_count).astype(jnp.int32) for k in range(1, 4)))
    local = slot - quarter * row_count
    kind = jnp.where((quarter == 1) | (quarter == 3), 0, 1)
    second = jnp.where(quarter >= 2, row_count, 0)
    row_bits = (row_count - 1).bit_length()
    word[...] = (rels[...] << (2 * row_bits + 1)) | (rows[...] << (row_bits + 1)) | (second + local)
    shape = (LANES, LANES)
    upto = (lax.broadcasted_iota(jnp.int32, shape, 0) <= lax.broadcasted_iota(jnp.int32, shape, 1))
    upto = upto.astype(jnp.float32).astype(jnp.bfloat16)
    shape = (lines, lines)
    above = (lax.broadcasted_iota(jnp.int32, shape, 0) > lax.broadcasted_iota(jnp.int32, shape, 1))
    above = above.astype(jnp.float32).astype(jnp.bfloat16)
    ones = jnp.ones((LANES, LANES), jnp.bfloat16)
    place = jnp.zeros((lines, LANES), jnp.float32)
    begin = jnp.zeros((1, LANES), jnp.float32)
    for k in range(2):
        chosen = (kind == k).astype(jnp.float32)
        onehot = chosen.astype(jnp.bfloat16)
        within = jnp.dot(onehot, upto, preferred_element_type=jnp.float32)
        per_line = jnp.dot(onehot, ones, preferred_element_type=jnp.float32)
        before = jnp.dot(above, per_line.astype(jnp.bfloat16), preferred_element_type=jnp.float32)
        count = jnp.sum(per_line, axis=0, keepdims=True)
        place = place + chosen * (begin + before + within - 1.0)
        meta[k : k + 1, :] = (begin + count).astype(jnp.int32)
        begin = begin + jnp.floor((count + (UNROLL - 0.5)) / UNROLL) * UNROLL
        meta[k + 2 : k + 3, :] = begin.astype(jnp.int32)
    spots = place.astype(jnp.int32)
    half = lines // 2
    pos[...] = spots[:half] | (spots[half:] << 16)
    wait(fetch([(pos, pos_buf), (word, word_buf), (meta, meta_buf)], sems))

    def step(i, carry):
        for u in range(LANES):
            spot = pos_buf[i, u]
            out_ref[spot & 0xFFFF] = word_buf[i, u]
            out_ref[spot >> 16] = word_buf[half + i, u]
        return carry

    lax.fori_loop(0, half, step, 0)
    dummy = rel_count << (2 * row_bits + 1)

    def fill(i, carry):
        out_ref[i] = dummy
        return carry

    for k in range(2):
        lax.fori_loop(meta_buf[k, 0], meta_buf[k + 2, 0], fill, 0)
        ends_ref[k] = meta_buf[k + 2, 0]


def split(values):
    high = values.astype(jnp.bfloat16)
    low = (values - high.astype(jnp.float32)).astype(jnp.bfloat16)
    return jnp.concatenate([high, low], axis=1)


def split_weight(weight):
    wide = split(weight)
    return jnp.concatenate([wide, wide], axis=0)


def times(values, wide):
    both = jnp.dot(split(values), wide, preferred_element_type=jnp.float32)
    return both[:, :LANES] + both[:, LANES:]


def outer(left, right):
    return lax.dot_general(
        split(left), split(right), (((0,), (0,)), ((), ())), preferred_element_type=jnp.float32
    )


def outer_rounded(left, right):
    return lax.dot_general(
        left, split(right), (((0,), (0,)), ((), ())), preferred_element_type=jnp.float32
    )


def quarters(wide):
    return (
        wide[:LANES, :LANES] + wide[LANES:, :LANES] + wide[:LANES, LANES:] + wide[LANES:, LANES:]
    )


def make_table(rels, index, table):
    count = rels.shape[2]
    for at in range(0, table.shape[0], LANES):
        size = min(LANES, count - at)
        piece = rels[index, :, at : at + size]
        if size < LANES:
            piece = jnp.concatenate([piece, jnp.zeros((DIM, LANES - size), jnp.float32)], axis=1)
        table[at : at + LANES, :] = jnp.concatenate([piece] * (LANES // DIM), axis=0).T


def block_weight(weight):
    repeat = LANES // DIM
    wide = jnp.concatenate([jnp.concatenate([weight] * repeat, axis=1)] * repeat, axis=0)
    row = lax.broadcasted_iota(jnp.int32, wide.shape, 0)
    lane = lax.broadcasted_iota(jnp.int32, wide.shape, 1)
    return jnp.where((row & -DIM) == (lane & -DIM), wide, 0.0)


def block_bias(bias):
    return jnp.concatenate([bias] * (LANES // DIM), axis=1)


def update_of(mixed, wide, bias):
    both = jnp.dot(mixed, wide, preferred_element_type=jnp.float32)
    return both[:, :LANES] + both[:, LANES:] + bias


def slope_from(values, sigma):
    return sigma * (1.0 + values * (1.0 - sigma))


def advance(state_buf, mixed_buf, window, first, wide, bias, slope_buf=None):
    spread(state_buf, window, first)

    def step(i, carry):
        at = pl.multiple_of(i * DENSE, DENSE)
        values = update_of(mixed_buf[pl.ds(at, DENSE), :], wide, bias)
        sigma = jax.nn.sigmoid(values)
        window[pl.ds(first + at, DENSE), :] += values * sigma
        if slope_buf is not None:
            slope_buf[pl.ds(at, DENSE), :] = slope_from(values, sigma)
        return carry

    lax.fori_loop(0, mixed_buf.shape[0] // DENSE, step, 0)


def send_total(sums, out, sems):
    parts = 4
    size = sums[0].shape[0] // parts
    stores = []
    for k in range(parts):

        def step(i, carry):
            at = pl.multiple_of(k * size + i * CHUNK, CHUNK)
            sums[0][pl.ds(at, CHUNK), :] = total_of(sums, at)
            return carry

        lax.fori_loop(0, size // CHUNK, step, 0)
        piece = pl.ds(k * size, size)
        stores += fetch([(sums[0].at[piece, :], out.at[piece, :])], sems.at[pl.ds(k, 1)])
    wait(stores)


def near_zero_kernel(
    groups, rels, flat, own, mirror, out,
    source, target, rel, tail, own_buf, mirror_buf, table_buf, window, sems, *sums,
):
    long = sums[0].shape[0]
    lists = fetch_lists(flat, (source, target, rel, tail), sems)
    states = fetch([(own, own_buf), (mirror, mirror_buf)], sems.at[pl.ds(5, 2)])
    make_table(rels, 0, table_buf)
    clear(sums)
    states[0].wait()
    spread(own_buf, window, 0)
    states[1].wait()
    spread(mirror_buf, window, long)
    wait(lists)
    walk(groups, 0, tail[0], source, target, rel, window, table_buf, sums)
    send_total(sums, out, sems.at[pl.ds(7, 4)])


def near_one_kernel(
    groups, rels, weights, biases, flat, own, mirror, mirror_mixed, out,
    source, target, rel, tail, own_buf, mirror_buf, mixed_buf, table_buf, window, sems, *sums,
):
    long = sums[0].shape[0]
    lists = fetch_lists(flat, (source, target, rel, tail), sems)
    states = fetch(
        [(own, own_buf), (mirror, mirror_buf), (mirror_mixed, mixed_buf)], sems.at[pl.ds(5, 3)]
    )
    make_table(rels, 1, table_buf)
    clear(sums)
    wait(states)
    spread(own_buf, window, 0)
    advance(mirror_buf, mixed_buf, window, long, split(block_weight(weights[0])), block_bias(biases[0:1, :]))
    wait(lists)
    walk(groups, 0, tail[0], source, target, rel, window, table_buf, sums)
    send_total(sums, out, sems.at[pl.ds(8, 4)])


def add_boundary(groups, heads, head_rows, ref, long):
    for q in range(head_rows.shape[0]):
        row = heads[2 + q]

        @pl.when((row >= 0) & (row < long // groups))
        def _():
            at = row * groups + q * DIM // LANES
            ref[pl.ds(at, 1), :] += head_rows[q : q + 1, :]


def fetch_lists(flat, bufs, sems):
    room = bufs[0].shape[0]
    pairs = [(flat.at[pl.ds(k * room, buf.shape[0])], buf) for k, buf in enumerate(bufs)]
    return fetch(pairs, sems)


def first_kernel(
    groups, rels, head_rows, weights, biases, flat, left, right, near, own, state, mixed,
    source, target, rel, tail, left_buf, right_buf, table_buf, own_buf, window, mixed_buf, state_buf,
    sems, *sums,
):
    long = sums[0].shape[0]
    lists = fetch_lists(flat, (source, target, rel, tail), sems)
    states = fetch([(left, left_buf), (right, right_buf), (near, sums[0])], sems.at[pl.ds(5, 3)])
    make_table(rels, 0, table_buf)
    clear(sums[1:])
    states[0].wait()
    spread(left_buf, window, 0)
    states[1].wait()
    spread(right_buf, window, long)
    states[2].wait()
    wait(lists)
    extra = fetch([(own, own_buf)], sems.at[pl.ds(8, 1)])
    add_boundary(groups, tail, head_rows, sums[0], long)
    walk(groups, tail[0], tail[1], source, target, rel, window, table_buf, sums)
    wait(extra)
    spread(own_buf, window, 0)
    wide = split_weight(block_weight(weights[0]))
    bias = block_bias(biases[0:1, :])
    parts = 4
    size = long // parts
    stores = []
    for k in range(parts):

        def step(i, carry):
            at = pl.multiple_of(k * size + i * DENSE, DENSE)
            rows = pl.ds(at, DENSE)
            mix = total_of(sums, at, DENSE)
            values = times(mix, wide) + bias
            mixed_buf[rows, :] = mix.astype(jnp.bfloat16)
            state_buf[rows, :] = (window[rows, :] + values * jax.nn.sigmoid(values)).astype(
                jnp.bfloat16
            )
            return carry

        lax.fori_loop(0, size // DENSE, step, 0)
        rows = pl.ds(k * size, size)
        stores += fetch(
            [(state_buf.at[rows, :], state.at[rows, :]), (mixed_buf.at[rows, :], mixed.at[rows, :])],
            sems.at[pl.ds(9 + 2 * k, 2)],
        )
    wait(stores)


def second_kernel(
    groups, rels, head_rows, weights, biases, flat, left, right, left_mixed, right_mixed, near, own,
    cotangent, state, grad_mixed, left_slope, right_slope, weight_sum, bias_sum,
    source, target, rel, tail, left_buf, right_buf, left_mixed_buf, right_mixed_buf, table_buf, own_buf,
    cotangent_buf, window, grad_mixed_buf, state_buf, left_slope_buf, right_slope_buf, wide_sum, sems, *sums,
):
    long = sums[0].shape[0]
    states = fetch(
        [(left, left_buf), (left_mixed, left_mixed_buf), (right, right_buf)]
        + [(right_mixed, right_mixed_buf), (near, sums[0])],
        sems.at[pl.ds(5, 5)],
    )
    lists = fetch_lists(flat, (source, target, rel, tail), sems)
    make_table(rels, 1, table_buf)
    clear(sums[1:])
    first = split(block_weight(weights[0]))
    first_bias = block_bias(biases[0:1, :])
    wait(states[:2])
    advance(left_buf, left_mixed_buf, window, 0, first, first_bias, left_slope_buf)
    wait(states[2:])
    advance(right_buf, right_mixed_buf, window, long, first, first_bias, right_slope_buf)
    stores = fetch(
        [(left_slope_buf, left_slope), (right_slope_buf, right_slope)], sems.at[pl.ds(14, 2)]
    )
    wait(lists)
    extra = fetch([(own, own_buf), (cotangent, cotangent_buf)], sems.at[pl.ds(10, 2)])
    add_boundary(groups, tail, head_rows, sums[0], long)
    walk(groups, tail[0], tail[1], source, target, rel, window, table_buf, sums)
    wait(extra)
    spread(own_buf, window, 0)
    spread(cotangent_buf, window, long)
    weight = block_weight(weights[1])
    wide = split_weight(weight)
    wide_back = split_weight(weight.T)
    bias = block_bias(biases[1:2, :])
    wide_sum[...] = jnp.zeros_like(wide_sum)
    bias_sum[...] = jnp.zeros_like(bias_sum)

    def step(i, carry):
        at = pl.multiple_of(i * DENSE, DENSE)
        rows = pl.ds(at, DENSE)
        mix = total_of(sums, at, DENSE)
        values = times(mix, wide) + bias
        sigma = jax.nn.sigmoid(values)
        window[rows, :] += values * sigma
        grad = window[pl.ds(long + at, DENSE), :] * slope_from(values, sigma)
        grad_mixed_buf[rows, :] = times(grad, wide_back).astype(jnp.bfloat16)
        wide_sum[...] += outer(mix, grad)
        bias_sum[...] += jnp.sum(grad, axis=0, keepdims=True)
        return carry

    lax.fori_loop(0, long // DENSE, step, 0)
    stores += fetch([(grad_mixed_buf, grad_mixed)], sems.at[pl.ds(12, 1)])
    size = CHUNK // groups

    def store(i, carry):
        at = pl.multiple_of(i * size, size)
        for j in range(groups):
            state_buf[pl.ds(at, size), j * LANES : (j + 1) * LANES] = window[
                pl.ds(at * groups + j, size, stride=groups), :
            ].astype(jnp.bfloat16)
        return carry

    lax.fori_loop(0, long // CHUNK, store, 0)
    stores += fetch([(state_buf, state)], sems.at[pl.ds(13, 1)])
    weight_sum[...] = quarters(wide_sum[...])
    wait(stores)


def folded(wide):
    value = wide[:DIM, :DIM]
    for g in range(1, LANES // DIM):
        value = value + wide[g * DIM : (g + 1) * DIM, g * DIM : (g + 1) * DIM]
    return value


def folded_row(wide):
    value = wide[:, :DIM]
    for g in range(1, LANES // DIM):
        value = value + wide[:, g * DIM : (g + 1) * DIM]
    return value


def prepare_kernel(
    weights, biases, cotangent, own, mirror, own_slope, mirror_slope, weight_sum, bias_sum, window, wide_sum
):
    spread(cotangent, window, 0)
    wide = split(block_weight(weights[0]))
    bias = block_bias(biases[0:1, :])
    wide_sum[...] = jnp.zeros_like(wide_sum)
    bias_sum[...] = jnp.zeros_like(bias_sum)

    def step(i, carry):
        rows = pl.ds(pl.multiple_of(i * DENSE, DENSE), DENSE)
        values = update_of(mirror[rows, :], wide, bias)
        mirror_slope[rows, :] = slope_from(values, jax.nn.sigmoid(values))
        mixed = own[rows, :]
        values = update_of(mixed, wide, bias)
        slope = slope_from(values, jax.nn.sigmoid(values))
        own_slope[rows, :] = slope
        grad = window[rows, :] * slope
        wide_sum[...] += outer_rounded(mixed, grad)
        bias_sum[...] += jnp.sum(grad, axis=0, keepdims=True)
        return carry

    lax.fori_loop(0, window.shape[0] // DENSE, step, 0)
    weight_sum[...] = wide_sum[:, :LANES] + wide_sum[:, LANES:]


def adjoint_kernel(
    groups, rels, weight_zero, bias_zero, weight_one, bias_one, flat, grad_mixed, *refs
):
    parts, refs = refs[:8], refs[8:]
    out, source, target, rel, tail, grad_mixed_buf, table_buf = refs[:7]
    bufs, refs = refs[7:15], refs[15:]
    window, wide_sum, bias_sum, sems = refs[:4]
    sums = refs[4:]
    long = window.shape[0]
    lists = fetch_lists(flat, (source, target, rel, tail), sems)
    loads = fetch([(grad_mixed, grad_mixed_buf)], sems.at[pl.ds(5, 1)])
    make_table(rels, 1, table_buf)
    clear(sums)
    wide_sum[...] = jnp.zeros_like(wide_sum)
    bias_sum[...] = bias_zero[...]
    wait(loads)
    spread(grad_mixed_buf, window, 0)
    wait(lists)
    late = fetch(list(zip(parts, bufs)), sems.at[pl.ds(6, 8)])

    def add_products(mixed_buf, slope_buf, first, again):
        def step(i, carry):
            at = pl.multiple_of(i * DENSE, DENSE)
            grad = total_of(sums, first + at, DENSE) * slope_buf[pl.ds(at, DENSE), :]
            if again:
                for ref in sums:
                    ref[pl.ds(first + at, DENSE), :] = jnp.zeros((DENSE, LANES), jnp.float32)
            wide_sum[...] += outer_rounded(mixed_buf[pl.ds(at, DENSE), :], grad)
            bias_sum[...] += jnp.sum(grad, axis=0, keepdims=True)
            return carry

        lax.fori_loop(0, long // DENSE, step, 0)

    walk(groups, tail[0], tail[1], target, source, rel, window, table_buf, sums)
    wait(late)
    add_products(bufs[0], bufs[1], 0, True)
    add_products(bufs[2], bufs[3], long, True)
    walk(groups, 0, tail[0], target, source, rel, window, table_buf, sums)
    add_products(bufs[4], bufs[5], 0, False)
    add_products(bufs[6], bufs[7], long, False)
    out[...] = jnp.zeros_like(out)
    out[0:DIM, 0:DIM] = folded(wide_sum[:, :LANES] + wide_sum[:, LANES:] + weight_zero[...])
    out[DIM : 2 * DIM, 0:DIM] = folded(weight_one[...])
    out[2 * DIM : 2 * DIM + 1, 0:DIM] = folded_row(bias_sum[...])
    out[2 * DIM + 1 : 2 * DIM + 2, 0:DIM] = folded_row(bias_one[...])


def copy_kernel(source, out, sems):
    wait(fetch([(source, out)], sems))


def edge_lists(edge_tiles, row_count, groups, rel_count):
    tile_count, _, slot_total = edge_tiles.shape
    lines = tile_count * slot_total // LANES
    row_bits = (row_count - 1).bit_length()
    room = (tile_count * slot_total + 3 * UNROLL + LINE - 1) // LINE * LINE
    flat = pltpu.VMEM((lines, LANES), jnp.int32)
    flat_smem = pltpu.SMEM((lines, LANES), jnp.int32)
    packed = pltpu.VMEM((lines // 2, LANES), jnp.int32)
    packed_smem = pltpu.SMEM((lines // 2, LANES), jnp.int32)
    words, ends = pl.pallas_call(
        functools.partial(
            bucket_kernel, tile_count=tile_count, row_count=row_count, rel_count=rel_count
        ),
        out_shape=[
            jax.ShapeDtypeStruct((room,), jnp.int32), jax.ShapeDtypeStruct((2,), jnp.int32)
        ],
        in_specs=[VMEM],
        out_specs=[SMEM] * 2,
        scratch_shapes=[flat] * 3
        + [packed, flat, pltpu.VMEM((8, LANES), jnp.int32), packed_smem, flat_smem]
        + [pltpu.SMEM((8, LANES), jnp.int32), pltpu.SemaphoreType.DMA((3,))],
        name="bucket",
    )(edge_tiles.transpose(1, 0, 2))
    source = (words & (2 * row_count - 1)) * groups
    target = ((words >> (row_bits + 1)) & (row_count - 1)) * groups
    return room, ends, source, target, words >> (2 * row_bits + 1)


def body(
    entity_state,
    edge_tiles,
    query_head,
    query_relation,
    query_table,
    rel_vectors,
    mix_weight,
    mix_bias,
    cotangent,
):
    row_count, col_count = entity_state.shape
    groups = col_count // LANES
    long = row_count * groups
    query_count = query_head.shape[0]
    rel_count = rel_vectors.shape[1]
    seats = Seats(lax.axis_size("node"), lax.axis_size("query"))

    def send(block, route):
        return lax.ppermute(block, AXES, route)

    def run(fn, args, specs, outs, out_specs, scratch):
        return pl.pallas_call(
            fn, out_shape=outs, in_specs=specs, out_specs=out_specs, scratch_shapes=scratch,
            compiler_params=pltpu.CompilerParams(vmem_limit_bytes=VMEM_LIMIT),
        )(*args)

    wide_f32 = jax.ShapeDtypeStruct((long, LANES), jnp.float32)
    wide_bf16 = jax.ShapeDtypeStruct((long, LANES), jnp.bfloat16)
    f32_buf = pltpu.VMEM((long, LANES), jnp.float32)
    bf16_buf = pltpu.VMEM((long, LANES), jnp.bfloat16)
    pair = pltpu.VMEM((2 * long, LANES), jnp.float32)
    sums = [f32_buf] * SUMS
    pair_sums = [pair] * SUMS
    square = jax.ShapeDtypeStruct((LANES, LANES), jnp.float32)
    line = jax.ShapeDtypeStruct((1, LANES), jnp.float32)

    state_zero = send(entity_state, seats.gather())
    room, ends, source, target, rel = edge_lists(edge_tiles, row_count, groups, rel_count)
    heads = query_head - lax.axis_index("node") * row_count
    tail = jnp.concatenate([ends, heads, query_relation])
    tail_room = -(-tail.shape[0] // LINE) * LINE
    tail = jnp.pad(tail, (0, tail_room - tail.shape[0]))
    flat = send(jnp.concatenate([source, target, rel, tail]), seats.gather())
    own_relation = flat[3 * room + 2 + query_count : 3 * room + 2 + 2 * query_count]
    grad_out = send(cotangent, seats.gather())

    choose_rel = (own_relation[:, None] == lax.iota(jnp.int32, query_table.shape[0])[None, :]).astype(
        jnp.float32
    )
    query_vec = (
        jnp.dot(choose_rel, query_table, precision=HIGHEST, preferred_element_type=jnp.float32)
        .astype(jnp.bfloat16)
        .astype(jnp.float32)
    )
    repeat = LANES // DIM
    lane_group = lax.iota(jnp.int32, LANES) // DIM
    head_rows = jnp.where(
        lane_group[None, :] == (lax.iota(jnp.int32, query_count) % repeat)[:, None],
        jnp.tile(query_vec, (1, repeat)),
        0.0,
    )
    rels = rel_vectors.transpose(0, 2, 1)
    list_bufs = [pltpu.SMEM((room,), jnp.int32)] * 3 + [pltpu.SMEM((tail_room,), jnp.int32)]
    table_buf = pltpu.VMEM(((rel_count // LANES + 1) * LANES, LANES), jnp.float32)

    def sems(count):
        return pltpu.SemaphoreType.DMA((count,))

    def halo(block):
        mirror = send(block, seats.mirror())
        left = send(block, seats.shift(1))
        right = send(block, seats.shift(-1))
        return mirror, left, right

    block_buf = pltpu.VMEM(state_zero.shape, jnp.bfloat16)
    mirror, left, right = halo(state_zero)
    near = run(
        functools.partial(near_zero_kernel, groups),
        [rels, flat, state_zero, mirror],
        [VMEM] + [HBM] * 3,
        wide_f32,
        HBM,
        [*list_bufs, block_buf, block_buf, table_buf, pair, sems(11), *sums],
    )
    state_one, mixed = run(
        functools.partial(first_kernel, groups),
        [rels, head_rows, mix_weight, mix_bias, flat, left, right, near, state_zero],
        [VMEM] * 4 + [HBM] * 5,
        [wide_bf16, wide_bf16],
        [HBM] * 2,
        [*list_bufs, block_buf, block_buf, table_buf, block_buf, pair, bf16_buf, bf16_buf, sems(17), *sums],
    )
    mirror_mixed, left_mixed, right_mixed = halo(mixed)
    near = run(
        functools.partial(near_one_kernel, groups),
        [rels, mix_weight, mix_bias, flat, state_one, mirror, mirror_mixed],
        [VMEM] * 3 + [HBM] * 4,
        wide_f32,
        HBM,
        [*list_bufs, bf16_buf, block_buf, bf16_buf, table_buf, pair, sems(12), *sums],
    )
    own_slope, mirror_slope, weight_zero, bias_zero = run(
        prepare_kernel,
        [mix_weight, mix_bias, grad_out, mixed, mirror_mixed],
        [VMEM] * 5,
        [wide_f32, wide_f32, square, line],
        [VMEM] * 4,
        [f32_buf, pltpu.VMEM((LANES, 2 * LANES), jnp.float32)],
    )
    state_two, grad_mixed, left_slope, right_slope, weight_one, bias_one = run(
        functools.partial(second_kernel, groups),
        [rels, head_rows, mix_weight, mix_bias, flat, left, right, left_mixed, right_mixed, near, state_one]
        + [grad_out],
        [VMEM] * 4 + [HBM] * 8,
        [jax.ShapeDtypeStruct(entity_state.shape, jnp.bfloat16), wide_bf16, wide_f32, wide_f32]
        + [square, line],
        [HBM] * 4 + [VMEM] * 2,
        [*list_bufs, block_buf, block_buf, bf16_buf, bf16_buf, table_buf, bf16_buf, block_buf, pair]
        + [bf16_buf, block_buf, f32_buf, f32_buf, pltpu.VMEM((2 * LANES, 2 * LANES), jnp.float32)]
        + [sems(16), *sums],
    )
    final_state = run(
        copy_kernel, [send(state_two, seats.give_back())], [HBM],
        jax.ShapeDtypeStruct(entity_state.shape, jnp.bfloat16), VMEM, [sems(1)],
    )
    grads = run(
        functools.partial(adjoint_kernel, groups),
        [rels, weight_zero, bias_zero, weight_one, bias_one, flat, grad_mixed, left_mixed, left_slope]
        + [right_mixed, right_slope, mixed, own_slope, mirror_mixed, mirror_slope],
        [VMEM] * 5 + [HBM] * 10,
        jax.ShapeDtypeStruct((2 * DIM + 8, LANES), jnp.float32),
        VMEM,
        [*list_bufs, bf16_buf, table_buf, *([bf16_buf, f32_buf] * 4), f32_buf]
        + [pltpu.VMEM((LANES, 2 * LANES), jnp.float32), pltpu.VMEM((1, LANES), jnp.float32), sems(14)]
        + pair_sums,
    )
    devices = seats.nodes * seats.queries
    reach = 1
    while reach < devices:
        grads = grads + send(grads, [(i, i ^ reach) for i in range(devices)])
        reach *= 2
    weight_grads = grads[: 2 * DIM, :DIM].reshape(2, DIM, DIM)
    bias_grads = grads[2 * DIM : 2 * DIM + 2, :DIM]
    return (final_state, weight_grads, bias_grads)


def solution(mesh):
    placed = (
        P("node", "query"),
        P("node", None, None),
        P("query"),
        P("query"),
        P(),
        P(),
        P(),
        P(),
        P("node", "query"),
    )

    return jax.shard_map(body, mesh=mesh, in_specs=placed, out_specs=(P("node", "query"), P(), P()), check_vma=False)
```
